256 devices in a mesh: leaf: 128 (over y, x, z_lo, core), player: 2 (over z_hi).
Axes of the slice: x: 4, y: 4, z: 8 (z_hi: 2, z_lo: 4; z = z_hi * 4 + z_lo), core: 2. Of those that a mesh axis runs over, the one named last changes fastest.
Arguments:
- chance_reach: float32 [2, 4096, 1326], P('player', 'leaf'), may hold values from 0.02 to 1
- regrets_start: float32 [2, 4096, 1326], P('player', 'leaf'), may hold values from -6 to 6
- pot: float32 [4096], P('leaf'), may hold values from 1 to 8
- parent: int32 [2, 4096], P('player'), may hold values from 0 to 2047, never falling along the last dimension, each value on 1 to 6 neighbouring positions
- hand_cards: int32 [1326, 2], replicated, may hold values from 0 to 51, as said below
- board_cards: int32 [512, 5], P('leaf'), may hold values from 0 to 51, as said below
- hand_rank: int32 [512, 1326], P('leaf'), may hold values from 0 to 1999
Outputs:
- regrets: float32 [2, 4096, 1326], P('player', 'leaf')
- values: float32 [2, 4096, 1326], P('player', 'leaf')
The draws below stay inside these ranges and needn't reach their ends.
Inputs may be any that keep to these rules, and one draw needn't show every extreme that they name: `parent`: along each row the node ids never fall; each node owns 1 to 6 consecutive leaves, one exactly 6; every id up to 2047 occurs. `hand_cards`: distinct pairs of two different cards, the smaller card first. `board_cards`: five different cards on each board.
All inputs are finite; a program needn't handle non-finite values.
Results may differ from the reference program's by a relative error of at most 0.0003.
Values sent between devices are 32-bit elements; how exact they have to be, the bound alone decides.
No kernel may reach another device: no remote copies, remote signals or barrier semaphores. Data moves between devices by JAX's collectives and lax.ppermute only.
A program may use at most 128 MiB of HBM per device.

```python
import math
import jax
import jax.numpy as jnp
import numpy as np
from jax import lax

H = 1326
BOARD_LEAVES = 8
MOST = 6
ITERS = 2
LEAVES = 4096
BOARDS = 512
NODES = 2048


def draw_hand_cards(key, part):
    lower_cards, upper_cards = np.triu_indices(52, 1)
    card_pairs = jnp.stack([jnp.asarray(lower_cards, jnp.int32), jnp.asarray(upper_cards, jnp.int32)], axis=1)
    chosen = jax.random.permutation(jax.random.fold_in(key, 3), card_pairs.shape[0])[:H]
    return card_pairs[chosen].astype(jnp.int32)


def draw_board_cards(key, part):
    board_keys = jax.random.split(jax.random.fold_in(key, 7), BOARDS)
    return jax.vmap(lambda board_key: jax.random.permutation(board_key, 52)[:5])(board_keys).astype(jnp.int32)


def place_ends(values, rng, least, high):
    longest = values.shape.index(max(values.shape))
    spots = []
    for shift in (0, 1):
        where = [jax.random.randint(jax.random.fold_in(rng, axis), (), 0, length) for axis, length in enumerate(values.shape)]
        where[longest] = (where[longest] + shift) % values.shape[longest]
        spots.append(tuple(where))
    return values.at[spots[0]].set(least).at[spots[1]].set(high)


def levels(rng, shape, cuts, least, top_value):
    factor_of, own = 1.0, jax.random.fold_in(rng, 6)
    for axis_at, blocks in cuts:
        draws = jnp.exp(jax.random.uniform(jax.random.fold_in(own, axis_at), (blocks,), jnp.float32, least / len(cuts), top_value / len(cuts)))
        factor_of = factor_of * jnp.repeat(draws, shape[axis_at] // blocks).reshape([-1 if axis == axis_at else 1 for axis in range(len(shape))])
    return factor_of


def profile(amount, total, limit, skew):
    portions = [(1 << 20) // math.isqrt(standing ** skew) + 1 for standing in range(2, amount + 1)]
    surplus, given = total - limit - (amount - 1), [1] * (amount - 1)
    while surplus > 0:
        movable = [i for i in range(amount - 1) if given[i] < limit]
        mass, budget = sum([portions[i] for i in movable]), surplus
        for i in movable:
            extra = min(limit - given[i], max(1, budget * portions[i] // mass), surplus)
            given[i] = given[i] + extra
            surplus = surplus - extra
    return np.array([limit] + given)


def ragged(key, number_of, total, most, slope):
    if number_of == 2:
        one = jax.random.randint(key, (), max(1, total - most), min(most, total - 1) + 1)
        return jnp.stack([one, total - one])
    lengths = jnp.asarray(profile(number_of, total, most, slope), jnp.int32)
    couples = (number_of - 1) // 2
    source_of, sink = lengths[1:1 + 2 * couples:2], lengths[2:2 + 2 * couples:2]
    room = jnp.minimum(source_of - 1, most - sink)
    shifted = jax.random.randint(jax.random.fold_in(key, 1), (couples,), 0, 1 << 20) % (room + 1)
    lengths = lengths.at[1:1 + 2 * couples:2].set(source_of - shifted).at[2:2 + 2 * couples:2].set(sink + shifted)
    return lengths[jax.random.permutation(jax.random.fold_in(key, 2), number_of)]


def bell_draw(rng, shape, width, bound, cuts=(), kind=jnp.bfloat16):
    factor_of = levels(rng, shape, cuts, -0.22, 0.18) if cuts else 1.0
    values = jax.random.normal(rng, shape, jnp.float32) * width * factor_of
    return jnp.minimum(jnp.maximum(values, -bound), bound).astype(kind)


def setup_inputs(seed: int = 0) -> dict:
    arg_keys = jax.random.split(jax.random.key(seed), 8)
    return {
        "chance_reach": jnp.clip(jnp.exp(math.log(1.0) - 3.912023 * jax.random.uniform(arg_keys[0], (2, LEAVES, H), jnp.float32) ** levels(arg_keys[0], (2, LEAVES, H), ((0, 2), (1, 128)), -0.2, 0.2)), 0.02, 1.0),
        "regrets_start": bell_draw(arg_keys[1], (2, LEAVES, H), 1.0, 6.0, ((0, 2), (1, 128)), jnp.float32),
        "pot": jnp.clip(jnp.exp(math.log(8.0) - 2.0794415 * jax.random.uniform(arg_keys[2], (LEAVES,), jnp.float32) ** levels(arg_keys[2], (LEAVES,), ((0, 128),), -0.2, 0.2)), 1.0, 8.0),
        "parent": jax.vmap(lambda own: jnp.searchsorted(jnp.cumsum(ragged(own, NODES, LEAVES, MOST, 2)), jnp.arange(LEAVES), side="right"))(jax.random.split(arg_keys[3], 2)).reshape((2, LEAVES)).astype(jnp.int32),
        "hand_cards": draw_hand_cards(jax.random.fold_in(arg_keys[7], 71), 0),
        "board_cards": draw_board_cards(jax.random.fold_in(arg_keys[7], 71), 0),
        "hand_rank": place_ends(jax.random.randint(arg_keys[6], (BOARDS, H), 0, 2000), jax.random.fold_in(arg_keys[6], 1), 0, 1999).astype(jnp.int32),
    }


DELTA = 0.05
EPSILON = 1e-06
DECK_SIZE = 52

def holding_table(hand_cards):
    deck_cards = jnp.arange(DECK_SIZE, dtype=jnp.int32)
    holding = (hand_cards[:, 0:1] == deck_cards[None, :]) | (hand_cards[:, 1:2] == deck_cards[None, :])
    return holding.astype(jnp.float32)

def board_free(board_cards, holding):
    deck_cards = jnp.arange(DECK_SIZE, dtype=jnp.int32)
    on_board = jnp.any(board_cards[:, :, None] == deck_cards[None, None, :], axis=1).astype(jnp.float32)
    touched = jnp.dot(on_board, holding.T, precision=lax.Precision.HIGHEST)
    return (touched < 0.5).astype(jnp.float32)

def payoff_matrix(rank_row, free_row, apart_mask):
    ranked = rank_row.astype(jnp.float32)
    sign_table = jnp.sign(ranked[:, None] - ranked[None, :])
    return sign_table * apart_mask * free_row[:, None] * free_row[None, :]

def node_totals(values, parents):
    totals = jax.ops.segment_sum(values, parents, num_segments=NODES)
    return totals[parents]

def reference(chance_reach, regrets_start, pot, parent, hand_cards, board_cards, hand_rank):
    holding = holding_table(hand_cards)
    apart_mask = (jnp.dot(holding, holding.T, precision=lax.Precision.HIGHEST) < 0.5).astype(jnp.float32)
    free_rows = board_free(board_cards, holding)
    pot_rows = pot.reshape(BOARDS, BOARD_LEAVES)
    regrets = regrets_start
    values = jnp.zeros_like(regrets_start)
    for iteration in range(ITERS):
        policy = []
        for player in range(2):
            positive = jnp.maximum(regrets[player], 0.0) + DELTA
            policy.append(positive / node_totals(positive, parent[player]))
        policy = jnp.stack(policy)
        own_reach = chance_reach * policy
        opposed = jnp.stack([own_reach[1], own_reach[0]]).reshape(2, BOARDS, BOARD_LEAVES, H).transpose(1, 0, 2, 3)

        def one_board(board_items):
            rank_row, free_row, opp_block, pot_row = board_items
            matrix = payoff_matrix(rank_row, free_row, apart_mask)
            summed = jnp.einsum('pkg,hg->pkh', opp_block, matrix, precision=lax.Precision.HIGHEST)
            return summed * (pot_row[None, :, None] * (1.0 / H))
        values = lax.map(one_board, (hand_rank, free_rows, opposed, pot_rows))
        values = values.transpose(1, 0, 2, 3).reshape(2, LEAVES, H)
        updated = []
        for player in range(2):
            instant = values[player] - node_totals(policy[player] * values[player], parent[player])
            norm_scale = jnp.sqrt(jnp.sum(instant * instant) / (LEAVES * H) + EPSILON)
            updated.append(regrets[player] + instant / norm_scale)
        regrets = jnp.stack(updated)
    return (regrets, values)
```

```python
import functools

import jax
import jax.numpy as jnp
from jax import lax
from jax.experimental import pallas as pl
from jax.experimental.pallas import tpu as pltpu
from jax.sharding import Mesh
from jax.sharding import PartitionSpec as P

LEAF = ("leaf_0", "leaf_1", "leaf_2", "leaf_3")
DELTA = 0.05
EPSILON = 1e-06
DECK_SIZE = 52

HANDS = 1326
WIDE = 1408
OWN = 32
SIDE = 16
WINDOW = OWN + 2 * SIDE
BOARD_LEAVES = 8
PIECES = 2
BF16 = jnp.bfloat16
F32 = jnp.float32
VMEM = functools.partial(pl.BlockSpec, memory_space=pltpu.VMEM)


def holding_table(hand_cards):
    deck_cards = jnp.arange(128, dtype=jnp.int32)
    holding = (hand_cards[:, 0:1] == deck_cards[None, :]) | (
        hand_cards[:, 1:2] == deck_cards[None, :]
    )
    return jnp.pad(holding, ((0, WIDE - HANDS), (0, 0))).astype(BF16)


ROWS = 32


def build_kernel(holding_ref, rank_ref, matrix_ref, apart_ref, column_ref, *, boards):
    @pl.loop(0, WIDE // 128)
    def _(i):
        rows = pl.ds(pl.multiple_of(i * 128, 128), 128)
        shared = lax.dot_general(
            holding_ref[rows, :],
            holding_ref[...],
            (((1,), (1,)), ((), ())),
            preferred_element_type=F32,
        )
        apart_ref[rows, :] = (1.0 - jnp.minimum(shared, 1.0)).astype(BF16)

    ranks = rank_ref[...]
    for t in range(WIDE // 128):
        lanes = slice(t * 128, (t + 1) * 128)
        tile = jnp.concatenate([ranks[:, lanes], jnp.zeros((120, 128), F32)], axis=0)
        column_ref[lanes, :] = tile.T

    @pl.loop(0, WIDE // ROWS)
    def _(i):
        rows = pl.ds(pl.multiple_of(i * ROWS, ROWS), ROWS)
        column = column_ref[rows, :]
        own = [jnp.broadcast_to(column[:, b : b + 1], (ROWS, 128)) for b in range(boards)]
        for t in range(WIDE // 128):
            lanes = slice(t * 128, (t + 1) * 128)
            apart = apart_ref[rows, lanes]
            minus = -apart
            for b in range(boards):
                gap = (own[b] - rank_ref[b : b + 1, lanes]).astype(BF16)
                matrix_ref[b, rows, lanes] = jnp.minimum(jnp.maximum(gap, minus), apart)


def build(holding, ranks, boards):
    return pl.pallas_call(
        functools.partial(build_kernel, boards=boards),
        out_shape=jax.ShapeDtypeStruct((boards, WIDE, WIDE), BF16),
        in_specs=[VMEM(), VMEM()],
        out_specs=VMEM(),
        scratch_shapes=[pltpu.VMEM((WIDE, WIDE), BF16), pltpu.VMEM((WIDE, 128), F32)],
        compiler_params=pltpu.CompilerParams(vmem_limit_bytes=40 << 20),
        cost_estimate=pl.CostEstimate(
            flops=boards * WIDE * WIDE * 8, bytes_accessed=boards * WIDE * WIDE, transcendentals=0
        ),
        name="build",
    )(holding, ranks)


def node_totals(same, values):
    high = values.astype(BF16)
    rest = values - high.astype(F32)
    middle = rest.astype(BF16)
    low = (rest - middle.astype(F32)).astype(BF16)
    parts = jnp.concatenate([high, middle, low], axis=0)
    return jnp.dot(same, parts, preferred_element_type=F32)


def policy_of(same, regrets):
    positive = jnp.maximum(regrets, 0.0) + DELTA
    return positive / node_totals(same, positive)


def split_terms(reach):
    high = reach.astype(BF16).astype(F32)
    return [high, reach - high]


def joined(out, first):
    middle = first + BOARD_LEAVES
    return out[first:middle] + out[middle : middle + BOARD_LEAVES]


def board_rows(free, boards):
    return jnp.concatenate(
        [jnp.broadcast_to(free[b : b + 1], (BOARD_LEAVES, WIDE)) for b in boards], axis=0
    )


def first_kernel(
    odd_ref,
    regrets_ref,
    chance_ref,
    even_ref,
    cross_ref,
    part_ref,
    edge_ref,
    same_ref,
    free_ref,
    pot_ref,
    own_matrix_ref,
    side_matrix_ref,
    window_ref,
    reached_ref,
    instant_ref,
    sums_ref,
    policy_ref,
    terms_ref,
    values_ref,
):
    odd = odd_ref[0] == 1
    even, cross = even_ref[...], cross_ref[...]
    left = jnp.where(odd, even, cross)
    right = jnp.where(odd, cross, even)
    window_ref[...] = jnp.zeros_like(window_ref)
    reached_ref[...] = jnp.zeros_like(reached_ref)
    policy_ref[...] = jnp.zeros_like(policy_ref)
    low, high = SIDE, SIDE + OWN
    window_ref[0, low - 15 : low, :HANDS] = left[0:15]
    window_ref[0, low:high, :HANDS] = regrets_ref[...]
    window_ref[0, high : high + 15, :HANDS] = right[0:15]
    policy_ref[0, low - 10 : low, :HANDS] = left[15:25]
    policy_ref[0, low:high, :HANDS] = chance_ref[...]
    policy_ref[0, high : high + 10, :HANDS] = right[15:25]
    window_ref[1, low - 10 : low, :HANDS] = edge_ref[0:10]
    window_ref[1, low:high, :HANDS] = part_ref[0:OWN]
    window_ref[1, high : high + 10, :HANDS] = edge_ref[10:20]
    reached_ref[low - 5 : low, :HANDS] = edge_ref[20:25]
    reached_ref[low:high, :HANDS] = part_ref[OWN : 2 * OWN]
    reached_ref[high : high + 5, :HANDS] = edge_ref[25:30]
    free = board_rows(free_ref, range(8))
    reached_ref[...] = reached_ref[...] * free
    terms = []
    for p in range(2):
        chance = policy_ref[0] * free if p == 0 else reached_ref[...]
        policy = policy_of(same_ref[p], window_ref[p])
        policy_ref[p] = policy
        terms.append(split_terms(chance * policy))
    for b in range(8):
        rows = slice(b * BOARD_LEAVES, (b + 1) * BOARD_LEAVES)
        block = jnp.concatenate([term[rows] for player in terms for term in player], axis=0)
        terms_ref[b] = block.astype(BF16)

    def board(b, matrix):
        out = jnp.dot(terms_ref[b], matrix, preferred_element_type=F32)
        rows = slice(b * BOARD_LEAVES, (b + 1) * BOARD_LEAVES)
        factor = pot_ref[rows, 0:1] * (-1.0 / HANDS)
        free = free_ref[b : b + 1, :]
        values_ref[1, rows, :] = joined(out, 0) * factor * free
        values_ref[0, rows, :] = joined(out, PIECES * BOARD_LEAVES) * factor * free

    for b in range(8):
        if 2 <= b < 6:
            board(b, own_matrix_ref[b - 2])
        else:
            board(b, side_matrix_ref[b if b < 2 else b - 4])

    sums = []
    for p in range(2):
        values = values_ref[p]
        instant = values - node_totals(same_ref[p], policy_ref[p] * values)
        instant_ref[p] = instant
        mine = instant[SIDE : SIDE + OWN]
        sums.append(jnp.sum(mine * mine))
    lane = lax.broadcasted_iota(jnp.int32, sums_ref.shape, 1)
    sums_ref[...] = jnp.where(lane == 0, sums[0], jnp.where(lane == 1, sums[1], 0.0))


def first(odd, regrets, chance, even, cross, part, edge, same, free, pot, own_matrix, side_matrix):
    shapes = (
        jax.ShapeDtypeStruct((2, WINDOW, WIDE), F32),
        jax.ShapeDtypeStruct((WINDOW, WIDE), F32),
        jax.ShapeDtypeStruct((2, WINDOW, WIDE), F32),
        jax.ShapeDtypeStruct((128, 128), F32),
    )
    arrays = (regrets, chance, even, cross, part, edge, same, free, pot)
    return pl.pallas_call(
        first_kernel,
        out_shape=shapes,
        in_specs=[pl.BlockSpec(memory_space=pltpu.SMEM)]
        + [VMEM()] * (len(arrays) + 2),
        out_specs=[VMEM()] * len(shapes),
        scratch_shapes=[
            pltpu.VMEM((2, WINDOW, WIDE), F32),
            pltpu.VMEM((8, 2 * PIECES * BOARD_LEAVES, WIDE), BF16),
            pltpu.VMEM((2, WINDOW, WIDE), F32),
        ],
        compiler_params=pltpu.CompilerParams(vmem_limit_bytes=40 << 20),
        name="first",
    )(odd, *arrays, own_matrix, side_matrix)


def second_kernel(
    gathered_ref,
    window_ref,
    reached_ref,
    instant_ref,
    same_ref,
    free_ref,
    pot_ref,
    own_matrix_ref,
    side_matrix_ref,
    out_values_ref,
    moved_ref,
    mine_ref,
    sums_ref,
    policy_ref,
    terms_ref,
    values_ref,
    *,
    count,
):
    values_ref[...] = jnp.zeros_like(values_ref)
    sums = jnp.sum(gathered_ref[...], axis=0, keepdims=True)
    scale = jnp.sqrt(sums / count + EPSILON)
    moved = window_ref[0] + instant_ref[0] / scale[:, 0:1]
    moved_ref[...] = moved[SIDE : SIDE + OWN]
    policy_ref[...] = policy_of(same_ref[0], moved)
    other = window_ref[1] + instant_ref[1] / scale[:, 1:2]
    terms = split_terms(reached_ref[...] * policy_of(same_ref[1], other))
    for b in range(8):
        rows = slice(b * BOARD_LEAVES, (b + 1) * BOARD_LEAVES)
        block = jnp.concatenate([term[rows] for term in terms], axis=0)
        terms_ref[b] = block.astype(BF16)

    def board(b, matrix):
        out = jnp.dot(terms_ref[b], matrix, preferred_element_type=F32)
        rows = slice(b * BOARD_LEAVES, (b + 1) * BOARD_LEAVES)
        factor = pot_ref[rows, 0:1] * (-1.0 / HANDS)
        values_ref[rows, :] = joined(out, 0) * factor * free_ref[b : b + 1, :]

    for b in range(1, 7):
        if 2 <= b < 6:
            board(b, own_matrix_ref[b - 2])
        else:
            board(b, side_matrix_ref[1 if b == 1 else 2])

    values = values_ref[...]
    instant = values - node_totals(same_ref[0], policy_ref[...] * values)
    mine = instant[SIDE : SIDE + OWN]
    mine_ref[...] = mine
    out_values_ref[...] = values[SIDE : SIDE + OWN, :HANDS]
    lane = lax.broadcasted_iota(jnp.int32, sums_ref.shape, 1)
    sums_ref[...] = jnp.where(lane == 0, jnp.sum(mine * mine), 0.0)


def second(gathered, window, reached, instant, same, free, pot, own_matrix, side_matrix, count):
    shapes = (
        jax.ShapeDtypeStruct((OWN, HANDS), F32),
        jax.ShapeDtypeStruct((OWN, WIDE), F32),
        jax.ShapeDtypeStruct((OWN, WIDE), F32),
        jax.ShapeDtypeStruct((128, 128), F32),
    )
    arrays = (gathered, window, reached, instant, same, free, pot)
    return pl.pallas_call(
        functools.partial(second_kernel, count=count),
        out_shape=shapes,
        in_specs=[VMEM()] * (len(arrays) + 2),
        out_specs=[VMEM()] * len(shapes),
        scratch_shapes=[
            pltpu.VMEM((WINDOW, WIDE), F32),
            pltpu.VMEM((8, PIECES * BOARD_LEAVES, WIDE), BF16),
            pltpu.VMEM((WINDOW, WIDE), F32),
        ],
        compiler_params=pltpu.CompilerParams(vmem_limit_bytes=40 << 20),
        name="second",
    )(*arrays, own_matrix, side_matrix)


def local(chance_reach, regrets_start, pot, parent, hand_cards, board_cards, hand_rank):
    chance = chance_reach[0]
    regrets = regrets_start[0]
    index = lax.axis_index(LEAF)
    devices = lax.axis_size(LEAF)
    leaf_count = parent.shape[1]
    odd = index % 2 == 1

    padded = jnp.concatenate(
        [jnp.full((SIDE,), -1, jnp.int32), parent[0], jnp.full((SIDE,), -2, jnp.int32)]
    )
    nodes = lax.dynamic_slice_in_dim(padded, index * OWN, WINDOW).astype(F32)
    ranks = hand_rank.astype(F32)
    held = board_cards[:, :, None, None] == hand_cards.T[None, None]
    free = 1.0 - jnp.any(held, axis=(1, 2)).astype(F32)

    def row(vector):
        return jnp.pad(vector[None], ((0, 0), (0, HANDS - vector.shape[0])))

    swap = [(0, 1), (1, 0)]
    part = lax.ppermute(
        jnp.concatenate([regrets, chance, row(nodes)], axis=0), "player", swap
    )
    last = jnp.concatenate(
        [regrets[OWN - 15 :], chance[OWN - 10 :], ranks[2:4], free[2:4], row(pot[SIDE:])], axis=0
    )
    start = jnp.concatenate(
        [regrets[:15], chance[:10], ranks[0:2], free[0:2], row(pot[:SIDE])], axis=0
    )
    even = lax.ppermute(
        jnp.where(odd, start, last), LEAF, [(i, i ^ 1) for i in range(devices)]
    )
    cross = lax.ppermute(
        jnp.where(odd, last, start),
        LEAF,
        [(i, i + 1) for i in range(1, devices - 1, 2)]
        + [(i + 1, i) for i in range(1, devices - 1, 2)],
    )
    left = jnp.where(odd, even, cross)
    right = jnp.where(odd, cross, even)
    edge = lax.ppermute(
        jnp.concatenate([left[5:15], right[0:10], left[20:25], right[15:20]], axis=0),
        "player",
        swap,
    )

    def widened(array):
        return jnp.pad(array, ((0, 8 - array.shape[0]), (0, WIDE - HANDS)))

    holding = holding_table(hand_cards)
    own_matrix = build(holding, widened(ranks), 4)
    side_matrix = build(holding, widened(jnp.concatenate([left[25:27], right[25:27]], axis=0)), 4)
    all_free = widened(jnp.concatenate([left[27:29], free, right[27:29]], axis=0))
    all_pot = jnp.concatenate([left[29, :SIDE], pot, right[29, :SIDE]])
    all_pot = jnp.broadcast_to(all_pot[:, None], (WINDOW, 128))
    both = jnp.stack([nodes, part[2 * OWN, :WINDOW]])
    same = (both[:, :, None] == both[:, None, :]).astype(BF16)
    same = jnp.concatenate([same, same, same], axis=2)

    def gathered(sums):
        return lax.all_to_all(sums.reshape(devices, 1, 128), LEAF, 0, 0).reshape(128, 128)

    count = float(leaf_count * HANDS)
    window, reached, instant, sums = first(
        odd.astype(jnp.int32)[None], regrets, chance, even, cross, part, edge,
        same, all_free, all_pot, own_matrix, side_matrix,
    )
    values, moved, mine, sums = second(
        gathered(sums), window, reached, instant, same, all_free, all_pot,
        own_matrix, side_matrix, count,
    )
    squares = jnp.sum(gathered(sums)[:, 0])
    scale = jnp.sqrt(squares / count + EPSILON)
    final = (moved + mine / scale)[:, :HANDS]
    return (final[None], values[None])


def solution(mesh):
    split = Mesh(
        mesh.devices.reshape(4, 4, 4, 2, mesh.shape["player"]),
        ("leaf_0", "leaf_1", "leaf_2", "leaf_3", "player"),
    )
    placed = (
        P("player", LEAF, None),
        P("player", LEAF, None),
        P(LEAF),
        P("player", None),
        P(),
        P(LEAF, None),
        P(LEAF, None),
    )
    return jax.shard_map(
        local,
        mesh=split,
        in_specs=placed,
        out_specs=(P("player", LEAF, None), P("player", LEAF, None)),
        check_vma=False,
    )
```

```python
import functools

import jax
import jax.numpy as jnp
from jax import lax
from jax.experimental import pallas as pl
from jax.experimental.pallas import tpu as pltpu
from jax.sharding import Mesh
from jax.sharding import PartitionSpec as P

LEAF = ("leaf_0", "leaf_1", "leaf_2", "leaf_3")
DELTA = 0.05
EPSILON = 1e-06

HANDS = 1326
WIDE = 1408
OWN = 32
SIDE = 16
WINDOW = OWN + 2 * SIDE
BOARD_LEAVES = 8
EDGE = 30
LIMIT = 16 << 20
SMALL = 6 << 20
PIECES = 2
BF16 = jnp.bfloat16
F32 = jnp.float32
VMEM = functools.partial(pl.BlockSpec, memory_space=pltpu.VMEM)


def pack_kernel(
    odd_ref, boards_hbm, pot_ref, regrets_hbm, chance_hbm, rank_hbm, cards_hbm,
    part_ref, even_ref, cross_ref, wide_rank_ref, free_ref, holding_ref,
    board_cards_ref, rank_ref, cards_ref, sems,
):
    regrets_ref, chance_ref = part_ref.at[:OWN], part_ref.at[OWN:]
    copies = [
        pltpu.make_async_copy(source, target, sems.at[at])
        for at, (source, target) in enumerate(
            [
                (regrets_hbm, regrets_ref),
                (chance_hbm, chance_ref),
                (rank_hbm, rank_ref),
                (cards_hbm, cards_ref),
                (boards_hbm, board_cards_ref),
            ]
        )
    ]
    for copy in copies:
        copy.start()
    for copy in copies:
        copy.wait()
    ranks = rank_ref[...].astype(F32)
    lower, upper = cards_ref[0:1, :], cards_ref[1:2, :]
    rows = []
    for b in range(4):
        taken = jnp.zeros((1, HANDS), jnp.bool_)
        for j in range(5):
            card = board_cards_ref[b, j]
            taken = taken | (lower == card) | (upper == card)
        rows.append(jnp.where(taken, 0.0, 1.0))
    wide_rank_ref[...] = jnp.zeros_like(wide_rank_ref)
    free_ref[...] = jnp.zeros_like(free_ref)
    wide_rank_ref[0:4, :HANDS] = ranks
    for b in range(4):
        free_ref[b : b + 1, :HANDS] = rows[b]
    deck = lax.broadcasted_iota(jnp.int32, (128, HANDS), 0)
    holding_ref[...] = jnp.zeros_like(holding_ref)
    holding_ref[:, :HANDS] = jnp.where((deck == lower) | (deck == upper), 1.0, 0.0).astype(BF16)

    def ends(ref, last):
        at = OWN - 15 if last else 0
        ref[0:15] = regrets_ref[at : at + 15]
        at = OWN - 10 if last else 0
        ref[15:25] = chance_ref[at : at + 10]
        at = 2 if last else 0
        ref[25:27] = ranks[at : at + 2]
        ref[27:28] = rows[at]
        ref[28:29] = rows[at + 1]
        ref[29:30] = jnp.zeros((1, HANDS), F32)
        at = SIDE if last else 0
        ref[29:30, 0:128] = pot_ref[at // SIDE : at // SIDE + 1, :]

    @pl.when(odd_ref[0] == 1)
    def _():
        ends(even_ref, False)
        ends(cross_ref, True)

    @pl.when(odd_ref[0] != 1)
    def _():
        ends(even_ref, True)
        ends(cross_ref, False)


SMEM = functools.partial(pl.BlockSpec, memory_space=pltpu.SMEM)
HBM = functools.partial(pl.BlockSpec, memory_space=pltpu.HBM)


def pack(odd, board_cards, pot_rows, regrets, chance, hand_rank, cards):
    shapes = (
        jax.ShapeDtypeStruct((2 * OWN, HANDS), F32),
        jax.ShapeDtypeStruct((EDGE, HANDS), F32),
        jax.ShapeDtypeStruct((EDGE, HANDS), F32),
        jax.ShapeDtypeStruct((8, WIDE), F32),
        jax.ShapeDtypeStruct((8, WIDE), F32),
        jax.ShapeDtypeStruct((128, WIDE), BF16),
    )
    return pl.pallas_call(
        pack_kernel,
        out_shape=shapes,
        in_specs=[SMEM(), HBM(), VMEM(), HBM(), HBM(), HBM(), HBM()],
        out_specs=[VMEM()] * len(shapes),
        scratch_shapes=[
            pltpu.SMEM((4, 5), jnp.int32),
            pltpu.VMEM((4, HANDS), jnp.int32),
            pltpu.VMEM((2, HANDS), jnp.int32),
            pltpu.SemaphoreType.DMA((5,)),
        ],
        compiler_params=pltpu.CompilerParams(vmem_limit_bytes=SMALL),
        name="pack",
    )(odd, board_cards, pot_rows, regrets, chance, hand_rank, cards)


def sides(odd_ref, even_ref, cross_ref, rows):
    odd = odd_ref[0] == 1
    even, cross = even_ref[rows], cross_ref[rows]
    return jnp.where(odd, even, cross), jnp.where(odd, cross, even)


def edges_kernel(odd_ref, even_ref, cross_ref, nodes_ref, token_ref, edge_ref):
    left, right = sides(odd_ref, even_ref, cross_ref, slice(0, 25))
    edge_ref[0:10] = left[5:15]
    edge_ref[10:20] = right[0:10]
    edge_ref[20:25] = left[20:25]
    edge_ref[25:30] = right[15:20]
    edge_ref[30:31] = jnp.zeros((1, HANDS), F32)
    edge_ref[30:31, 0:128] = nodes_ref[...] + token_ref[0:1, :]


def edges(odd, even, cross, nodes, token):
    return pl.pallas_call(
        edges_kernel,
        out_shape=jax.ShapeDtypeStruct((31, HANDS), F32),
        in_specs=[SMEM()] + [VMEM()] * 4,
        out_specs=VMEM(),
        compiler_params=pltpu.CompilerParams(vmem_limit_bytes=SMALL),
        name="edges",
    )(odd, even, cross, nodes, token)


ROWS = 128


def fill(rank_ref, apart_ref, column_ref, targets):
    ranks = rank_ref[...]
    for t in range(WIDE // 128):
        lanes = slice(t * 128, (t + 1) * 128)
        tile = jnp.concatenate([ranks[:, lanes], jnp.zeros((120, 128), F32)], axis=0)
        column_ref[lanes, :] = tile.T

    @pl.loop(0, WIDE // ROWS)
    def _(i):
        rows = pl.ds(pl.multiple_of(i * ROWS, ROWS), ROWS)
        column = column_ref[rows, :]
        own = [jnp.broadcast_to(column[:, b : b + 1], (ROWS, 128)) for b, _, _ in targets]
        for t in range(WIDE // 128):
            lanes = slice(t * 128, (t + 1) * 128)
            apart = apart_ref[rows, lanes]
            minus = -apart
            for at, (b, matrix_ref, slot) in enumerate(targets):
                gap = (own[at] - rank_ref[b : b + 1, lanes]).astype(BF16)
                matrix_ref[slot, rows, lanes] = jnp.minimum(jnp.maximum(gap, minus), apart)


def build_a_kernel(holding_ref, rank_ref, matrix_ref, apart_ref, token_ref, column_ref):
    token_ref[...] = jnp.zeros_like(token_ref)
    holding = holding_ref[...]
    shared = jnp.dot(holding.T, holding, preferred_element_type=F32)
    apart_ref[...] = (1.0 - jnp.minimum(shared, 1.0)).astype(BF16)
    fill(rank_ref, apart_ref, column_ref, [(0, matrix_ref, 0), (1, matrix_ref, 1)])


def build_b_kernel(
    odd_ref, even_ref, cross_ref, own_rank_ref, apart_ref,
    matrix_ref, near_ref, far_ref, rank_ref, column_ref,
):
    left, right = sides(odd_ref, even_ref, cross_ref, slice(25, 27))
    rank_ref[...] = own_rank_ref[...]
    rank_ref[4:6, :HANDS] = left
    rank_ref[6:8, :HANDS] = right
    targets = [(2, matrix_ref, 0), (3, matrix_ref, 1), (5, near_ref, 0), (6, near_ref, 1)]
    fill(rank_ref, apart_ref, column_ref, targets + [(4, far_ref, 0), (7, far_ref, 1)])


def cost(boards):
    return pl.CostEstimate(
        flops=boards * WIDE * WIDE * 8, bytes_accessed=boards * WIDE * WIDE * 2, transcendentals=0
    )


MATRIX = jax.ShapeDtypeStruct((2, WIDE, WIDE), BF16)


def build_a(holding, ranks):
    return pl.pallas_call(
        build_a_kernel,
        out_shape=(
            MATRIX,
            jax.ShapeDtypeStruct((WIDE, WIDE), BF16),
            jax.ShapeDtypeStruct((8, 128), F32),
        ),
        in_specs=[VMEM()] * 2,
        out_specs=[VMEM()] * 3,
        scratch_shapes=[pltpu.VMEM((WIDE, 128), F32)],
        compiler_params=pltpu.CompilerParams(vmem_limit_bytes=LIMIT),
        cost_estimate=cost(2),
        name="build_a",
    )(holding, ranks)


def build_b(odd, even, cross, ranks, apart):
    return pl.pallas_call(
        build_b_kernel,
        out_shape=(MATRIX, MATRIX, MATRIX),
        in_specs=[SMEM()] + [VMEM()] * 4,
        out_specs=[VMEM()] * 3,
        scratch_shapes=[pltpu.VMEM((8, WIDE), F32), pltpu.VMEM((WIDE, 128), F32)],
        compiler_params=pltpu.CompilerParams(vmem_limit_bytes=LIMIT),
        cost_estimate=cost(6),
        name="build_b",
    )(odd, even, cross, ranks, apart)


def node_totals(same, values):
    high = values.astype(BF16)
    rest = values - high.astype(F32)
    middle = rest.astype(BF16)
    low = (rest - middle.astype(F32)).astype(BF16)
    parts = jnp.concatenate([high, middle, low], axis=0)
    return jnp.dot(same, parts, preferred_element_type=F32)


def policy_of(same, regrets):
    positive = jnp.maximum(regrets, 0.0) + DELTA
    return positive / node_totals(same, positive)


def split_terms(reach):
    high = reach.astype(BF16).astype(F32)
    return [high, reach - high]


def joined(out, first):
    middle = first + BOARD_LEAVES
    return out[first:middle] + out[middle : middle + BOARD_LEAVES]


def column_of(row):
    return jnp.broadcast_to(row, (128, 128)).T


def same_node(row):
    equal = jnp.where(jnp.broadcast_to(row, (128, 128)) == column_of(row), 1.0, 0.0)
    equal = equal[:WINDOW, :WINDOW]
    return jnp.concatenate([equal, equal, equal], axis=1).astype(BF16)


def board_rows(free, boards):
    return jnp.concatenate(
        [jnp.broadcast_to(free[b : b + 1], (BOARD_LEAVES, WIDE)) for b in boards], axis=0
    )


def first_kernel(
    odd_ref,
    packed_ref,
    even_ref,
    cross_ref,
    part_ref,
    edge_ref,
    nodes_ref,
    own_free_ref,
    own_pot_ref,
    first_matrix_ref,
    last_matrix_ref,
    near_ref,
    far_ref,
    window_ref,
    reached_ref,
    instant_ref,
    sums_ref,
    same_ref,
    free_ref,
    pot_ref,
    policy_ref,
    terms_ref,
    values_ref,
):
    left, right = sides(odd_ref, even_ref, cross_ref, slice(0, EDGE))
    same_ref[0] = same_node(nodes_ref[...])
    same_ref[1] = same_node(edge_ref[30:31, 0:128])
    free_ref[...] = jnp.zeros_like(free_ref)
    free_ref[0:2, :HANDS] = left[27:29]
    free_ref[2:6] = own_free_ref[0:4]
    free_ref[6:8, :HANDS] = right[27:29]
    pot_ref[0:SIDE] = column_of(left[29:30, 0:128])[:SIDE]
    pot_ref[SIDE : 2 * SIDE] = column_of(own_pot_ref[0:1, :])[:SIDE]
    pot_ref[2 * SIDE : 3 * SIDE] = column_of(own_pot_ref[1:2, :])[:SIDE]
    pot_ref[3 * SIDE : 4 * SIDE] = column_of(right[29:30, 0:128])[:SIDE]
    window_ref[...] = jnp.zeros_like(window_ref)
    reached_ref[...] = jnp.zeros_like(reached_ref)
    policy_ref[...] = jnp.zeros_like(policy_ref)
    low, high = SIDE, SIDE + OWN
    window_ref[0, low - 15 : low, :HANDS] = left[0:15]
    window_ref[0, low:high, :HANDS] = packed_ref[:OWN]
    window_ref[0, high : high + 15, :HANDS] = right[0:15]
    policy_ref[0, low - 10 : low, :HANDS] = left[15:25]
    policy_ref[0, low:high, :HANDS] = packed_ref[OWN:]
    policy_ref[0, high : high + 10, :HANDS] = right[15:25]
    window_ref[1, low - 10 : low, :HANDS] = edge_ref[0:10]
    window_ref[1, low:high, :HANDS] = part_ref[0:OWN]
    window_ref[1, high : high + 10, :HANDS] = edge_ref[10:20]
    reached_ref[low - 5 : low, :HANDS] = edge_ref[20:25]
    reached_ref[low:high, :HANDS] = part_ref[OWN : 2 * OWN]
    reached_ref[high : high + 5, :HANDS] = edge_ref[25:30]
    free = board_rows(free_ref, range(8))
    reached_ref[...] = reached_ref[...] * free
    terms = []
    for p in range(2):
        chance = policy_ref[0] * free if p == 0 else reached_ref[...]
        policy = policy_of(same_ref[p], window_ref[p])
        policy_ref[p] = policy
        terms.append(split_terms(chance * policy))
    for b in range(8):
        rows = slice(b * BOARD_LEAVES, (b + 1) * BOARD_LEAVES)
        block = jnp.concatenate([term[rows] for player in terms for term in player], axis=0)
        terms_ref[b] = block.astype(BF16)

    def board(b, matrix):
        out = jnp.dot(terms_ref[b], matrix, preferred_element_type=F32)
        rows = slice(b * BOARD_LEAVES, (b + 1) * BOARD_LEAVES)
        factor = pot_ref[rows, 0:1] * (-1.0 / HANDS)
        free = free_ref[b : b + 1, :]
        values_ref[1, rows, :] = joined(out, 0) * factor * free
        values_ref[0, rows, :] = joined(out, PIECES * BOARD_LEAVES) * factor * free

    board(2, first_matrix_ref[0])
    board(3, first_matrix_ref[1])
    board(4, last_matrix_ref[0])
    board(5, last_matrix_ref[1])
    board(1, near_ref[0])
    board(6, near_ref[1])
    board(0, far_ref[0])
    board(7, far_ref[1])

    sums = []
    for p in range(2):
        values = values_ref[p]
        instant = values - node_totals(same_ref[p], policy_ref[p] * values)
        instant_ref[p] = instant
        mine = instant[SIDE : SIDE + OWN]
        sums.append(jnp.sum(mine * mine))
    lane = lax.broadcasted_iota(jnp.int32, sums_ref.shape, 1)
    sums_ref[...] = jnp.where(lane == 0, sums[0], jnp.where(lane == 1, sums[1], 0.0))


def first(odd, packed, even, cross, part, edge, nodes, free, pot_rows, matrices):
    shapes = (
        jax.ShapeDtypeStruct((2, WINDOW, WIDE), F32),
        jax.ShapeDtypeStruct((WINDOW, WIDE), F32),
        jax.ShapeDtypeStruct((2, WINDOW, WIDE), F32),
        jax.ShapeDtypeStruct((128, 128), F32),
        jax.ShapeDtypeStruct((2, WINDOW, 3 * WINDOW), BF16),
        jax.ShapeDtypeStruct((8, WIDE), F32),
        jax.ShapeDtypeStruct((WINDOW, 128), F32),
    )
    arrays = (packed, even, cross, part, edge, nodes, free, pot_rows) + matrices
    return pl.pallas_call(
        first_kernel,
        out_shape=shapes,
        in_specs=[SMEM()] + [VMEM()] * len(arrays),
        out_specs=[VMEM()] * len(shapes),
        scratch_shapes=[
            pltpu.VMEM((2, WINDOW, WIDE), F32),
            pltpu.VMEM((8, 2 * PIECES * BOARD_LEAVES, WIDE), BF16),
            pltpu.VMEM((2, WINDOW, WIDE), F32),
        ],
        compiler_params=pltpu.CompilerParams(vmem_limit_bytes=LIMIT),
        name="first",
    )(odd, *arrays)


def second_kernel(
    gathered_ref,
    window_ref,
    reached_ref,
    instant_ref,
    same_ref,
    free_ref,
    pot_ref,
    first_matrix_ref,
    last_matrix_ref,
    near_ref,
    out_values_ref,
    moved_ref,
    mine_ref,
    sums_ref,
    policy_ref,
    terms_ref,
    values_ref,
    *,
    count,
):
    values_ref[...] = jnp.zeros_like(values_ref)
    sums = jnp.sum(gathered_ref[...], axis=0, keepdims=True)
    scale = jnp.sqrt(sums / count + EPSILON)
    moved = window_ref[0] + instant_ref[0] / scale[:, 0:1]
    moved_ref[...] = moved[SIDE : SIDE + OWN]
    policy_ref[...] = policy_of(same_ref[0], moved)
    other = window_ref[1] + instant_ref[1] / scale[:, 1:2]
    terms = split_terms(reached_ref[...] * policy_of(same_ref[1], other))
    for b in range(8):
        rows = slice(b * BOARD_LEAVES, (b + 1) * BOARD_LEAVES)
        block = jnp.concatenate([term[rows] for term in terms], axis=0)
        terms_ref[b] = block.astype(BF16)

    def board(b, matrix):
        out = jnp.dot(terms_ref[b], matrix, preferred_element_type=F32)
        rows = slice(b * BOARD_LEAVES, (b + 1) * BOARD_LEAVES)
        factor = pot_ref[rows, 0:1] * (-1.0 / HANDS)
        values_ref[rows, :] = joined(out, 0) * factor * free_ref[b : b + 1, :]

    board(2, first_matrix_ref[0])
    board(3, first_matrix_ref[1])
    board(4, last_matrix_ref[0])
    board(5, last_matrix_ref[1])
    board(1, near_ref[0])
    board(6, near_ref[1])

    values = values_ref[...]
    instant = values - node_totals(same_ref[0], policy_ref[...] * values)
    mine = instant[SIDE : SIDE + OWN]
    mine_ref[...] = mine
    out_values_ref[...] = values[SIDE : SIDE + OWN, :HANDS]
    lane = lax.broadcasted_iota(jnp.int32, sums_ref.shape, 1)
    sums_ref[...] = jnp.where(lane == 0, jnp.sum(mine * mine), 0.0)


def second(gathered, window, reached, instant, same, free, pot, matrices, count):
    shapes = (
        jax.ShapeDtypeStruct((OWN, HANDS), F32),
        jax.ShapeDtypeStruct((OWN, WIDE), F32),
        jax.ShapeDtypeStruct((OWN, WIDE), F32),
        jax.ShapeDtypeStruct((128, 128), F32),
    )
    arrays = (gathered, window, reached, instant, same, free, pot) + matrices
    return pl.pallas_call(
        functools.partial(second_kernel, count=count),
        out_shape=shapes,
        in_specs=[VMEM()] * len(arrays),
        out_specs=[VMEM()] * len(shapes),
        scratch_shapes=[
            pltpu.VMEM((WINDOW, WIDE), F32),
            pltpu.VMEM((8, PIECES * BOARD_LEAVES, WIDE), BF16),
            pltpu.VMEM((WINDOW, WIDE), F32),
        ],
        compiler_params=pltpu.CompilerParams(vmem_limit_bytes=LIMIT),
        name="second",
    )(*arrays)


def tail_kernel(gathered_ref, moved_ref, mine_ref, out_ref, *, count):
    sums = jnp.sum(gathered_ref[...], axis=0, keepdims=True)
    scale = jnp.sqrt(sums / count + EPSILON)[:, 0:1]
    out_ref[...] = (moved_ref[...] + mine_ref[...] / scale)[:, :HANDS]


def tail(gathered, moved, mine, count):
    return pl.pallas_call(
        functools.partial(tail_kernel, count=count),
        out_shape=jax.ShapeDtypeStruct((OWN, HANDS), F32),
        in_specs=[VMEM()] * 3,
        out_specs=VMEM(),
        compiler_params=pltpu.CompilerParams(vmem_limit_bytes=SMALL),
        name="tail",
    )(gathered, moved, mine)


def local(chance_reach, regrets_start, pot, parent, hand_cards, board_cards, hand_rank):
    chance = chance_reach[0]
    regrets = regrets_start[0]
    index = lax.axis_index(LEAF)
    devices = lax.axis_size(LEAF)
    leaf_count = parent.shape[1]
    odd = lax.rem(index, 2).astype(jnp.int32)[None]

    pot_rows = jnp.pad(pot.reshape(2, SIDE), ((0, 0), (0, 128 - SIDE)))
    packed, even, cross, ranks, free, holding = pack(
        odd, board_cards, pot_rows, regrets, chance, hand_rank, hand_cards.T
    )
    swap = [(0, 1), (1, 0)]
    part = lax.ppermute(packed, "player", swap)
    even = lax.ppermute(even, LEAF, [(i, i ^ 1) for i in range(devices)])
    cross = lax.ppermute(
        cross,
        LEAF,
        [(i, i + 1) for i in range(1, devices - 1, 2)]
        + [(i + 1, i) for i in range(1, devices - 1, 2)],
    )
    padded = jnp.pad(parent[0], (SIDE, 128), constant_values=-1)
    nodes = lax.dynamic_slice_in_dim(padded, index * OWN, 128).astype(F32)[None]
    first_matrix, apart, token = build_a(holding, ranks)
    edge = lax.ppermute(edges(odd, even, cross, nodes, token), "player", swap)
    last_matrix, near, far = build_b(odd, even, cross, ranks, apart)

    def gathered(sums):
        return lax.all_to_all(sums.reshape(devices, 1, 128), LEAF, 0, 0).reshape(128, 128)

    count = float(leaf_count * HANDS)
    window, reached, instant, sums, same, all_free, all_pot = first(
        odd, packed, even, cross, part, edge, nodes, free, pot_rows,
        (first_matrix, last_matrix, near, far),
    )
    values, moved, mine, sums = second(
        gathered(sums), window, reached, instant, same, all_free, all_pot,
        (first_matrix, last_matrix, near), count,
    )
    final = tail(gathered(sums), moved, mine, count)
    return (final[None], values[None])


def solution(mesh):
    split = Mesh(
        mesh.devices.reshape(4, 4, 4, 2, mesh.shape["player"]),
        ("leaf_0", "leaf_1", "leaf_2", "leaf_3", "player"),
    )
    placed = (
        P("player", LEAF, None),
        P("player", LEAF, None),
        P(LEAF),
        P("player", None),
        P(),
        P(LEAF, None),
        P(LEAF, None),
    )
    return jax.shard_map(
        local,
        mesh=split,
        in_specs=placed,
        out_specs=(P("player", LEAF, None), P("player", LEAF, None)),
        check_vma=False,
    )
```

```python
import functools

import jax
import jax.numpy as jnp
from jax import lax
from jax.experimental import pallas as pl
from jax.experimental.pallas import tpu as pltpu
from jax.sharding import Mesh
from jax.sharding import PartitionSpec as P

LEAF = ("leaf_0", "leaf_1", "leaf_2", "leaf_3")
DELTA = 0.05
EPSILON = 1e-06

HANDS = 1326
WIDE = 1408
OWN = 32
SIDE = 16
WINDOW = OWN + 2 * SIDE
BOARD_LEAVES = 8
EDGE = 30
LIMIT = 10 << 20
SMALL = 6 << 20
PIECES = 2
BF16 = jnp.bfloat16
F32 = jnp.float32
VMEM = functools.partial(pl.BlockSpec, memory_space=pltpu.VMEM)


def pack_kernel(
    place_ref, boards_hbm, pot_ref, regrets_hbm, chance_hbm, rank_hbm, cards_hbm, parent_hbm,
    part_ref, even_ref, cross_ref, even_other_ref, cross_other_ref,
    wide_rank_ref, free_ref, holding_ref, pots_ref, nodes_ref,
    board_cards_ref, rank_ref, cards_ref, parent_ref, sems,
):
    regrets_ref, chance_ref = part_ref.at[:OWN], part_ref.at[OWN : 2 * OWN]
    moves = [
        (boards_hbm, board_cards_ref),
        (rank_hbm, rank_ref),
        (cards_hbm, cards_ref),
        (parent_hbm, parent_ref),
        (regrets_hbm, regrets_ref),
        (chance_hbm, chance_ref),
    ]
    copies = [
        pltpu.make_async_copy(source, target, sems.at[at])
        for at, (source, target) in enumerate(moves)
    ]
    for copy in copies:
        copy.start()
    pots_ref[...] = jnp.zeros_like(pots_ref)
    pots_ref[0:1, 0:OWN] = pot_ref[...]
    wide_rank_ref[...] = jnp.zeros_like(wide_rank_ref)
    free_ref[...] = jnp.zeros_like(free_ref)
    holding_ref[...] = jnp.zeros_like(holding_ref)
    for copy in copies[:4]:
        copy.wait()
    ranks = rank_ref[...].astype(F32)
    lower, upper = cards_ref[0:1, :], cards_ref[1:2, :]
    rows = []
    for b in range(4):
        taken = jnp.zeros((1, HANDS), jnp.bool_)
        for j in range(5):
            card = board_cards_ref[b, j]
            taken = taken | (lower == card) | (upper == card)
        rows.append(jnp.where(taken, 0.0, 1.0))
    wide_rank_ref[0:4, :HANDS] = ranks
    for b in range(4):
        free_ref[b : b + 1, :HANDS] = rows[b]
    deck = lax.broadcasted_iota(jnp.int32, (128, HANDS), 0)
    holding_ref[:, :HANDS] = jnp.where((deck == lower) | (deck == upper), 1.0, 0.0).astype(BF16)

    leaves = parent_ref.shape[0] * 128
    begin = place_ref[0] * OWN - SIDE
    line = (begin + 128) // 128 - 1
    held = [
        parent_ref[pl.ds(jnp.clip(line + j, 0, leaves // 128 - 1), 1), :].astype(F32)
        for j in range(2)
    ]
    held = jnp.broadcast_to(jnp.concatenate(held, axis=1), (8, 256))
    held = pltpu.roll(held, lax.rem((line + 2) * 128 - begin, 256), 1)[0:1, 0:128]
    leaf = begin + lax.broadcasted_iota(jnp.int32, (1, 128), 1)
    held = jnp.where((leaf >= 0) & (leaf < leaves), held, -1.0)
    nodes_ref[...] = jnp.broadcast_to(held, nodes_ref.shape)
    for copy in copies[4:]:
        copy.wait()

    def ends(ref, other_ref, last):
        at = OWN - 15 if last else 0
        ref[0:15] = regrets_ref[at : at + 15]
        at = OWN - 10 if last else 0
        ref[15:25] = chance_ref[at : at + 10]
        other_ref[0:10] = regrets_ref[at : at + 10]
        at = OWN - 5 if last else 0
        other_ref[10:15] = chance_ref[at : at + 5]
        other_ref[15:16] = jnp.zeros((1, HANDS), F32)
        at = 2 if last else 0
        ref[25:27] = ranks[at : at + 2]
        ref[27:28] = rows[at]
        ref[28:29] = rows[at + 1]
        ref[29:30] = jnp.zeros((1, HANDS), F32)
        ref[29:30, 0:128] = pots_ref[0:1, :]

    @pl.when(place_ref[1] == 1)
    def _():
        ends(even_ref, even_other_ref, False)
        ends(cross_ref, cross_other_ref, True)

    @pl.when(place_ref[1] != 1)
    def _():
        ends(even_ref, even_other_ref, True)
        ends(cross_ref, cross_other_ref, False)

    part_ref[2 * OWN :] = jnp.zeros((1, HANDS), F32)
    part_ref[2 * OWN :, 0:128] = held


SMEM = functools.partial(pl.BlockSpec, memory_space=pltpu.SMEM)
HBM = functools.partial(pl.BlockSpec, memory_space=pltpu.HBM)


def in_hbm(array):
    return pltpu.with_memory_space_constraint(array, pltpu.HBM)


def pack(place, board_cards, pot_row, regrets, chance, hand_rank, cards, parent):
    shapes = (
        jax.ShapeDtypeStruct((2 * OWN + 1, HANDS), F32),
        jax.ShapeDtypeStruct((EDGE, HANDS), F32),
        jax.ShapeDtypeStruct((EDGE, HANDS), F32),
        jax.ShapeDtypeStruct((16, HANDS), F32),
        jax.ShapeDtypeStruct((16, HANDS), F32),
        jax.ShapeDtypeStruct((8, WIDE), F32),
        jax.ShapeDtypeStruct((8, WIDE), F32),
        jax.ShapeDtypeStruct((128, WIDE), BF16),
        jax.ShapeDtypeStruct((8, 128), F32),
        jax.ShapeDtypeStruct((8, 128), F32),
    )
    large = (regrets, chance, hand_rank, cards, parent)
    return pl.pallas_call(
        pack_kernel,
        out_shape=shapes,
        in_specs=[SMEM(), HBM(), VMEM()] + [HBM()] * len(large),
        out_specs=[VMEM()] * len(shapes),
        scratch_shapes=[
            pltpu.SMEM((4, 5), jnp.int32),
            pltpu.VMEM((4, HANDS), jnp.int32),
            pltpu.VMEM((2, HANDS), jnp.int32),
            pltpu.VMEM(parent.shape, jnp.int32),
            pltpu.SemaphoreType.DMA((6,)),
        ],
        compiler_params=pltpu.CompilerParams(vmem_limit_bytes=SMALL),
        name="pack",
    )(place, in_hbm(board_cards), pot_row, *map(in_hbm, large))


def sides(place_ref, even_ref, cross_ref, rows):
    odd = place_ref[1] == 1
    even, cross = even_ref[rows], cross_ref[rows]
    return jnp.where(odd, even, cross), jnp.where(odd, cross, even)


ROWS = 128


def fill(rank_ref, apart_ref, column_ref, targets):
    ranks = rank_ref[...]
    for t in range(WIDE // 128):
        lanes = slice(t * 128, (t + 1) * 128)
        tile = jnp.concatenate([ranks[:, lanes], jnp.zeros((120, 128), F32)], axis=0)
        column_ref[lanes, :] = tile.T

    @pl.loop(0, WIDE // ROWS)
    def _(i):
        rows = pl.ds(pl.multiple_of(i * ROWS, ROWS), ROWS)
        column = column_ref[rows, :]
        own = [jnp.broadcast_to(column[:, b : b + 1], (ROWS, 128)) for b, _, _ in targets]
        for t in range(WIDE // 128):
            lanes = slice(t * 128, (t + 1) * 128)
            apart = apart_ref[rows, lanes]
            minus = -apart
            for at, (b, matrix_ref, slot) in enumerate(targets):
                gap = (own[at] - rank_ref[b : b + 1, lanes]).astype(BF16)
                matrix_ref[slot, rows, lanes] = jnp.minimum(jnp.maximum(gap, minus), apart)


def build_own_kernel(holding_ref, rank_ref, matrix_ref, apart_ref, column_ref):
    holding = holding_ref[...]
    half = WIDE // 2
    for rows in (slice(0, half), slice(half, WIDE)):
        shared = jnp.dot(holding.T[rows], holding, preferred_element_type=F32)
        apart_ref[rows, :] = (1.0 - jnp.minimum(shared, 1.0)).astype(BF16)
    fill(rank_ref, apart_ref, column_ref, [(b, matrix_ref, b) for b in range(4)])


def build_side_kernel(
    place_ref, even_ref, cross_ref, apart_ref, near_ref, far_ref, rank_ref, column_ref
):
    left, right = sides(place_ref, even_ref, cross_ref, slice(25, 27))
    rank_ref[...] = jnp.zeros_like(rank_ref)
    rank_ref[0:2, :HANDS] = left
    rank_ref[2:4, :HANDS] = right
    targets = [(1, near_ref, 0), (2, near_ref, 1), (0, far_ref, 0), (3, far_ref, 1)]
    fill(rank_ref, apart_ref, column_ref, targets)


BUILD_COST = pl.CostEstimate(
    flops=32 * WIDE * WIDE, bytes_accessed=8 * WIDE * WIDE, transcendentals=0
)


def matrices_shape(boards):
    return jax.ShapeDtypeStruct((boards, WIDE, WIDE), BF16)


def build_own(holding, ranks):
    return pl.pallas_call(
        build_own_kernel,
        out_shape=(matrices_shape(4), jax.ShapeDtypeStruct((WIDE, WIDE), BF16)),
        in_specs=[VMEM()] * 2,
        out_specs=[VMEM()] * 2,
        scratch_shapes=[pltpu.VMEM((WIDE, 128), F32)],
        compiler_params=pltpu.CompilerParams(vmem_limit_bytes=LIMIT),
        cost_estimate=BUILD_COST,
        name="build_own",
    )(holding, ranks)


def build_side(place, even, cross, apart):
    return pl.pallas_call(
        build_side_kernel,
        out_shape=(matrices_shape(2), matrices_shape(2)),
        in_specs=[SMEM()] + [VMEM()] * 3,
        out_specs=[VMEM()] * 2,
        scratch_shapes=[pltpu.VMEM((8, WIDE), F32), pltpu.VMEM((WIDE, 128), F32)],
        compiler_params=pltpu.CompilerParams(vmem_limit_bytes=LIMIT),
        cost_estimate=BUILD_COST,
        name="build_side",
    )(place, even, cross, apart)


def node_totals(same, values):
    high = values.astype(BF16)
    rest = values - high.astype(F32)
    middle = rest.astype(BF16)
    low = (rest - middle.astype(F32)).astype(BF16)
    parts = jnp.concatenate([high, middle, low], axis=0)
    return jnp.dot(same, parts, preferred_element_type=F32)


def policy_of(same, regrets):
    positive = jnp.maximum(regrets, 0.0) + DELTA
    return positive / node_totals(same, positive)


def split_terms(reach):
    high = reach.astype(BF16).astype(F32)
    return [high, reach - high]


def joined(out, first):
    middle = first + BOARD_LEAVES
    return out[first:middle] + out[middle : middle + BOARD_LEAVES]


def column_of(row):
    return jnp.broadcast_to(row, (128, 128)).T


def same_node(row):
    equal = jnp.where(jnp.broadcast_to(row, (128, 128)) == column_of(row), 1.0, 0.0)
    equal = equal[:WINDOW, :WINDOW]
    return jnp.concatenate([equal, equal, equal], axis=1).astype(BF16)


def board_rows(free, boards):
    return jnp.concatenate(
        [jnp.broadcast_to(free[b : b + 1], (BOARD_LEAVES, WIDE)) for b in boards], axis=0
    )


def first_kernel(
    place_ref,
    packed_ref,
    even_ref,
    cross_ref,
    part_ref,
    even_other_ref,
    cross_other_ref,
    nodes_ref,
    own_free_ref,
    pots_ref,
    own_matrix_ref,
    near_ref,
    far_ref,
    window_ref,
    reached_ref,
    instant_ref,
    sums_ref,
    same_ref,
    free_ref,
    pot_ref,
    policy_ref,
    terms_ref,
    values_ref,
):
    left, right = sides(place_ref, even_ref, cross_ref, slice(0, EDGE))
    left_other, right_other = sides(place_ref, even_other_ref, cross_other_ref, slice(0, 15))
    same_ref[0] = same_node(nodes_ref[0:1, :])
    same_ref[1] = same_node(part_ref[2 * OWN :, 0:128])
    free_ref[...] = jnp.zeros_like(free_ref)
    free_ref[0:2, :HANDS] = left[27:29]
    free_ref[2:6] = own_free_ref[0:4]
    free_ref[6:8, :HANDS] = right[27:29]
    pot_ref[0:SIDE] = column_of(left[29:30, 0:128])[SIDE:OWN]
    pot_ref[SIDE : SIDE + OWN] = column_of(pots_ref[0:1, :])[:OWN]
    pot_ref[SIDE + OWN :] = column_of(right[29:30, 0:128])[:SIDE]
    window_ref[...] = jnp.zeros_like(window_ref)
    reached_ref[...] = jnp.zeros_like(reached_ref)
    policy_ref[...] = jnp.zeros_like(policy_ref)
    low, high = SIDE, SIDE + OWN
    window_ref[0, low - 15 : low, :HANDS] = left[0:15]
    window_ref[0, low:high, :HANDS] = packed_ref[:OWN]
    window_ref[0, high : high + 15, :HANDS] = right[0:15]
    policy_ref[0, low - 10 : low, :HANDS] = left[15:25]
    policy_ref[0, low:high, :HANDS] = packed_ref[OWN : 2 * OWN]
    policy_ref[0, high : high + 10, :HANDS] = right[15:25]
    window_ref[1, low - 10 : low, :HANDS] = left_other[0:10]
    window_ref[1, low:high, :HANDS] = part_ref[0:OWN]
    window_ref[1, high : high + 10, :HANDS] = right_other[0:10]
    reached_ref[low - 5 : low, :HANDS] = left_other[10:15]
    reached_ref[low:high, :HANDS] = part_ref[OWN : 2 * OWN]
    reached_ref[high : high + 5, :HANDS] = right_other[10:15]
    free = board_rows(free_ref, range(8))
    reached_ref[...] = reached_ref[...] * free
    terms = []
    for p in range(2):
        chance = policy_ref[0] * free if p == 0 else reached_ref[...]
        policy = policy_of(same_ref[p], window_ref[p])
        policy_ref[p] = policy
        terms.append(split_terms(chance * policy))
    for b in range(8):
        rows = slice(b * BOARD_LEAVES, (b + 1) * BOARD_LEAVES)
        block = jnp.concatenate([term[rows] for player in terms for term in player], axis=0)
        terms_ref[b] = block.astype(BF16)

    def board(b, matrix):
        out = jnp.dot(terms_ref[b], matrix, preferred_element_type=F32)
        rows = slice(b * BOARD_LEAVES, (b + 1) * BOARD_LEAVES)
        factor = pot_ref[rows, 0:1] * (-1.0 / HANDS)
        free = free_ref[b : b + 1, :]
        values_ref[1, rows, :] = joined(out, 0) * factor * free
        values_ref[0, rows, :] = joined(out, PIECES * BOARD_LEAVES) * factor * free

    for b in range(4):
        board(b + 2, own_matrix_ref[b])
    board(1, near_ref[0])
    board(6, near_ref[1])
    board(0, far_ref[0])
    board(7, far_ref[1])

    sums = []
    for p in range(2):
        values = values_ref[p]
        instant = values - node_totals(same_ref[p], policy_ref[p] * values)
        instant_ref[p] = instant
        mine = instant[SIDE : SIDE + OWN]
        sums.append(jnp.sum(mine * mine))
    lane = lax.broadcasted_iota(jnp.int32, sums_ref.shape, 1)
    sums_ref[...] = jnp.where(lane == 0, sums[0], jnp.where(lane == 1, sums[1], 0.0))


def first(place, arrays):
    shapes = (
        jax.ShapeDtypeStruct((2, WINDOW, WIDE), F32),
        jax.ShapeDtypeStruct((WINDOW, WIDE), F32),
        jax.ShapeDtypeStruct((2, WINDOW, WIDE), F32),
        jax.ShapeDtypeStruct((128, 128), F32),
        jax.ShapeDtypeStruct((2, WINDOW, 3 * WINDOW), BF16),
        jax.ShapeDtypeStruct((8, WIDE), F32),
        jax.ShapeDtypeStruct((WINDOW, 128), F32),
    )
    return pl.pallas_call(
        first_kernel,
        out_shape=shapes,
        in_specs=[SMEM()] + [VMEM()] * len(arrays),
        out_specs=[VMEM()] * len(shapes),
        scratch_shapes=[
            pltpu.VMEM((2, WINDOW, WIDE), F32),
            pltpu.VMEM((8, 2 * PIECES * BOARD_LEAVES, WIDE), BF16),
            pltpu.VMEM((2, WINDOW, WIDE), F32),
        ],
        compiler_params=pltpu.CompilerParams(vmem_limit_bytes=LIMIT),
        name="first",
    )(place, *arrays)


def second_kernel(
    gathered_ref,
    window_ref,
    reached_ref,
    instant_ref,
    same_ref,
    free_ref,
    pot_ref,
    own_matrix_ref,
    near_ref,
    out_values_ref,
    moved_ref,
    mine_ref,
    sums_ref,
    policy_ref,
    terms_ref,
    values_ref,
    *,
    count,
):
    values_ref[...] = jnp.zeros_like(values_ref)
    sums = jnp.sum(gathered_ref[...], axis=0, keepdims=True)
    scale = jnp.sqrt(sums / count + EPSILON)
    moved = window_ref[0] + instant_ref[0] / scale[:, 0:1]
    moved_ref[...] = moved[SIDE : SIDE + OWN]
    policy_ref[...] = policy_of(same_ref[0], moved)
    other = window_ref[1] + instant_ref[1] / scale[:, 1:2]
    terms = split_terms(reached_ref[...] * policy_of(same_ref[1], other))
    for b in range(8):
        rows = slice(b * BOARD_LEAVES, (b + 1) * BOARD_LEAVES)
        block = jnp.concatenate([term[rows] for term in terms], axis=0)
        terms_ref[b] = block.astype(BF16)

    def board(b, matrix):
        out = jnp.dot(terms_ref[b], matrix, preferred_element_type=F32)
        rows = slice(b * BOARD_LEAVES, (b + 1) * BOARD_LEAVES)
        factor = pot_ref[rows, 0:1] * (-1.0 / HANDS)
        values_ref[rows, :] = joined(out, 0) * factor * free_ref[b : b + 1, :]

    for b in range(4):
        board(b + 2, own_matrix_ref[b])
    board(1, near_ref[0])
    board(6, near_ref[1])

    values = values_ref[...]
    instant = values - node_totals(same_ref[0], policy_ref[...] * values)
    mine = instant[SIDE : SIDE + OWN]
    mine_ref[...] = mine
    out_values_ref[...] = values[SIDE : SIDE + OWN, :HANDS]
    lane = lax.broadcasted_iota(jnp.int32, sums_ref.shape, 1)
    sums_ref[...] = jnp.where(lane == 0, jnp.sum(mine * mine), 0.0)


def second(gathered, window, reached, instant, same, free, pot, matrices, count):
    shapes = (
        jax.ShapeDtypeStruct((OWN, HANDS), F32),
        jax.ShapeDtypeStruct((OWN, WIDE), F32),
        jax.ShapeDtypeStruct((OWN, WIDE), F32),
        jax.ShapeDtypeStruct((128, 128), F32),
    )
    arrays = (gathered, window, reached, instant, same, free, pot) + matrices
    return pl.pallas_call(
        functools.partial(second_kernel, count=count),
        out_shape=shapes,
        in_specs=[VMEM()] * len(arrays),
        out_specs=[VMEM()] * len(shapes),
        scratch_shapes=[
            pltpu.VMEM((WINDOW, WIDE), F32),
            pltpu.VMEM((8, PIECES * BOARD_LEAVES, WIDE), BF16),
            pltpu.VMEM((WINDOW, WIDE), F32),
        ],
        compiler_params=pltpu.CompilerParams(vmem_limit_bytes=LIMIT),
        name="second",
    )(*arrays)


def tail_kernel(gathered_ref, moved_ref, mine_ref, out_ref, *, count):
    sums = jnp.sum(gathered_ref[...], axis=0, keepdims=True)
    scale = jnp.sqrt(sums / count + EPSILON)[:, 0:1]
    out_ref[...] = (moved_ref[...] + mine_ref[...] / scale)[:, :HANDS]


def tail(gathered, moved, mine, count):
    return pl.pallas_call(
        functools.partial(tail_kernel, count=count),
        out_shape=jax.ShapeDtypeStruct((OWN, HANDS), F32),
        in_specs=[VMEM()] * 3,
        out_specs=VMEM(),
        compiler_params=pltpu.CompilerParams(vmem_limit_bytes=SMALL),
        name="tail",
    )(gathered, moved, mine)


def local(chance_reach, regrets_start, pot, parent, hand_cards, board_cards, hand_rank):
    index = lax.axis_index(LEAF).astype(jnp.int32)
    devices = lax.axis_size(LEAF)
    leaf_count = parent.shape[1]
    place = jnp.stack([index, lax.rem(index, 2)])

    even_pairs = [(i, i ^ 1) for i in range(devices)]
    cross_pairs = [(i, i + 1) for i in range(1, devices - 1, 2)]
    cross_pairs = cross_pairs + [(j, i) for i, j in cross_pairs]

    def diagonal(pairs):
        return [(2 * i + p, 2 * j + 1 - p) for i, j in pairs for p in range(2)]

    packed, even, cross, even_other, cross_other, ranks, free, holding, pots, nodes = pack(
        place, board_cards, pot[None], regrets_start[0], chance_reach[0], hand_rank,
        hand_cards.T, parent.reshape(-1, 128),
    )
    both = LEAF + ("player",)
    part = lax.ppermute(packed, "player", [(0, 1), (1, 0)])
    even = lax.ppermute(even, LEAF, even_pairs)
    cross = lax.ppermute(cross, LEAF, cross_pairs)
    even_other = lax.ppermute(even_other, both, diagonal(even_pairs))
    cross_other = lax.ppermute(cross_other, both, diagonal(cross_pairs))

    own_matrix, apart = build_own(holding, ranks)
    near, far = build_side(place, even, cross, apart)

    def gathered(sums):
        return lax.all_to_all(sums.reshape(devices, 1, 128), LEAF, 0, 0).reshape(128, 128)

    count = float(leaf_count * HANDS)
    window, reached, instant, sums, same, all_free, all_pot = first(
        place,
        (packed, even, cross, part, even_other, cross_other, nodes, free, pots)
        + (own_matrix, near, far),
    )
    values, moved, mine, sums = second(
        gathered(sums), window, reached, instant, same, all_free, all_pot,
        (own_matrix, near), count,
    )
    final = tail(gathered(sums), moved, mine, count)
    return (final[None], values[None])


def solution(mesh):
    split = Mesh(
        mesh.devices.reshape(4, 4, 4, 2, mesh.shape["player"]),
        ("leaf_0", "leaf_1", "leaf_2", "leaf_3", "player"),
    )
    placed = (
        P("player", LEAF, None),
        P("player", LEAF, None),
        P(LEAF),
        P("player", None),
        P(),
        P(LEAF, None),
        P(LEAF, None),
    )
    return jax.shard_map(
        local,
        mesh=split,
        in_specs=placed,
        out_specs=(P("player", LEAF, None), P("player", LEAF, None)),
        check_vma=False,
    )
```

```python
import functools

import jax
import jax.numpy as jnp
from jax import lax
from jax.experimental import pallas as pl
from jax.experimental.pallas import tpu as pltpu
from jax.sharding import Mesh
from jax.sharding import PartitionSpec as P

LEAF = ("leaf_0", "leaf_1", "leaf_2", "leaf_3")
DELTA = 0.05
EPSILON = 1e-06

HANDS = 1326
WIDE = 1408
OWN = 32
SIDE = 16
WINDOW = OWN + 2 * SIDE
BOARD_LEAVES = 8
EDGE = 66
LIMIT = 10 << 20
SMALL = 6 << 20
PIECES = 2
BF16 = jnp.bfloat16
F32 = jnp.float32
VMEM = functools.partial(pl.BlockSpec, memory_space=pltpu.VMEM)


def edge_rows(rows_ref, edge_ref, last):
    at = OWN - 10 if last else 0
    edge_ref[0:10] = rows_ref[at : at + 10]
    at = 2 * OWN - 5 if last else OWN
    edge_ref[10:15] = rows_ref[at : at + 5]
    edge_ref[15:16] = jnp.zeros((1, HANDS), F32)


def forward_kernel(place_ref, part_ref, after_ref, edge_ref):
    @pl.when(place_ref[1] == 1)
    def _():
        edge_rows(part_ref, edge_ref, False)

    @pl.when(place_ref[1] != 1)
    def _():
        edge_rows(part_ref, edge_ref, True)


def forward(place, part, after):
    return pl.pallas_call(
        forward_kernel,
        out_shape=jax.ShapeDtypeStruct((16, HANDS), F32),
        in_specs=[SMEM(), VMEM(), VMEM()],
        out_specs=VMEM(),
        compiler_params=pltpu.CompilerParams(vmem_limit_bytes=SMALL),
        name="forward",
    )(place, part, after)


def pack_kernel(
    place_ref, boards_hbm, pot_ref, regrets_hbm, chance_hbm, rank_hbm, cards_hbm, parent_hbm,
    part_ref, even_ref, cross_ref, cross_other_ref,
    wide_rank_ref, free_ref, holding_ref, pots_ref, nodes_ref,
    board_cards_ref, rank_ref, cards_ref, parent_ref, sems,
):
    regrets_ref, chance_ref = part_ref.at[:OWN], part_ref.at[OWN : 2 * OWN]
    moves = [
        (boards_hbm, board_cards_ref),
        (rank_hbm, rank_ref),
        (cards_hbm, cards_ref),
        (parent_hbm, parent_ref),
        (regrets_hbm, regrets_ref),
        (chance_hbm, chance_ref),
    ]
    copies = [
        pltpu.make_async_copy(source, target, sems.at[at])
        for at, (source, target) in enumerate(moves)
    ]
    for copy in copies:
        copy.start()
    pots_ref[...] = jnp.zeros_like(pots_ref)
    pots_ref[0:1, 0:OWN] = pot_ref[...]
    wide_rank_ref[...] = jnp.zeros_like(wide_rank_ref)
    free_ref[...] = jnp.zeros_like(free_ref)
    holding_ref[...] = jnp.zeros_like(holding_ref)
    for copy in copies[:4]:
        copy.wait()
    ranks = rank_ref[...].astype(F32)
    lower, upper = cards_ref[0:1, :], cards_ref[1:2, :]
    rows = []
    for b in range(4):
        taken = jnp.zeros((1, HANDS), jnp.bool_)
        for j in range(5):
            card = board_cards_ref[b, j]
            taken = taken | (lower == card) | (upper == card)
        rows.append(jnp.where(taken, 0.0, 1.0))
    wide_rank_ref[0:4, :HANDS] = ranks
    for b in range(4):
        free_ref[b : b + 1, :HANDS] = rows[b]
    deck = lax.broadcasted_iota(jnp.int32, (128, HANDS), 0)
    holding_ref[:, :HANDS] = jnp.where((deck == lower) | (deck == upper), 1.0, 0.0).astype(BF16)

    leaves = parent_ref.shape[0] * 128
    begin = place_ref[0] * OWN - SIDE
    line = (begin + 128) // 128 - 1
    held = [
        parent_ref[pl.ds(jnp.clip(line + j, 0, leaves // 128 - 1), 1), :].astype(F32)
        for j in range(2)
    ]
    held = jnp.broadcast_to(jnp.concatenate(held, axis=1), (8, 256))
    held = pltpu.roll(held, lax.rem((line + 2) * 128 - begin, 256), 1)[0:1, 0:128]
    leaf = begin + lax.broadcasted_iota(jnp.int32, (1, 128), 1)
    held = jnp.where((leaf >= 0) & (leaf < leaves), held, -1.0)
    nodes_ref[...] = jnp.broadcast_to(held, nodes_ref.shape)
    for copy in copies[4:]:
        copy.wait()

    def ends(ref, last):
        at = OWN - 15 if last else 0
        ref[0:15] = regrets_ref[at : at + 15]
        at = OWN - 10 if last else 0
        ref[15:25] = chance_ref[at : at + 10]
        at = 2 if last else 0
        ref[25:27] = ranks[at : at + 2]
        ref[27:28] = rows[at]
        ref[28:29] = rows[at + 1]
        ref[29:30] = jnp.zeros((1, HANDS), F32)
        ref[29:30, 0:128] = pots_ref[0:1, :]
        ref[30:] = jnp.zeros((EDGE - 30, HANDS), F32)

    @pl.when(place_ref[1] == 1)
    def _():
        ends(even_ref, False)
        ends(cross_ref, True)
        edge_rows(part_ref, cross_other_ref, True)

    @pl.when(place_ref[1] != 1)
    def _():
        ends(even_ref, True)
        ends(cross_ref, False)
        edge_rows(part_ref, cross_other_ref, False)

    part_ref[2 * OWN :] = jnp.zeros((1, HANDS), F32)
    part_ref[2 * OWN :, 0:128] = held


SMEM = functools.partial(pl.BlockSpec, memory_space=pltpu.SMEM)
HBM = functools.partial(pl.BlockSpec, memory_space=pltpu.HBM)


def in_hbm(array):
    return pltpu.with_memory_space_constraint(array, pltpu.HBM)


def pack(place, board_cards, pot_row, regrets, chance, hand_rank, cards, parent):
    shapes = (
        jax.ShapeDtypeStruct((2 * OWN + 1, HANDS), F32),
        jax.ShapeDtypeStruct((EDGE, HANDS), F32),
        jax.ShapeDtypeStruct((EDGE, HANDS), F32),
        jax.ShapeDtypeStruct((16, HANDS), F32),
        jax.ShapeDtypeStruct((8, WIDE), F32),
        jax.ShapeDtypeStruct((8, WIDE), F32),
        jax.ShapeDtypeStruct((128, WIDE), BF16),
        jax.ShapeDtypeStruct((8, 128), F32),
        jax.ShapeDtypeStruct((8, 128), F32),
    )
    large = (regrets, chance, hand_rank, cards, parent)
    return pl.pallas_call(
        pack_kernel,
        out_shape=shapes,
        in_specs=[SMEM(), HBM(), VMEM()] + [HBM()] * len(large),
        out_specs=[VMEM()] * len(shapes),
        scratch_shapes=[
            pltpu.SMEM((4, 5), jnp.int32),
            pltpu.VMEM((4, HANDS), jnp.int32),
            pltpu.VMEM((2, HANDS), jnp.int32),
            pltpu.VMEM(parent.shape, jnp.int32),
            pltpu.SemaphoreType.DMA((6,)),
        ],
        compiler_params=pltpu.CompilerParams(vmem_limit_bytes=SMALL),
        name="pack",
    )(place, in_hbm(board_cards), pot_row, *map(in_hbm, large))


def sides(place_ref, even_ref, cross_ref, rows):
    odd = place_ref[1] == 1
    even, cross = even_ref[rows], cross_ref[rows]
    return jnp.where(odd, even, cross), jnp.where(odd, cross, even)


ROWS = 128


def fill(rank_ref, apart_ref, column_ref, targets):
    ranks = rank_ref[...]
    for t in range(WIDE // 128):
        lanes = slice(t * 128, (t + 1) * 128)
        tile = jnp.concatenate([ranks[:, lanes], jnp.zeros((120, 128), F32)], axis=0)
        column_ref[lanes, :] = tile.T

    @pl.loop(0, WIDE // ROWS)
    def _(i):
        rows = pl.ds(pl.multiple_of(i * ROWS, ROWS), ROWS)
        column = column_ref[rows, :]
        own = [jnp.broadcast_to(column[:, b : b + 1], (ROWS, 128)) for b, _, _ in targets]
        for t in range(WIDE // 128):
            lanes = slice(t * 128, (t + 1) * 128)
            apart = apart_ref[rows, lanes]
            minus = -apart
            for at, (b, matrix_ref, slot) in enumerate(targets):
                gap = (own[at] - rank_ref[b : b + 1, lanes]).astype(BF16)
                matrix_ref[slot, rows, lanes] = jnp.minimum(jnp.maximum(gap, minus), apart)


def build_own_kernel(holding_ref, rank_ref, matrix_ref, apart_ref, column_ref):
    holding = holding_ref[...]
    half = WIDE // 2
    for rows in (slice(0, half), slice(half, WIDE)):
        shared = jnp.dot(holding.T[rows], holding, preferred_element_type=F32)
        apart_ref[rows, :] = (1.0 - jnp.minimum(shared, 1.0)).astype(BF16)
    fill(rank_ref, apart_ref, column_ref, [(b, matrix_ref, b) for b in range(4)])


def build_side_kernel(
    place_ref, even_ref, cross_ref, apart_ref, near_ref, far_ref, token_ref, rank_ref, column_ref
):
    token_ref[...] = jnp.zeros_like(token_ref)
    left, right = sides(place_ref, even_ref, cross_ref, slice(25, 27))
    rank_ref[...] = jnp.zeros_like(rank_ref)
    rank_ref[0:2, :HANDS] = left
    rank_ref[2:4, :HANDS] = right
    targets = [(1, near_ref, 0), (2, near_ref, 1), (0, far_ref, 0), (3, far_ref, 1)]
    fill(rank_ref, apart_ref, column_ref, targets)


BUILD_COST = pl.CostEstimate(
    flops=32 * WIDE * WIDE, bytes_accessed=8 * WIDE * WIDE, transcendentals=0
)


def matrices_shape(boards):
    return jax.ShapeDtypeStruct((boards, WIDE, WIDE), BF16)


def build_own(holding, ranks):
    return pl.pallas_call(
        build_own_kernel,
        out_shape=(matrices_shape(4), jax.ShapeDtypeStruct((WIDE, WIDE), BF16)),
        in_specs=[VMEM()] * 2,
        out_specs=[VMEM()] * 2,
        scratch_shapes=[pltpu.VMEM((WIDE, 128), F32)],
        compiler_params=pltpu.CompilerParams(vmem_limit_bytes=LIMIT),
        cost_estimate=BUILD_COST,
        name="build_own",
    )(holding, ranks)


def build_side(place, even, cross, apart):
    return pl.pallas_call(
        build_side_kernel,
        out_shape=(
            matrices_shape(2),
            matrices_shape(2),
            jax.ShapeDtypeStruct((8, 128), F32),
        ),
        in_specs=[SMEM()] + [VMEM()] * 3,
        out_specs=[VMEM()] * 3,
        scratch_shapes=[pltpu.VMEM((8, WIDE), F32), pltpu.VMEM((WIDE, 128), F32)],
        compiler_params=pltpu.CompilerParams(vmem_limit_bytes=LIMIT),
        cost_estimate=BUILD_COST,
        name="build_side",
    )(place, even, cross, apart)


def node_totals(same, values):
    high = values.astype(BF16)
    rest = values - high.astype(F32)
    middle = rest.astype(BF16)
    low = (rest - middle.astype(F32)).astype(BF16)
    parts = jnp.concatenate([high, middle, low], axis=0)
    return jnp.dot(same, parts, preferred_element_type=F32)


def policy_of(same, regrets):
    positive = jnp.maximum(regrets, 0.0) + DELTA
    return positive / node_totals(same, positive)


def split_terms(reach):
    high = reach.astype(BF16).astype(F32)
    return [high, reach - high]


def joined(out, first):
    middle = first + BOARD_LEAVES
    return out[first:middle] + out[middle : middle + BOARD_LEAVES]


def column_of(row):
    return jnp.broadcast_to(row, (128, 128)).T


def same_node(row):
    equal = jnp.where(jnp.broadcast_to(row, (128, 128)) == column_of(row), 1.0, 0.0)
    equal = equal[:WINDOW, :WINDOW]
    return jnp.concatenate([equal, equal, equal], axis=1).astype(BF16)


def board_rows(free, boards):
    return jnp.concatenate(
        [jnp.broadcast_to(free[b : b + 1], (BOARD_LEAVES, WIDE)) for b in boards], axis=0
    )


def first_kernel(
    place_ref,
    packed_ref,
    even_ref,
    cross_ref,
    part_ref,
    even_other_ref,
    cross_other_ref,
    nodes_ref,
    own_free_ref,
    pots_ref,
    own_matrix_ref,
    near_ref,
    far_ref,
    window_ref,
    reached_ref,
    instant_ref,
    sums_ref,
    same_ref,
    free_ref,
    pot_ref,
    policy_ref,
    terms_ref,
    values_ref,
):
    left, right = sides(place_ref, even_ref, cross_ref, slice(0, 30))
    left_other, right_other = sides(place_ref, even_other_ref, cross_other_ref, slice(0, 15))
    same_ref[0] = same_node(nodes_ref[0:1, :])
    same_ref[1] = same_node(part_ref[2 * OWN :, 0:128])
    free_ref[...] = jnp.zeros_like(free_ref)
    free_ref[0:2, :HANDS] = left[27:29]
    free_ref[2:6] = own_free_ref[0:4]
    free_ref[6:8, :HANDS] = right[27:29]
    pot_ref[0:SIDE] = column_of(left[29:30, 0:128])[SIDE:OWN]
    pot_ref[SIDE : SIDE + OWN] = column_of(pots_ref[0:1, :])[:OWN]
    pot_ref[SIDE + OWN :] = column_of(right[29:30, 0:128])[:SIDE]
    window_ref[...] = jnp.zeros_like(window_ref)
    reached_ref[...] = jnp.zeros_like(reached_ref)
    policy_ref[...] = jnp.zeros_like(policy_ref)
    low, high = SIDE, SIDE + OWN
    window_ref[0, low - 15 : low, :HANDS] = left[0:15]
    window_ref[0, low:high, :HANDS] = packed_ref[:OWN]
    window_ref[0, high : high + 15, :HANDS] = right[0:15]
    policy_ref[0, low - 10 : low, :HANDS] = left[15:25]
    policy_ref[0, low:high, :HANDS] = packed_ref[OWN : 2 * OWN]
    policy_ref[0, high : high + 10, :HANDS] = right[15:25]
    window_ref[1, low - 10 : low, :HANDS] = left_other[0:10]
    window_ref[1, low:high, :HANDS] = part_ref[0:OWN]
    window_ref[1, high : high + 10, :HANDS] = right_other[0:10]
    reached_ref[low - 5 : low, :HANDS] = left_other[10:15]
    reached_ref[low:high, :HANDS] = part_ref[OWN : 2 * OWN]
    reached_ref[high : high + 5, :HANDS] = right_other[10:15]
    free = board_rows(free_ref, range(8))
    reached_ref[...] = reached_ref[...] * free
    terms = []
    for p in range(2):
        chance = policy_ref[0] * free if p == 0 else reached_ref[...]
        policy = policy_of(same_ref[p], window_ref[p])
        policy_ref[p] = policy
        terms.append(split_terms(chance * policy))
    for b in range(8):
        rows = slice(b * BOARD_LEAVES, (b + 1) * BOARD_LEAVES)
        block = jnp.concatenate([term[rows] for player in terms for term in player], axis=0)
        terms_ref[b] = block.astype(BF16)

    def board(b, matrix):
        out = jnp.dot(terms_ref[b], matrix, preferred_element_type=F32)
        rows = slice(b * BOARD_LEAVES, (b + 1) * BOARD_LEAVES)
        factor = pot_ref[rows, 0:1] * (-1.0 / HANDS)
        free = free_ref[b : b + 1, :]
        values_ref[1, rows, :] = joined(out, 0) * factor * free
        values_ref[0, rows, :] = joined(out, PIECES * BOARD_LEAVES) * factor * free

    for b in range(4):
        board(b + 2, own_matrix_ref[b])
    board(1, near_ref[0])
    board(6, near_ref[1])
    board(0, far_ref[0])
    board(7, far_ref[1])

    sums = []
    for p in range(2):
        values = values_ref[p]
        instant = values - node_totals(same_ref[p], policy_ref[p] * values)
        instant_ref[p] = instant
        mine = instant[SIDE : SIDE + OWN]
        sums.append(jnp.sum(mine * mine))
    lane = lax.broadcasted_iota(jnp.int32, sums_ref.shape, 1)
    sums_ref[...] = jnp.where(lane == 0, sums[0], jnp.where(lane == 1, sums[1], 0.0))


def first(place, arrays):
    shapes = (
        jax.ShapeDtypeStruct((2, WINDOW, WIDE), F32),
        jax.ShapeDtypeStruct((WINDOW, WIDE), F32),
        jax.ShapeDtypeStruct((2, WINDOW, WIDE), F32),
        jax.ShapeDtypeStruct((128, 128), F32),
        jax.ShapeDtypeStruct((2, WINDOW, 3 * WINDOW), BF16),
        jax.ShapeDtypeStruct((8, WIDE), F32),
        jax.ShapeDtypeStruct((WINDOW, 128), F32),
    )
    return pl.pallas_call(
        first_kernel,
        out_shape=shapes,
        in_specs=[SMEM()] + [VMEM()] * len(arrays),
        out_specs=[VMEM()] * len(shapes),
        scratch_shapes=[
            pltpu.VMEM((2, WINDOW, WIDE), F32),
            pltpu.VMEM((8, 2 * PIECES * BOARD_LEAVES, WIDE), BF16),
            pltpu.VMEM((2, WINDOW, WIDE), F32),
        ],
        compiler_params=pltpu.CompilerParams(vmem_limit_bytes=LIMIT),
        name="first",
    )(place, *arrays)


def second_kernel(
    gathered_ref,
    window_ref,
    reached_ref,
    instant_ref,
    same_ref,
    free_ref,
    pot_ref,
    own_matrix_ref,
    near_ref,
    out_values_ref,
    moved_ref,
    mine_ref,
    sums_ref,
    policy_ref,
    terms_ref,
    values_ref,
    *,
    count,
):
    values_ref[...] = jnp.zeros_like(values_ref)
    sums = jnp.sum(gathered_ref[...], axis=0, keepdims=True)
    scale = jnp.sqrt(sums / count + EPSILON)
    moved = window_ref[0] + instant_ref[0] / scale[:, 0:1]
    moved_ref[...] = moved[SIDE : SIDE + OWN]
    policy_ref[...] = policy_of(same_ref[0], moved)
    other = window_ref[1] + instant_ref[1] / scale[:, 1:2]
    terms = split_terms(reached_ref[...] * policy_of(same_ref[1], other))
    for b in range(8):
        rows = slice(b * BOARD_LEAVES, (b + 1) * BOARD_LEAVES)
        block = jnp.concatenate([term[rows] for term in terms], axis=0)
        terms_ref[b] = block.astype(BF16)

    def board(b, matrix):
        out = jnp.dot(terms_ref[b], matrix, preferred_element_type=F32)
        rows = slice(b * BOARD_LEAVES, (b + 1) * BOARD_LEAVES)
        factor = pot_ref[rows, 0:1] * (-1.0 / HANDS)
        values_ref[rows, :] = joined(out, 0) * factor * free_ref[b : b + 1, :]

    for b in range(4):
        board(b + 2, own_matrix_ref[b])
    board(1, near_ref[0])
    board(6, near_ref[1])

    values = values_ref[...]
    instant = values - node_totals(same_ref[0], policy_ref[...] * values)
    mine = instant[SIDE : SIDE + OWN]
    mine_ref[...] = mine
    out_values_ref[...] = values[SIDE : SIDE + OWN, :HANDS]
    lane = lax.broadcasted_iota(jnp.int32, sums_ref.shape, 1)
    sums_ref[...] = jnp.where(lane == 0, jnp.sum(mine * mine), 0.0)


def second(gathered, window, reached, instant, same, free, pot, matrices, count):
    shapes = (
        jax.ShapeDtypeStruct((OWN, HANDS), F32),
        jax.ShapeDtypeStruct((OWN, WIDE), F32),
        jax.ShapeDtypeStruct((OWN, WIDE), F32),
        jax.ShapeDtypeStruct((128, 128), F32),
    )
    arrays = (gathered, window, reached, instant, same, free, pot) + matrices
    return pl.pallas_call(
        functools.partial(second_kernel, count=count),
        out_shape=shapes,
        in_specs=[VMEM()] * len(arrays),
        out_specs=[VMEM()] * len(shapes),
        scratch_shapes=[
            pltpu.VMEM((WINDOW, WIDE), F32),
            pltpu.VMEM((8, PIECES * BOARD_LEAVES, WIDE), BF16),
            pltpu.VMEM((WINDOW, WIDE), F32),
        ],
        compiler_params=pltpu.CompilerParams(vmem_limit_bytes=LIMIT),
        name="second",
    )(*arrays)


def tail_kernel(gathered_ref, moved_ref, mine_ref, out_ref, *, count):
    sums = jnp.sum(gathered_ref[...], axis=0, keepdims=True)
    scale = jnp.sqrt(sums / count + EPSILON)[:, 0:1]
    out_ref[...] = (moved_ref[...] + mine_ref[...] / scale)[:, :HANDS]


def tail(gathered, moved, mine, count):
    return pl.pallas_call(
        functools.partial(tail_kernel, count=count),
        out_shape=jax.ShapeDtypeStruct((OWN, HANDS), F32),
        in_specs=[VMEM()] * 3,
        out_specs=VMEM(),
        compiler_params=pltpu.CompilerParams(vmem_limit_bytes=SMALL),
        name="tail",
    )(gathered, moved, mine)


def local(chance_reach, regrets_start, pot, parent, hand_cards, board_cards, hand_rank):
    index = lax.axis_index(LEAF).astype(jnp.int32)
    devices = lax.axis_size(LEAF)
    leaf_count = parent.shape[1]
    place = jnp.stack([index, lax.rem(index, 2)])

    even_pairs = [(i, i ^ 1) for i in range(devices)]
    cross_pairs = [(i, i + 1) for i in range(1, devices - 1, 2)]
    cross_pairs = cross_pairs + [(j, i) for i, j in cross_pairs]

    diagonal = [(2 * i + p, 2 * j + 1 - p) for i, j in cross_pairs for p in range(2)]

    packed, even, cross, cross_other, ranks, free, holding, pots, nodes = pack(
        place, board_cards, pot[None], regrets_start[0], chance_reach[0], hand_rank,
        hand_cards.T, parent.reshape(-1, 128),
    )
    cross = lax.ppermute(cross, LEAF, cross_pairs)
    even = lax.ppermute(even, LEAF, even_pairs)
    part = lax.ppermute(packed, "player", [(0, 1), (1, 0)])
    cross_other = lax.ppermute(cross_other, LEAF + ("player",), diagonal)

    own_matrix, apart = build_own(holding, ranks)
    near, far, built = build_side(place, even, cross, apart)

    even_other = lax.ppermute(forward(place, part, built), LEAF, even_pairs)

    def gathered(sums):
        return lax.all_to_all(sums.reshape(devices, 1, 128), LEAF, 0, 0).reshape(128, 128)

    count = float(leaf_count * HANDS)
    window, reached, instant, sums, same, all_free, all_pot = first(
        place,
        (packed, even, cross, part, even_other, cross_other, nodes, free, pots)
        + (own_matrix, near, far),
    )
    values, moved, mine, sums = second(
        gathered(sums), window, reached, instant, same, all_free, all_pot,
        (own_matrix, near), count,
    )
    final = tail(gathered(sums), moved, mine, count)
    return (final[None], values[None])


def solution(mesh):
    split = Mesh(
        mesh.devices.reshape(4, 4, 4, 2, mesh.shape["player"]),
        ("leaf_0", "leaf_1", "leaf_2", "leaf_3", "player"),
    )
    placed = (
        P("player", LEAF, None),
        P("player", LEAF, None),
        P(LEAF),
        P("player", None),
        P(),
        P(LEAF, None),
        P(LEAF, None),
    )
    return jax.shard_map(
        local,
        mesh=split,
        in_specs=placed,
        out_specs=(P("player", LEAF, None), P("player", LEAF, None)),
        check_vma=False,
    )
```

```python
import functools

import jax
import jax.numpy as jnp
from jax import lax
from jax.experimental import pallas as pl
from jax.experimental.pallas import tpu as pltpu
from jax.sharding import Mesh
from jax.sharding import PartitionSpec as P

LEAF = ("leaf_0", "leaf_1", "leaf_2", "leaf_3")
DELTA = 0.05
EPSILON = 1e-06

HANDS = 1326
WIDE = 1408
OWN = 32
SIDE = 16
WINDOW = OWN + 2 * SIDE
BOARD_LEAVES = 8
EDGE = 34
LIMIT = 10 << 20
SMALL = 6 << 20
PIECES = 2
BF16 = jnp.bfloat16
F32 = jnp.float32
VMEM = functools.partial(pl.BlockSpec, memory_space=pltpu.VMEM)


def edge_rows(regrets_ref, chance_ref, edge_ref, last):
    at = OWN - 10 if last else 0
    edge_ref[0:10] = regrets_ref[at : at + 10]
    at = OWN - 5 if last else 0
    edge_ref[10:15] = chance_ref[at : at + 5]
    edge_ref[15:16] = jnp.zeros((1, HANDS), F32)


def forward_kernel(place_ref, regrets_ref, chance_ref, after_ref, edge_ref):
    @pl.when(place_ref[1] == 1)
    def _():
        edge_rows(regrets_ref, chance_ref, edge_ref, False)

    @pl.when(place_ref[1] != 1)
    def _():
        edge_rows(regrets_ref, chance_ref, edge_ref, True)


def forward(place, regrets, chance, after):
    return pl.pallas_call(
        forward_kernel,
        out_shape=jax.ShapeDtypeStruct((16, HANDS), F32),
        in_specs=[SMEM()] + [VMEM()] * 3,
        out_specs=VMEM(),
        compiler_params=pltpu.CompilerParams(vmem_limit_bytes=SMALL),
        name="forward",
    )(place, regrets, chance, after)


def pack_kernel(
    place_ref, boards_hbm, pot_ref, regrets_hbm, chance_hbm, rank_hbm, cards_hbm, parent_hbm,
    regrets_ref, chance_ref, even_ref, cross_ref, cross_other_ref,
    wide_rank_ref, free_ref, holding_ref, pots_ref, nodes_ref,
    board_cards_ref, rank_ref, cards_ref, parent_ref, sems,
):
    moves = [
        (boards_hbm, board_cards_ref),
        (rank_hbm, rank_ref),
        (cards_hbm, cards_ref),
        (parent_hbm, parent_ref),
        (regrets_hbm, regrets_ref.at[:OWN]),
        (chance_hbm, chance_ref),
    ]
    copies = [
        pltpu.make_async_copy(source, target, sems.at[at])
        for at, (source, target) in enumerate(moves)
    ]
    for copy in copies:
        copy.start()
    pots_ref[...] = jnp.zeros_like(pots_ref)
    pots_ref[0:1, 0:OWN] = pot_ref[...]
    wide_rank_ref[...] = jnp.zeros_like(wide_rank_ref)
    free_ref[...] = jnp.zeros_like(free_ref)
    holding_ref[...] = jnp.zeros_like(holding_ref)
    for copy in copies[:4]:
        copy.wait()
    ranks = rank_ref[...].astype(F32)
    lower, upper = cards_ref[0:1, :], cards_ref[1:2, :]
    rows = []
    for b in range(4):
        taken = jnp.zeros((1, HANDS), jnp.bool_)
        for j in range(5):
            card = board_cards_ref[b, j]
            taken = taken | (lower == card) | (upper == card)
        rows.append(jnp.where(taken, 0.0, 1.0))
    wide_rank_ref[0:4, :HANDS] = ranks
    for b in range(4):
        free_ref[b : b + 1, :HANDS] = rows[b]
    deck = lax.broadcasted_iota(jnp.int32, (128, HANDS), 0)
    holding_ref[:, :HANDS] = jnp.where((deck == lower) | (deck == upper), 1.0, 0.0).astype(BF16)

    leaves = parent_ref.shape[0] * 128
    begin = place_ref[0] * OWN - SIDE
    line = (begin + 128) // 128 - 1
    held = [
        parent_ref[pl.ds(jnp.clip(line + j, 0, leaves // 128 - 1), 1), :].astype(F32)
        for j in range(2)
    ]
    held = jnp.broadcast_to(jnp.concatenate(held, axis=1), (8, 256))
    held = pltpu.roll(held, lax.rem((line + 2) * 128 - begin, 256), 1)[0:1, 0:128]
    leaf = begin + lax.broadcasted_iota(jnp.int32, (1, 128), 1)
    held = jnp.where((leaf >= 0) & (leaf < leaves), held, -1.0)
    nodes_ref[...] = jnp.broadcast_to(held, nodes_ref.shape)
    for copy in copies[4:]:
        copy.wait()

    def ends(ref, last):
        at = OWN - 15 if last else 0
        ref[0:15] = regrets_ref[at : at + 15]
        at = OWN - 10 if last else 0
        ref[15:25] = chance_ref[at : at + 10]
        at = 2 if last else 0
        ref[25:27] = ranks[at : at + 2]
        ref[27:28] = rows[at]
        ref[28:29] = rows[at + 1]
        ref[29:30] = jnp.zeros((1, HANDS), F32)
        ref[29:30, 0:128] = pots_ref[0:1, :]
        ref[30:] = jnp.zeros((EDGE - 30, HANDS), F32)

    @pl.when(place_ref[1] == 1)
    def _():
        ends(even_ref, False)
        ends(cross_ref, True)
        edge_rows(regrets_ref, chance_ref, cross_other_ref, True)

    @pl.when(place_ref[1] != 1)
    def _():
        ends(even_ref, True)
        ends(cross_ref, False)
        edge_rows(regrets_ref, chance_ref, cross_other_ref, False)

    regrets_ref[OWN:] = jnp.zeros((1, HANDS), F32)
    regrets_ref[OWN:, 0:128] = held


SMEM = functools.partial(pl.BlockSpec, memory_space=pltpu.SMEM)
HBM = functools.partial(pl.BlockSpec, memory_space=pltpu.HBM)


def in_hbm(array):
    return pltpu.with_memory_space_constraint(array, pltpu.HBM)


def pack(place, board_cards, pot_row, regrets, chance, hand_rank, cards, parent):
    shapes = (
        jax.ShapeDtypeStruct((OWN + 1, HANDS), F32),
        jax.ShapeDtypeStruct((OWN, HANDS), F32),
        jax.ShapeDtypeStruct((EDGE, HANDS), F32),
        jax.ShapeDtypeStruct((EDGE, HANDS), F32),
        jax.ShapeDtypeStruct((16, HANDS), F32),
        jax.ShapeDtypeStruct((8, WIDE), F32),
        jax.ShapeDtypeStruct((8, WIDE), F32),
        jax.ShapeDtypeStruct((128, WIDE), BF16),
        jax.ShapeDtypeStruct((8, 128), F32),
        jax.ShapeDtypeStruct((8, 128), F32),
    )
    large = (regrets, chance, hand_rank, cards, parent)
    return pl.pallas_call(
        pack_kernel,
        out_shape=shapes,
        in_specs=[SMEM(), HBM(), VMEM()] + [HBM()] * len(large),
        out_specs=[VMEM()] * len(shapes),
        scratch_shapes=[
            pltpu.SMEM((4, 5), jnp.int32),
            pltpu.VMEM((4, HANDS), jnp.int32),
            pltpu.VMEM((2, HANDS), jnp.int32),
            pltpu.VMEM(parent.shape, jnp.int32),
            pltpu.SemaphoreType.DMA((6,)),
        ],
        compiler_params=pltpu.CompilerParams(vmem_limit_bytes=SMALL),
        name="pack",
    )(place, in_hbm(board_cards), pot_row, *map(in_hbm, large))


def sides(place_ref, even_ref, cross_ref, rows):
    odd = place_ref[1] == 1
    even, cross = even_ref[rows], cross_ref[rows]
    return jnp.where(odd, even, cross), jnp.where(odd, cross, even)


ROWS = 128


def fill(rank_ref, apart_ref, column_ref, targets):
    ranks = rank_ref[...]
    for t in range(WIDE // 128):
        lanes = slice(t * 128, (t + 1) * 128)
        tile = jnp.concatenate([ranks[:, lanes], jnp.zeros((120, 128), F32)], axis=0)
        column_ref[lanes, :] = tile.T

    @pl.loop(0, WIDE // ROWS)
    def _(i):
        rows = pl.ds(pl.multiple_of(i * ROWS, ROWS), ROWS)
        column = column_ref[rows, :]
        own = [jnp.broadcast_to(column[:, b : b + 1], (ROWS, 128)) for b, _, _ in targets]
        for t in range(WIDE // 128):
            lanes = slice(t * 128, (t + 1) * 128)
            apart = apart_ref[rows, lanes]
            minus = -apart
            for at, (b, matrix_ref, slot) in enumerate(targets):
                gap = (own[at] - rank_ref[b : b + 1, lanes]).astype(BF16)
                matrix_ref[slot, rows, lanes] = jnp.minimum(jnp.maximum(gap, minus), apart)


def build_own_kernel(holding_ref, rank_ref, matrix_ref, apart_ref, column_ref):
    holding = holding_ref[...]
    half = WIDE // 2
    for rows in (slice(0, half), slice(half, WIDE)):
        shared = jnp.dot(holding.T[rows], holding, preferred_element_type=F32)
        apart_ref[rows, :] = (1.0 - jnp.minimum(shared, 1.0)).astype(BF16)
    fill(rank_ref, apart_ref, column_ref, [(b, matrix_ref, b) for b in range(4)])


def build_side_kernel(
    place_ref, even_ref, cross_ref, apart_ref, near_ref, far_ref, token_ref, rank_ref, column_ref
):
    token_ref[...] = jnp.zeros_like(token_ref)
    left, right = sides(place_ref, even_ref, cross_ref, slice(25, 27))
    rank_ref[...] = jnp.zeros_like(rank_ref)
    rank_ref[0:2, :HANDS] = left
    rank_ref[2:4, :HANDS] = right
    targets = [(1, near_ref, 0), (2, near_ref, 1), (0, far_ref, 0), (3, far_ref, 1)]
    fill(rank_ref, apart_ref, column_ref, targets)


BUILD_COST = pl.CostEstimate(
    flops=32 * WIDE * WIDE, bytes_accessed=8 * WIDE * WIDE, transcendentals=0
)


def matrices_shape(boards):
    return jax.ShapeDtypeStruct((boards, WIDE, WIDE), BF16)


def build_own(holding, ranks):
    return pl.pallas_call(
        build_own_kernel,
        out_shape=(matrices_shape(4), jax.ShapeDtypeStruct((WIDE, WIDE), BF16)),
        in_specs=[VMEM()] * 2,
        out_specs=[VMEM()] * 2,
        scratch_shapes=[pltpu.VMEM((WIDE, 128), F32)],
        compiler_params=pltpu.CompilerParams(vmem_limit_bytes=LIMIT),
        cost_estimate=BUILD_COST,
        name="build_own",
    )(holding, ranks)


def build_side(place, even, cross, apart):
    return pl.pallas_call(
        build_side_kernel,
        out_shape=(
            matrices_shape(2),
            matrices_shape(2),
            jax.ShapeDtypeStruct((8, 128), F32),
        ),
        in_specs=[SMEM()] + [VMEM()] * 3,
        out_specs=[VMEM()] * 3,
        scratch_shapes=[pltpu.VMEM((8, WIDE), F32), pltpu.VMEM((WIDE, 128), F32)],
        compiler_params=pltpu.CompilerParams(vmem_limit_bytes=LIMIT),
        cost_estimate=BUILD_COST,
        name="build_side",
    )(place, even, cross, apart)


def node_totals(same, values):
    high = values.astype(BF16)
    rest = values - high.astype(F32)
    middle = rest.astype(BF16)
    low = (rest - middle.astype(F32)).astype(BF16)
    parts = jnp.concatenate([high, middle, low], axis=0)
    return jnp.dot(same, parts, preferred_element_type=F32)


def policy_of(same, regrets):
    positive = jnp.maximum(regrets, 0.0) + DELTA
    return positive / node_totals(same, positive)


def split_terms(reach):
    high = reach.astype(BF16).astype(F32)
    return [high, reach - high]


def joined(out, first):
    middle = first + BOARD_LEAVES
    return out[first:middle] + out[middle : middle + BOARD_LEAVES]


def column_of(row):
    return jnp.broadcast_to(row, (128, 128)).T


def same_node(row):
    equal = jnp.where(jnp.broadcast_to(row, (128, 128)) == column_of(row), 1.0, 0.0)
    equal = equal[:WINDOW, :WINDOW]
    return jnp.concatenate([equal, equal, equal], axis=1).astype(BF16)


def board_rows(free, boards):
    return jnp.concatenate(
        [jnp.broadcast_to(free[b : b + 1], (BOARD_LEAVES, WIDE)) for b in boards], axis=0
    )


def first_kernel(
    place_ref,
    regrets_ref,
    chance_ref,
    even_ref,
    cross_ref,
    regrets_other_ref,
    chance_other_ref,
    even_other_ref,
    cross_other_ref,
    nodes_ref,
    own_free_ref,
    pots_ref,
    own_matrix_ref,
    near_ref,
    far_ref,
    window_ref,
    reached_ref,
    instant_ref,
    sums_ref,
    same_ref,
    free_ref,
    pot_ref,
    policy_ref,
    terms_ref,
    values_ref,
):
    left, right = sides(place_ref, even_ref, cross_ref, slice(0, 30))
    left_other, right_other = sides(place_ref, even_other_ref, cross_other_ref, slice(0, 15))
    same_ref[0] = same_node(nodes_ref[0:1, :])
    same_ref[1] = same_node(regrets_other_ref[OWN:, 0:128])
    free_ref[...] = jnp.zeros_like(free_ref)
    free_ref[0:2, :HANDS] = left[27:29]
    free_ref[2:6] = own_free_ref[0:4]
    free_ref[6:8, :HANDS] = right[27:29]
    pot_ref[0:SIDE] = column_of(left[29:30, 0:128])[SIDE:OWN]
    pot_ref[SIDE : SIDE + OWN] = column_of(pots_ref[0:1, :])[:OWN]
    pot_ref[SIDE + OWN :] = column_of(right[29:30, 0:128])[:SIDE]
    window_ref[...] = jnp.zeros_like(window_ref)
    reached_ref[...] = jnp.zeros_like(reached_ref)
    policy_ref[...] = jnp.zeros_like(policy_ref)
    low, high = SIDE, SIDE + OWN
    window_ref[0, low - 15 : low, :HANDS] = left[0:15]
    window_ref[0, low:high, :HANDS] = regrets_ref[:OWN]
    window_ref[0, high : high + 15, :HANDS] = right[0:15]
    policy_ref[0, low - 10 : low, :HANDS] = left[15:25]
    policy_ref[0, low:high, :HANDS] = chance_ref[...]
    policy_ref[0, high : high + 10, :HANDS] = right[15:25]
    window_ref[1, low - 10 : low, :HANDS] = left_other[0:10]
    window_ref[1, low:high, :HANDS] = regrets_other_ref[:OWN]
    window_ref[1, high : high + 10, :HANDS] = right_other[0:10]
    reached_ref[low - 5 : low, :HANDS] = left_other[10:15]
    reached_ref[low:high, :HANDS] = chance_other_ref[...]
    reached_ref[high : high + 5, :HANDS] = right_other[10:15]
    free = board_rows(free_ref, range(8))
    reached_ref[...] = reached_ref[...] * free
    terms = []
    for p in range(2):
        chance = policy_ref[0] * free if p == 0 else reached_ref[...]
        policy = policy_of(same_ref[p], window_ref[p])
        policy_ref[p] = policy
        terms.append(split_terms(chance * policy))
    for b in range(8):
        rows = slice(b * BOARD_LEAVES, (b + 1) * BOARD_LEAVES)
        block = jnp.concatenate([term[rows] for player in terms for term in player], axis=0)
        terms_ref[b] = block.astype(BF16)

    def board(b, matrix):
        out = jnp.dot(terms_ref[b], matrix, preferred_element_type=F32)
        rows = slice(b * BOARD_LEAVES, (b + 1) * BOARD_LEAVES)
        factor = pot_ref[rows, 0:1] * (-1.0 / HANDS)
        free = free_ref[b : b + 1, :]
        values_ref[1, rows, :] = joined(out, 0) * factor * free
        values_ref[0, rows, :] = joined(out, PIECES * BOARD_LEAVES) * factor * free

    for b in range(4):
        board(b + 2, own_matrix_ref[b])
    board(1, near_ref[0])
    board(6, near_ref[1])
    board(0, far_ref[0])
    board(7, far_ref[1])

    sums = []
    for p in range(2):
        values = values_ref[p]
        instant = values - node_totals(same_ref[p], policy_ref[p] * values)
        instant_ref[p] = instant
        mine = instant[SIDE : SIDE + OWN]
        sums.append(jnp.sum(mine * mine))
    lane = lax.broadcasted_iota(jnp.int32, sums_ref.shape, 1)
    sums_ref[...] = jnp.where(lane == 0, sums[0], jnp.where(lane == 1, sums[1], 0.0))


def first(place, arrays):
    shapes = (
        jax.ShapeDtypeStruct((2, WINDOW, WIDE), F32),
        jax.ShapeDtypeStruct((WINDOW, WIDE), F32),
        jax.ShapeDtypeStruct((2, WINDOW, WIDE), F32),
        jax.ShapeDtypeStruct((128, 128), F32),
        jax.ShapeDtypeStruct((2, WINDOW, 3 * WINDOW), BF16),
        jax.ShapeDtypeStruct((8, WIDE), F32),
        jax.ShapeDtypeStruct((WINDOW, 128), F32),
    )
    return pl.pallas_call(
        first_kernel,
        out_shape=shapes,
        in_specs=[SMEM()] + [VMEM()] * len(arrays),
        out_specs=[VMEM()] * len(shapes),
        scratch_shapes=[
            pltpu.VMEM((2, WINDOW, WIDE), F32),
            pltpu.VMEM((8, 2 * PIECES * BOARD_LEAVES, WIDE), BF16),
            pltpu.VMEM((2, WINDOW, WIDE), F32),
        ],
        compiler_params=pltpu.CompilerParams(vmem_limit_bytes=LIMIT),
        name="first",
    )(place, *arrays)


def second_kernel(
    gathered_ref,
    window_ref,
    reached_ref,
    instant_ref,
    same_ref,
    free_ref,
    pot_ref,
    own_matrix_ref,
    near_ref,
    out_values_ref,
    moved_ref,
    mine_ref,
    sums_ref,
    policy_ref,
    terms_ref,
    values_ref,
    *,
    count,
):
    values_ref[...] = jnp.zeros_like(values_ref)
    sums = jnp.sum(gathered_ref[...], axis=0, keepdims=True)
    scale = jnp.sqrt(sums / count + EPSILON)
    moved = window_ref[0] + instant_ref[0] / scale[:, 0:1]
    moved_ref[...] = moved[SIDE : SIDE + OWN]
    policy_ref[...] = policy_of(same_ref[0], moved)
    other = window_ref[1] + instant_ref[1] / scale[:, 1:2]
    terms = split_terms(reached_ref[...] * policy_of(same_ref[1], other))
    for b in range(8):
        rows = slice(b * BOARD_LEAVES, (b + 1) * BOARD_LEAVES)
        block = jnp.concatenate([term[rows] for term in terms], axis=0)
        terms_ref[b] = block.astype(BF16)

    def board(b, matrix):
        out = jnp.dot(terms_ref[b], matrix, preferred_element_type=F32)
        rows = slice(b * BOARD_LEAVES, (b + 1) * BOARD_LEAVES)
        factor = pot_ref[rows, 0:1] * (-1.0 / HANDS)
        values_ref[rows, :] = joined(out, 0) * factor * free_ref[b : b + 1, :]

    for b in range(4):
        board(b + 2, own_matrix_ref[b])
    board(1, near_ref[0])
    board(6, near_ref[1])

    values = values_ref[...]
    instant = values - node_totals(same_ref[0], policy_ref[...] * values)
    mine = instant[SIDE : SIDE + OWN]
    mine_ref[...] = mine
    out_values_ref[...] = values[SIDE : SIDE + OWN, :HANDS]
    lane = lax.broadcasted_iota(jnp.int32, sums_ref.shape, 1)
    sums_ref[...] = jnp.where(lane == 0, jnp.sum(mine * mine), 0.0)


def second(gathered, window, reached, instant, same, free, pot, matrices, count):
    shapes = (
        jax.ShapeDtypeStruct((OWN, HANDS), F32),
        jax.ShapeDtypeStruct((OWN, WIDE), F32),
        jax.ShapeDtypeStruct((OWN, WIDE), F32),
        jax.ShapeDtypeStruct((128, 128), F32),
    )
    arrays = (gathered, window, reached, instant, same, free, pot) + matrices
    return pl.pallas_call(
        functools.partial(second_kernel, count=count),
        out_shape=shapes,
        in_specs=[VMEM()] * len(arrays),
        out_specs=[VMEM()] * len(shapes),
        scratch_shapes=[
            pltpu.VMEM((WINDOW, WIDE), F32),
            pltpu.VMEM((8, PIECES * BOARD_LEAVES, WIDE), BF16),
            pltpu.VMEM((WINDOW, WIDE), F32),
        ],
        compiler_params=pltpu.CompilerParams(vmem_limit_bytes=LIMIT),
        name="second",
    )(*arrays)


def tail_kernel(gathered_ref, moved_ref, mine_ref, out_ref, *, count):
    sums = jnp.sum(gathered_ref[...], axis=0, keepdims=True)
    scale = jnp.sqrt(sums / count + EPSILON)[:, 0:1]
    out_ref[...] = (moved_ref[...] + mine_ref[...] / scale)[:, :HANDS]


def tail(gathered, moved, mine, count):
    return pl.pallas_call(
        functools.partial(tail_kernel, count=count),
        out_shape=jax.ShapeDtypeStruct((OWN, HANDS), F32),
        in_specs=[VMEM()] * 3,
        out_specs=VMEM(),
        compiler_params=pltpu.CompilerParams(vmem_limit_bytes=SMALL),
        name="tail",
    )(gathered, moved, mine)


def local(chance_reach, regrets_start, pot, parent, hand_cards, board_cards, hand_rank):
    index = lax.axis_index(LEAF).astype(jnp.int32)
    devices = lax.axis_size(LEAF)
    leaf_count = parent.shape[1]
    place = jnp.stack([index, lax.rem(index, 2)])

    even_pairs = [(i, i ^ 1) for i in range(devices)]
    cross_pairs = [(i, i + 1) for i in range(1, devices - 1, 2)]
    cross_pairs = cross_pairs + [(j, i) for i, j in cross_pairs]

    diagonal = [(2 * i + p, 2 * j + 1 - p) for i, j in cross_pairs for p in range(2)]

    regrets, chance, even, cross, cross_other, ranks, free, holding, pots, nodes = pack(
        place, board_cards, pot[None], regrets_start[0], chance_reach[0], hand_rank,
        hand_cards.T, parent.reshape(-1, 128),
    )
    cross = lax.ppermute(cross, LEAF, cross_pairs)
    even = lax.ppermute(even, LEAF, even_pairs)
    regrets_other = lax.ppermute(regrets, "player", [(0, 1), (1, 0)])
    chance_other = lax.ppermute(chance, "player", [(0, 1), (1, 0)])
    cross_other = lax.ppermute(cross_other, LEAF + ("player",), diagonal)

    own_matrix, apart = build_own(holding, ranks)
    near, far, built = build_side(place, even, cross, apart)

    even_other = lax.ppermute(forward(place, regrets_other, chance_other, built), LEAF, even_pairs)

    def gathered(sums):
        return lax.all_to_all(sums.reshape(devices, 1, 128), LEAF, 0, 0).reshape(128, 128)

    count = float(leaf_count * HANDS)
    window, reached, instant, sums, same, all_free, all_pot = first(
        place,
        (regrets, chance, even, cross, regrets_other, chance_other, even_other, cross_other)
        + (nodes, free, pots, own_matrix, near, far),
    )
    values, moved, mine, sums = second(
        gathered(sums), window, reached, instant, same, all_free, all_pot,
        (own_matrix, near), count,
    )
    final = tail(gathered(sums), moved, mine, count)
    return (final[None], values[None])


def solution(mesh):
    split = Mesh(
        mesh.devices.reshape(4, 4, 4, 2, mesh.shape["player"]),
        ("leaf_0", "leaf_1", "leaf_2", "leaf_3", "player"),
    )
    placed = (
        P("player", LEAF, None),
        P("player", LEAF, None),
        P(LEAF),
        P("player", None),
        P(),
        P(LEAF, None),
        P(LEAF, None),
    )
    return jax.shard_map(
        local,
        mesh=split,
        in_specs=placed,
        out_specs=(P("player", LEAF, None), P("player", LEAF, None)),
        check_vma=False,
    )
```

```python
import functools

import jax
import jax.numpy as jnp
from jax import lax
from jax.experimental import pallas as pl
from jax.experimental.pallas import tpu as pltpu
from jax.sharding import Mesh
from jax.sharding import PartitionSpec as P

LEAF = ("leaf_0", "leaf_1", "leaf_2", "leaf_3")
DELTA = 0.05
EPSILON = 1e-06

HANDS = 1326
WIDE = 1408
OWN = 32
SIDE = 16
WINDOW = OWN + 2 * SIDE
BOARD_LEAVES = 8
EDGE = 32
EARLY = 2
LIMIT = 10 << 20
SMALL = 6 << 20
PIECES = 2
BF16 = jnp.bfloat16
F32 = jnp.float32
VMEM = functools.partial(pl.BlockSpec, memory_space=pltpu.VMEM)


def edge_rows(regrets_ref, chance_ref, edge_ref, last):
    at = OWN - 10 if last else 0
    edge_ref[0:10] = regrets_ref[at : at + 10]
    if last:
        edge_ref[10 : 15 - EARLY] = chance_ref[OWN - 5 : OWN - EARLY]
        edge_ref[15 - EARLY : 15] = regrets_ref[OWN + 1 :]
    else:
        edge_ref[10:15] = chance_ref[0:5]
    edge_ref[15:16] = jnp.zeros((1, HANDS), F32)


def forward_kernel(place_ref, regrets_ref, chance_ref, after_ref, edge_ref):
    @pl.when(place_ref[1] == 1)
    def _():
        edge_rows(regrets_ref, chance_ref, edge_ref, False)

    @pl.when(place_ref[1] != 1)
    def _():
        edge_rows(regrets_ref, chance_ref, edge_ref, True)


def forward(place, regrets, chance, after):
    return pl.pallas_call(
        forward_kernel,
        out_shape=jax.ShapeDtypeStruct((16, HANDS), F32),
        in_specs=[SMEM(), VMEM(), VMEM(), SMEM()],
        out_specs=VMEM(),
        compiler_params=pltpu.CompilerParams(vmem_limit_bytes=SMALL),
        name="forward",
    )(place, regrets, chance, after)


def pack_kernel(
    place_ref, boards_hbm, pot_hbm, regrets_hbm, chance_hbm, rank_hbm, cards_hbm, parent_hbm,
    regrets_ref, chance_ref, even_ref, cross_ref, cross_other_ref,
    wide_rank_ref, free_ref, holding_ref, pots_ref, nodes_ref,
    board_cards_ref, pot_ref, rank_ref, cards_ref, parent_ref, all_chance_ref, sems,
):
    moves = [
        (boards_hbm, board_cards_ref),
        (rank_hbm, rank_ref),
        (cards_hbm, cards_ref),
        (parent_hbm, parent_ref),
        (regrets_hbm, regrets_ref.at[:OWN]),
        (chance_hbm, all_chance_ref),
        (pot_hbm, pot_ref),
    ]
    copies = [
        pltpu.make_async_copy(source, target, sems.at[at])
        for at, (source, target) in enumerate(moves)
    ]
    for copy in copies:
        copy.start()
    pots_ref[...] = jnp.zeros_like(pots_ref)
    wide_rank_ref[...] = jnp.zeros_like(wide_rank_ref)
    free_ref[...] = jnp.zeros_like(free_ref)
    holding_ref[...] = jnp.zeros_like(holding_ref)
    for copy in copies[:4]:
        copy.wait()
    ranks = rank_ref[...].astype(F32)
    lower, upper = cards_ref[0:1, :], cards_ref[1:2, :]
    rows = []
    for b in range(4):
        taken = jnp.zeros((1, HANDS), jnp.bool_)
        for j in range(5):
            card = board_cards_ref[b, j]
            taken = taken | (lower == card) | (upper == card)
        rows.append(jnp.where(taken, 0.0, 1.0))
    wide_rank_ref[0:4, :HANDS] = ranks
    for b in range(4):
        free_ref[b : b + 1, :HANDS] = rows[b]
    deck = lax.broadcasted_iota(jnp.int32, (128, HANDS), 0)
    holding_ref[:, :HANDS] = jnp.where((deck == lower) | (deck == upper), 1.0, 0.0).astype(BF16)

    leaves = parent_ref.shape[0] * 128
    begin = place_ref[0] * OWN - SIDE
    line = (begin + 128) // 128 - 1
    held = [
        parent_ref[pl.ds(jnp.clip(line + j, 0, leaves // 128 - 1), 1), :].astype(F32)
        for j in range(2)
    ]
    held = jnp.broadcast_to(jnp.concatenate(held, axis=1), (8, 256))
    held = pltpu.roll(held, lax.rem((line + 2) * 128 - begin, 256), 1)[0:1, 0:128]
    leaf = begin + lax.broadcasted_iota(jnp.int32, (1, 128), 1)
    held = jnp.where((leaf >= 0) & (leaf < leaves), held, -1.0)
    nodes_ref[...] = jnp.broadcast_to(held, nodes_ref.shape)
    for copy in copies[4:]:
        copy.wait()
    pots_ref[0:1, 0:OWN] = pot_ref[...]
    chance_ref[...] = all_chance_ref[0 : OWN - EARLY]
    regrets_ref[OWN + 1 :] = all_chance_ref[OWN - EARLY :]

    def ends(ref, last):
        at = OWN - 15 if last else 0
        ref[0:15] = regrets_ref[at : at + 15]
        at = OWN - 10 if last else 0
        ref[15:25] = all_chance_ref[at : at + 10]
        at = 2 if last else 0
        ref[25:27] = ranks[at : at + 2]
        ref[27:28] = rows[at]
        ref[28:29] = rows[at + 1]
        ref[29:30] = jnp.zeros((1, HANDS), F32)
        ref[29:30, 0:128] = pots_ref[0:1, :]
        ref[30:] = jnp.zeros((EDGE - 30, HANDS), F32)

    @pl.when(place_ref[1] == 1)
    def _():
        ends(even_ref, False)
        ends(cross_ref, True)
        edge_rows(regrets_ref, chance_ref, cross_other_ref, True)

    @pl.when(place_ref[1] != 1)
    def _():
        ends(even_ref, True)
        ends(cross_ref, False)
        edge_rows(regrets_ref, chance_ref, cross_other_ref, False)

    regrets_ref[OWN : OWN + 1] = jnp.zeros((1, HANDS), F32)
    regrets_ref[OWN : OWN + 1, 0:128] = held


SMEM = functools.partial(pl.BlockSpec, memory_space=pltpu.SMEM)
HBM = functools.partial(pl.BlockSpec, memory_space=pltpu.HBM)


def in_hbm(array):
    return pltpu.with_memory_space_constraint(array, pltpu.HBM)


def pack(place, board_cards, pot_row, regrets, chance, hand_rank, cards, parent):
    shapes = (
        jax.ShapeDtypeStruct((OWN + 1 + EARLY, HANDS), F32),
        jax.ShapeDtypeStruct((OWN - EARLY, HANDS), F32),
        jax.ShapeDtypeStruct((EDGE, HANDS), F32),
        jax.ShapeDtypeStruct((EDGE, HANDS), F32),
        jax.ShapeDtypeStruct((16, HANDS), F32),
        jax.ShapeDtypeStruct((8, WIDE), F32),
        jax.ShapeDtypeStruct((8, WIDE), F32),
        jax.ShapeDtypeStruct((128, WIDE), BF16),
        jax.ShapeDtypeStruct((8, 128), F32),
        jax.ShapeDtypeStruct((8, 128), F32),
    )
    large = (board_cards, pot_row, regrets, chance, hand_rank, cards, parent)
    return pl.pallas_call(
        pack_kernel,
        out_shape=shapes,
        in_specs=[SMEM()] + [HBM()] * len(large),
        out_specs=[VMEM()] * len(shapes),
        scratch_shapes=[
            pltpu.SMEM((4, 5), jnp.int32),
            pltpu.VMEM((1, OWN), F32),
            pltpu.VMEM((4, HANDS), jnp.int32),
            pltpu.VMEM((2, HANDS), jnp.int32),
            pltpu.VMEM(parent.shape, jnp.int32),
            pltpu.VMEM((OWN, HANDS), F32),
            pltpu.SemaphoreType.DMA((7,)),
        ],
        compiler_params=pltpu.CompilerParams(vmem_limit_bytes=SMALL),
        name="pack",
    )(place, *map(in_hbm, large))


def sides(place_ref, even_ref, cross_ref, rows):
    odd = place_ref[1] == 1
    even, cross = even_ref[rows], cross_ref[rows]
    return jnp.where(odd, even, cross), jnp.where(odd, cross, even)


ROWS = 128


def fill(rank_ref, apart_ref, column_ref, targets):
    ranks = rank_ref[...]
    for t in range(WIDE // 128):
        lanes = slice(t * 128, (t + 1) * 128)
        tile = jnp.concatenate([ranks[:, lanes], jnp.zeros((120, 128), F32)], axis=0)
        column_ref[lanes, :] = tile.T

    @pl.loop(0, WIDE // ROWS)
    def _(i):
        rows = pl.ds(pl.multiple_of(i * ROWS, ROWS), ROWS)
        column = column_ref[rows, :]
        own = [jnp.broadcast_to(column[:, b : b + 1], (ROWS, 128)) for b, _, _ in targets]
        for t in range(WIDE // 128):
            lanes = slice(t * 128, (t + 1) * 128)
            apart = apart_ref[rows, lanes]
            minus = -apart
            for at, (b, matrix_ref, slot) in enumerate(targets):
                gap = (own[at] - rank_ref[b : b + 1, lanes]).astype(BF16)
                matrix_ref[slot, rows, lanes] = jnp.minimum(jnp.maximum(gap, minus), apart)


def build_own_kernel(holding_ref, rank_ref, matrix_ref, apart_ref, column_ref):
    holding = holding_ref[...]
    half = WIDE // 2
    for rows in (slice(0, half), slice(half, WIDE)):
        shared = jnp.dot(holding.T[rows], holding, preferred_element_type=F32)
        apart_ref[rows, :] = (1.0 - jnp.minimum(shared, 1.0)).astype(BF16)
    fill(rank_ref, apart_ref, column_ref, [(b, matrix_ref, b) for b in range(4)])


def outer_boards(mine, other):
    leaf = lax.broadcasted_iota(jnp.int32, mine.shape, 1)
    inside = leaf < WINDOW

    def node_at(row, at):
        return jnp.max(jnp.where(leaf == at, row, -2.0))

    def ends_of(row, node):
        held = inside & (row == node)
        return jnp.min(jnp.where(held, leaf, WINDOW)), jnp.max(jnp.where(held, leaf, -1))

    begin, _ = ends_of(mine, node_at(mine, SIDE))
    begin, _ = ends_of(other, node_at(other, begin))
    _, end = ends_of(mine, node_at(mine, SIDE + OWN - 1))
    _, end = ends_of(other, node_at(other, end))
    return (begin < BOARD_LEAVES) | (end >= WINDOW - BOARD_LEAVES)


def build_side_kernel(
    place_ref, even_ref, cross_ref, nodes_ref, regrets_other_ref, apart_ref,
    near_ref, far_ref, token_ref, rank_ref, column_ref,
):
    outer = outer_boards(nodes_ref[0:1, :], regrets_other_ref[OWN : OWN + 1, 0:128])
    token_ref[0] = outer.astype(jnp.int32)
    left, right = sides(place_ref, even_ref, cross_ref, slice(25, 27))
    rank_ref[...] = jnp.zeros_like(rank_ref)
    rank_ref[0:2, :HANDS] = left
    rank_ref[2:4, :HANDS] = right
    fill(rank_ref, apart_ref, column_ref, [(1, near_ref, 0), (2, near_ref, 1)])

    @pl.when(outer)
    def _():
        fill(rank_ref, apart_ref, column_ref, [(0, far_ref, 0), (3, far_ref, 1)])


BUILD_COST = pl.CostEstimate(
    flops=32 * WIDE * WIDE, bytes_accessed=8 * WIDE * WIDE, transcendentals=0
)


def matrices_shape(boards):
    return jax.ShapeDtypeStruct((boards, WIDE, WIDE), BF16)


def build_own(holding, ranks):
    return pl.pallas_call(
        build_own_kernel,
        out_shape=(matrices_shape(4), jax.ShapeDtypeStruct((WIDE, WIDE), BF16)),
        in_specs=[VMEM()] * 2,
        out_specs=[VMEM()] * 2,
        scratch_shapes=[pltpu.VMEM((WIDE, 128), F32)],
        compiler_params=pltpu.CompilerParams(vmem_limit_bytes=LIMIT),
        cost_estimate=BUILD_COST,
        name="build_own",
    )(holding, ranks)


def build_side(place, even, cross, nodes, regrets_other, apart):
    return pl.pallas_call(
        build_side_kernel,
        out_shape=(
            matrices_shape(2),
            matrices_shape(2),
            jax.ShapeDtypeStruct((1,), jnp.int32),
        ),
        in_specs=[SMEM()] + [VMEM()] * 5,
        out_specs=[VMEM(), VMEM(), SMEM()],
        scratch_shapes=[pltpu.VMEM((8, WIDE), F32), pltpu.VMEM((WIDE, 128), F32)],
        compiler_params=pltpu.CompilerParams(vmem_limit_bytes=LIMIT),
        cost_estimate=BUILD_COST,
        name="build_side",
    )(place, even, cross, nodes, regrets_other, apart)


def node_totals(same, values):
    high = values.astype(BF16)
    rest = values - high.astype(F32)
    middle = rest.astype(BF16)
    low = (rest - middle.astype(F32)).astype(BF16)
    parts = jnp.concatenate([high, middle, low], axis=0)
    return jnp.dot(same, parts, preferred_element_type=F32)


def policy_of(same, regrets):
    positive = jnp.maximum(regrets, 0.0) + DELTA
    return positive / node_totals(same, positive)


def split_terms(reach):
    high = reach.astype(BF16).astype(F32)
    return [high, reach - high]


def joined(out, first):
    middle = first + BOARD_LEAVES
    return out[first:middle] + out[middle : middle + BOARD_LEAVES]


def column_of(row):
    return jnp.broadcast_to(row, (128, 128)).T


def same_node(row):
    equal = jnp.where(jnp.broadcast_to(row, (128, 128)) == column_of(row), 1.0, 0.0)
    equal = equal[:WINDOW, :WINDOW]
    return jnp.concatenate([equal, equal, equal], axis=1).astype(BF16)


def board_rows(free, boards):
    return jnp.concatenate(
        [jnp.broadcast_to(free[b : b + 1], (BOARD_LEAVES, WIDE)) for b in boards], axis=0
    )


def first_kernel(
    place_ref,
    outer_ref,
    regrets_ref,
    chance_ref,
    even_ref,
    cross_ref,
    regrets_other_ref,
    chance_other_ref,
    even_other_ref,
    cross_other_ref,
    nodes_ref,
    own_free_ref,
    pots_ref,
    own_matrix_ref,
    near_ref,
    far_ref,
    window_ref,
    reached_ref,
    instant_ref,
    sums_ref,
    same_ref,
    free_ref,
    pot_ref,
    policy_ref,
    terms_ref,
    values_ref,
):
    left, right = sides(place_ref, even_ref, cross_ref, slice(0, 30))
    left_other, right_other = sides(place_ref, even_other_ref, cross_other_ref, slice(0, 15))
    same_ref[0] = same_node(nodes_ref[0:1, :])
    same_ref[1] = same_node(regrets_other_ref[OWN : OWN + 1, 0:128])
    free_ref[...] = jnp.zeros_like(free_ref)
    free_ref[0:2, :HANDS] = left[27:29]
    free_ref[2:6] = own_free_ref[0:4]
    free_ref[6:8, :HANDS] = right[27:29]
    pot_ref[0:SIDE] = column_of(left[29:30, 0:128])[SIDE:OWN]
    pot_ref[SIDE : SIDE + OWN] = column_of(pots_ref[0:1, :])[:OWN]
    pot_ref[SIDE + OWN :] = column_of(right[29:30, 0:128])[:SIDE]
    window_ref[...] = jnp.zeros_like(window_ref)
    reached_ref[...] = jnp.zeros_like(reached_ref)
    policy_ref[...] = jnp.zeros_like(policy_ref)
    low, high = SIDE, SIDE + OWN
    window_ref[0, low - 15 : low, :HANDS] = left[0:15]
    window_ref[0, low:high, :HANDS] = regrets_ref[:OWN]
    window_ref[0, high : high + 15, :HANDS] = right[0:15]
    policy_ref[0, low - 10 : low, :HANDS] = left[15:25]
    policy_ref[0, low : high - EARLY, :HANDS] = chance_ref[...]
    policy_ref[0, high - EARLY : high, :HANDS] = regrets_ref[OWN + 1 :]
    policy_ref[0, high : high + 10, :HANDS] = right[15:25]
    window_ref[1, low - 10 : low, :HANDS] = left_other[0:10]
    window_ref[1, low:high, :HANDS] = regrets_other_ref[:OWN]
    window_ref[1, high : high + 10, :HANDS] = right_other[0:10]
    reached_ref[low - 5 : low, :HANDS] = left_other[10:15]
    reached_ref[low : high - EARLY, :HANDS] = chance_other_ref[...]
    reached_ref[high - EARLY : high, :HANDS] = regrets_other_ref[OWN + 1 :]
    reached_ref[high : high + 5, :HANDS] = right_other[10:15]
    free = board_rows(free_ref, range(8))
    reached_ref[...] = reached_ref[...] * free
    terms = []
    for p in range(2):
        chance = policy_ref[0] * free if p == 0 else reached_ref[...]
        policy = policy_of(same_ref[p], window_ref[p])
        policy_ref[p] = policy
        terms.append(split_terms(chance * policy))
    for b in range(8):
        rows = slice(b * BOARD_LEAVES, (b + 1) * BOARD_LEAVES)
        block = jnp.concatenate([term[rows] for player in terms for term in player], axis=0)
        terms_ref[b] = block.astype(BF16)

    def board(b, matrix):
        out = jnp.dot(terms_ref[b], matrix, preferred_element_type=F32)
        rows = slice(b * BOARD_LEAVES, (b + 1) * BOARD_LEAVES)
        factor = pot_ref[rows, 0:1] * (-1.0 / HANDS)
        free = free_ref[b : b + 1, :]
        values_ref[1, rows, :] = joined(out, 0) * factor * free
        values_ref[0, rows, :] = joined(out, PIECES * BOARD_LEAVES) * factor * free

    for b in range(4):
        board(b + 2, own_matrix_ref[b])
    board(1, near_ref[0])
    board(6, near_ref[1])

    @pl.when(outer_ref[0] == 1)
    def _():
        board(0, far_ref[0])
        board(7, far_ref[1])

    @pl.when(outer_ref[0] != 1)
    def _():
        for p in range(2):
            for b in (0, 7):
                rows = slice(b * BOARD_LEAVES, (b + 1) * BOARD_LEAVES)
                values_ref[p, rows, :] = jnp.zeros((BOARD_LEAVES, WIDE), F32)

    sums = []
    for p in range(2):
        values = values_ref[p]
        instant = values - node_totals(same_ref[p], policy_ref[p] * values)
        instant_ref[p] = instant
        mine = instant[SIDE : SIDE + OWN]
        sums.append(jnp.sum(mine * mine))
    lane = lax.broadcasted_iota(jnp.int32, sums_ref.shape, 1)
    sums_ref[...] = jnp.where(lane == 0, sums[0], jnp.where(lane == 1, sums[1], 0.0))


def first(place, outer, arrays):
    shapes = (
        jax.ShapeDtypeStruct((2, WINDOW, WIDE), F32),
        jax.ShapeDtypeStruct((WINDOW, WIDE), F32),
        jax.ShapeDtypeStruct((2, WINDOW, WIDE), F32),
        jax.ShapeDtypeStruct((128, 128), F32),
        jax.ShapeDtypeStruct((2, WINDOW, 3 * WINDOW), BF16),
        jax.ShapeDtypeStruct((8, WIDE), F32),
        jax.ShapeDtypeStruct((WINDOW, 128), F32),
    )
    return pl.pallas_call(
        first_kernel,
        out_shape=shapes,
        in_specs=[SMEM(), SMEM()] + [VMEM()] * len(arrays),
        out_specs=[VMEM()] * len(shapes),
        scratch_shapes=[
            pltpu.VMEM((2, WINDOW, WIDE), F32),
            pltpu.VMEM((8, 2 * PIECES * BOARD_LEAVES, WIDE), BF16),
            pltpu.VMEM((2, WINDOW, WIDE), F32),
        ],
        compiler_params=pltpu.CompilerParams(vmem_limit_bytes=LIMIT),
        name="first",
    )(place, outer, *arrays)


def second_kernel(
    gathered_ref,
    window_ref,
    reached_ref,
    instant_ref,
    same_ref,
    free_ref,
    pot_ref,
    own_matrix_ref,
    near_ref,
    out_values_ref,
    moved_ref,
    mine_ref,
    sums_ref,
    policy_ref,
    terms_ref,
    values_ref,
    *,
    count,
):
    values_ref[...] = jnp.zeros_like(values_ref)
    sums = jnp.sum(gathered_ref[...], axis=0, keepdims=True)
    scale = jnp.sqrt(sums / count + EPSILON)
    moved = window_ref[0] + instant_ref[0] / scale[:, 0:1]
    moved_ref[...] = moved[SIDE : SIDE + OWN]
    policy_ref[...] = policy_of(same_ref[0], moved)
    other = window_ref[1] + instant_ref[1] / scale[:, 1:2]
    terms = split_terms(reached_ref[...] * policy_of(same_ref[1], other))
    for b in range(8):
        rows = slice(b * BOARD_LEAVES, (b + 1) * BOARD_LEAVES)
        block = jnp.concatenate([term[rows] for term in terms], axis=0)
        terms_ref[b] = block.astype(BF16)

    def board(b, matrix):
        out = jnp.dot(terms_ref[b], matrix, preferred_element_type=F32)
        rows = slice(b * BOARD_LEAVES, (b + 1) * BOARD_LEAVES)
        factor = pot_ref[rows, 0:1] * (-1.0 / HANDS)
        values_ref[rows, :] = joined(out, 0) * factor * free_ref[b : b + 1, :]

    for b in range(4):
        board(b + 2, own_matrix_ref[b])
    board(1, near_ref[0])
    board(6, near_ref[1])

    values = values_ref[...]
    instant = values - node_totals(same_ref[0], policy_ref[...] * values)
    mine = instant[SIDE : SIDE + OWN]
    mine_ref[...] = mine
    out_values_ref[...] = values[SIDE : SIDE + OWN, :HANDS]
    lane = lax.broadcasted_iota(jnp.int32, sums_ref.shape, 1)
    sums_ref[...] = jnp.where(lane == 0, jnp.sum(mine * mine), 0.0)


def second(gathered, window, reached, instant, same, free, pot, matrices, count):
    shapes = (
        jax.ShapeDtypeStruct((OWN, HANDS), F32),
        jax.ShapeDtypeStruct((OWN, WIDE), F32),
        jax.ShapeDtypeStruct((OWN, WIDE), F32),
        jax.ShapeDtypeStruct((128, 128), F32),
    )
    arrays = (gathered, window, reached, instant, same, free, pot) + matrices
    return pl.pallas_call(
        functools.partial(second_kernel, count=count),
        out_shape=shapes,
        in_specs=[VMEM()] * len(arrays),
        out_specs=[VMEM()] * len(shapes),
        scratch_shapes=[
            pltpu.VMEM((WINDOW, WIDE), F32),
            pltpu.VMEM((8, PIECES * BOARD_LEAVES, WIDE), BF16),
            pltpu.VMEM((WINDOW, WIDE), F32),
        ],
        compiler_params=pltpu.CompilerParams(vmem_limit_bytes=LIMIT),
        name="second",
    )(*arrays)


def tail_kernel(gathered_ref, moved_ref, mine_ref, out_ref, *, count):
    sums = jnp.sum(gathered_ref[...], axis=0, keepdims=True)
    scale = jnp.sqrt(sums / count + EPSILON)[:, 0:1]
    out_ref[...] = (moved_ref[...] + mine_ref[...] / scale)[:, :HANDS]


def tail(gathered, moved, mine, count):
    return pl.pallas_call(
        functools.partial(tail_kernel, count=count),
        out_shape=jax.ShapeDtypeStruct((OWN, HANDS), F32),
        in_specs=[VMEM()] * 3,
        out_specs=VMEM(),
        compiler_params=pltpu.CompilerParams(vmem_limit_bytes=SMALL),
        name="tail",
    )(gathered, moved, mine)


def local(chance_reach, regrets_start, pot, parent, hand_cards, board_cards, hand_rank):
    index = lax.axis_index(LEAF).astype(jnp.int32)
    devices = lax.axis_size(LEAF)
    leaf_count = parent.shape[1]
    place = jnp.stack([index, lax.rem(index, 2)])

    even_pairs = [(i, i ^ 1) for i in range(devices)]
    cross_pairs = [(i, i + 1) for i in range(1, devices - 1, 2)]
    cross_pairs = cross_pairs + [(j, i) for i, j in cross_pairs]

    diagonal = [(2 * i + p, 2 * j + 1 - p) for i, j in cross_pairs for p in range(2)]

    regrets, chance, even, cross, cross_other, ranks, free, holding, pots, nodes = pack(
        place, board_cards, pot[None], regrets_start[0], chance_reach[0], hand_rank,
        hand_cards.T, parent.reshape(-1, 128),
    )
    cross = lax.ppermute(cross, LEAF, cross_pairs)
    even = lax.ppermute(even, LEAF, even_pairs)
    regrets_other = lax.ppermute(regrets, "player", [(0, 1), (1, 0)])
    chance_other = lax.ppermute(chance, "player", [(0, 1), (1, 0)])
    cross_other = lax.ppermute(cross_other, LEAF + ("player",), diagonal)

    own_matrix, apart = build_own(holding, ranks)
    near, far, outer = build_side(place, even, cross, nodes, regrets_other, apart)

    even_other = lax.ppermute(forward(place, regrets_other, chance_other, outer), LEAF, even_pairs)

    def gathered(sums):
        return lax.all_to_all(sums.reshape(devices, 1, 128), LEAF, 0, 0).reshape(128, 128)

    count = float(leaf_count * HANDS)
    window, reached, instant, sums, same, all_free, all_pot = first(
        place,
        outer,
        (regrets, chance, even, cross, regrets_other, chance_other, even_other, cross_other)
        + (nodes, free, pots, own_matrix, near, far),
    )
    values, moved, mine, sums = second(
        gathered(sums), window, reached, instant, same, all_free, all_pot,
        (own_matrix, near), count,
    )
    final = tail(gathered(sums), moved, mine, count)
    return (final[None], values[None])


def solution(mesh):
    split = Mesh(
        mesh.devices.reshape(4, 4, 4, 2, mesh.shape["player"]),
        ("leaf_0", "leaf_1", "leaf_2", "leaf_3", "player"),
    )
    placed = (
        P("player", LEAF, None),
        P("player", LEAF, None),
        P(LEAF),
        P("player", None),
        P(),
        P(LEAF, None),
        P(LEAF, None),
    )
    return jax.shard_map(
        local,
        mesh=split,
        in_specs=placed,
        out_specs=(P("player", LEAF, None), P("player", LEAF, None)),
        check_vma=False,
    )
```

```python
import functools

import jax
import jax.numpy as jnp
from jax import lax
from jax.experimental import pallas as pl
from jax.experimental.pallas import tpu as pltpu
from jax.sharding import Mesh
from jax.sharding import PartitionSpec as P

LEAF = ("leaf_0", "leaf_1", "leaf_2", "leaf_3")
LEAF_SIZES = (4, 4, 4, 2)
DELTA = 0.05
EPSILON = 1e-06

HANDS = 1326
WIDE = 1408
OWN = 32
SIDE = 16
WINDOW = OWN + 2 * SIDE
BOARD_LEAVES = 8
EDGE = 32
EARLY = 2
LIMIT = 10 << 20
SMALL = 6 << 20
PIECES = 2
BF16 = jnp.bfloat16
F32 = jnp.float32
VMEM = functools.partial(pl.BlockSpec, memory_space=pltpu.VMEM)


def leaf_block():
    index = 0
    for axis, size in zip(LEAF, LEAF_SIZES):
        index = index * size + lax.axis_index(axis)
    return index


def is_odd():
    return lax.axis_index(LEAF[-1]) == 1


def edge_rows(regrets_ref, chance_ref, edge_ref, last):
    at = OWN - 10 if last else 0
    edge_ref[0:10] = regrets_ref[at : at + 10]
    if last:
        edge_ref[10 : 15 - EARLY] = chance_ref[OWN - 5 : OWN - EARLY]
        edge_ref[15 - EARLY : 15] = regrets_ref[OWN + 1 :]
    else:
        edge_ref[10:15] = chance_ref[0:5]
    edge_ref[15:16] = jnp.zeros((1, HANDS), F32)


def forward_kernel(regrets_ref, chance_ref, after_ref, edge_ref):
    odd = is_odd()

    @pl.when(odd)
    def _():
        edge_rows(regrets_ref, chance_ref, edge_ref, False)

    @pl.when(jnp.logical_not(odd))
    def _():
        edge_rows(regrets_ref, chance_ref, edge_ref, True)


def forward(regrets, chance, after):
    return pl.pallas_call(
        forward_kernel,
        out_shape=jax.ShapeDtypeStruct((16, HANDS), F32),
        in_specs=[VMEM()] * 3,
        out_specs=VMEM(),
        compiler_params=pltpu.CompilerParams(vmem_limit_bytes=SMALL),
        name="forward",
    )(regrets, chance, after)


def pack_kernel(
    boards_hbm, pot_hbm, regrets_hbm, chance_hbm, rank_hbm, cards_hbm, parent_hbm,
    regrets_ref, chance_ref, even_ref, cross_ref, cross_other_ref,
    wide_rank_ref, free_ref, holding_ref, pots_ref, nodes_ref,
    board_cards_ref, pot_ref, rank_ref, cards_ref, parent_ref, all_chance_ref, sems,
):
    moves = [
        (boards_hbm, board_cards_ref),
        (rank_hbm, rank_ref),
        (cards_hbm, cards_ref),
        (parent_hbm, parent_ref),
        (regrets_hbm, regrets_ref.at[:OWN]),
        (chance_hbm, all_chance_ref),
        (pot_hbm, pot_ref),
    ]
    copies = [
        pltpu.make_async_copy(source, target, sems.at[at])
        for at, (source, target) in enumerate(moves)
    ]
    for copy in copies:
        copy.start()
    pots_ref[...] = jnp.zeros_like(pots_ref)
    wide_rank_ref[...] = jnp.zeros_like(wide_rank_ref)
    free_ref[...] = jnp.zeros_like(free_ref)
    holding_ref[...] = jnp.zeros_like(holding_ref)
    for copy in copies[:4]:
        copy.wait()
    ranks = rank_ref[...].astype(F32)
    lower, upper = cards_ref[0:1, :], cards_ref[1:2, :]
    rows = []
    for b in range(4):
        taken = jnp.zeros((1, HANDS), jnp.bool_)
        for j in range(5):
            card = board_cards_ref[b, j]
            taken = taken | (lower == card) | (upper == card)
        rows.append(jnp.where(taken, 0.0, 1.0))
    wide_rank_ref[0:4, :HANDS] = ranks
    for b in range(4):
        free_ref[b : b + 1, :HANDS] = rows[b]
    deck = lax.broadcasted_iota(jnp.int32, (128, HANDS), 0)
    holding_ref[:, :HANDS] = jnp.where((deck == lower) | (deck == upper), 1.0, 0.0).astype(BF16)

    leaves = parent_ref.shape[0] * 128
    begin = leaf_block() * OWN - SIDE
    line = (begin + 128) // 128 - 1
    held = [
        parent_ref[pl.ds(jnp.clip(line + j, 0, leaves // 128 - 1), 1), :].astype(F32)
        for j in range(2)
    ]
    held = jnp.broadcast_to(jnp.concatenate(held, axis=1), (8, 256))
    held = pltpu.roll(held, lax.rem((line + 2) * 128 - begin, 256), 1)[0:1, 0:128]
    leaf = begin + lax.broadcasted_iota(jnp.int32, (1, 128), 1)
    held = jnp.where((leaf >= 0) & (leaf < leaves), held, -1.0)
    nodes_ref[...] = jnp.broadcast_to(held, nodes_ref.shape)
    for copy in copies[4:]:
        copy.wait()
    pots_ref[0:1, 0:OWN] = pot_ref[...]
    chance_ref[...] = all_chance_ref[0 : OWN - EARLY]
    regrets_ref[OWN + 1 :] = all_chance_ref[OWN - EARLY :]

    odd = is_odd()

    def ends(ref, last):
        at = OWN - 15 if last else 0
        ref[0:15] = regrets_ref[at : at + 15]
        at = OWN - 10 if last else 0
        ref[15:25] = all_chance_ref[at : at + 10]
        at = 2 if last else 0
        ref[25:27] = ranks[at : at + 2]
        ref[27:28] = rows[at]
        ref[28:29] = rows[at + 1]
        ref[29:30] = jnp.zeros((1, HANDS), F32)
        ref[29:30, 0:128] = pots_ref[0:1, :]
        ref[30:] = jnp.zeros((EDGE - 30, HANDS), F32)

    @pl.when(odd)
    def _():
        ends(even_ref, False)
        ends(cross_ref, True)
        edge_rows(regrets_ref, chance_ref, cross_other_ref, True)

    @pl.when(jnp.logical_not(odd))
    def _():
        ends(even_ref, True)
        ends(cross_ref, False)
        edge_rows(regrets_ref, chance_ref, cross_other_ref, False)

    regrets_ref[OWN : OWN + 1] = jnp.zeros((1, HANDS), F32)
    regrets_ref[OWN : OWN + 1, 0:128] = held


HBM = functools.partial(pl.BlockSpec, memory_space=pltpu.HBM)


def in_hbm(array):
    return pltpu.with_memory_space_constraint(array, pltpu.HBM)


def pack(board_cards, pot_row, regrets, chance, hand_rank, cards, parent):
    shapes = (
        jax.ShapeDtypeStruct((OWN + 1 + EARLY, HANDS), F32),
        jax.ShapeDtypeStruct((OWN - EARLY, HANDS), F32),
        jax.ShapeDtypeStruct((EDGE, HANDS), F32),
        jax.ShapeDtypeStruct((EDGE, HANDS), F32),
        jax.ShapeDtypeStruct((16, HANDS), F32),
        jax.ShapeDtypeStruct((8, WIDE), F32),
        jax.ShapeDtypeStruct((8, WIDE), F32),
        jax.ShapeDtypeStruct((128, WIDE), BF16),
        jax.ShapeDtypeStruct((8, 128), F32),
        jax.ShapeDtypeStruct((8, 128), F32),
    )
    large = (board_cards, pot_row, regrets, chance, hand_rank, cards, parent)
    return pl.pallas_call(
        pack_kernel,
        out_shape=shapes,
        in_specs=[HBM()] * len(large),
        out_specs=[VMEM()] * len(shapes),
        scratch_shapes=[
            pltpu.SMEM((4, 5), jnp.int32),
            pltpu.VMEM((1, OWN), F32),
            pltpu.VMEM((4, HANDS), jnp.int32),
            pltpu.VMEM((2, HANDS), jnp.int32),
            pltpu.VMEM(parent.shape, jnp.int32),
            pltpu.VMEM((OWN, HANDS), F32),
            pltpu.SemaphoreType.DMA((7,)),
        ],
        compiler_params=pltpu.CompilerParams(vmem_limit_bytes=SMALL),
        name="pack",
    )(*map(in_hbm, large))


def sides(even_ref, cross_ref, rows):
    odd = is_odd()
    even, cross = even_ref[rows], cross_ref[rows]
    return jnp.where(odd, even, cross), jnp.where(odd, cross, even)


ROWS = 128


def fill(rank_ref, apart_ref, column_ref, targets):
    ranks = rank_ref[...]
    for t in range(WIDE // 128):
        lanes = slice(t * 128, (t + 1) * 128)
        tile = jnp.concatenate([ranks[:, lanes], jnp.zeros((120, 128), F32)], axis=0)
        column_ref[lanes, :] = tile.T

    @pl.loop(0, WIDE // ROWS)
    def _(i):
        rows = pl.ds(pl.multiple_of(i * ROWS, ROWS), ROWS)
        column = column_ref[rows, :]
        own = [jnp.broadcast_to(column[:, b : b + 1], (ROWS, 128)) for b, _, _ in targets]
        for t in range(WIDE // 128):
            lanes = slice(t * 128, (t + 1) * 128)
            apart = apart_ref[rows, lanes]
            minus = -apart
            for at, (b, matrix_ref, slot) in enumerate(targets):
                gap = (own[at] - rank_ref[b : b + 1, lanes]).astype(BF16)
                matrix_ref[slot, rows, lanes] = jnp.minimum(jnp.maximum(gap, minus), apart)


def build_own_kernel(holding_ref, rank_ref, matrix_ref, apart_ref, column_ref):
    holding = holding_ref[...]
    half = WIDE // 2
    for rows in (slice(0, half), slice(half, WIDE)):
        shared = jnp.dot(holding.T[rows], holding, preferred_element_type=F32)
        apart_ref[rows, :] = (1.0 - jnp.minimum(shared, 1.0)).astype(BF16)
    fill(rank_ref, apart_ref, column_ref, [(b, matrix_ref, b) for b in range(4)])


def outer_boards(mine, other):
    leaf = lax.broadcasted_iota(jnp.int32, mine.shape, 1)
    inside = leaf < WINDOW

    def node_at(row, at):
        return jnp.max(jnp.where(leaf == at, row, -2.0))

    def ends_of(row, node):
        held = inside & (row == node)
        return jnp.min(jnp.where(held, leaf, WINDOW)), jnp.max(jnp.where(held, leaf, -1))

    begin, _ = ends_of(mine, node_at(mine, SIDE))
    begin, _ = ends_of(other, node_at(other, begin))
    _, end = ends_of(mine, node_at(mine, SIDE + OWN - 1))
    _, end = ends_of(other, node_at(other, end))
    return (begin < BOARD_LEAVES) | (end >= WINDOW - BOARD_LEAVES)


def build_side_kernel(
    even_ref, cross_ref, nodes_ref, regrets_other_ref, apart_ref,
    near_ref, far_ref, outer_ref, rank_ref, column_ref,
):
    outer = outer_boards(nodes_ref[0:1, :], regrets_other_ref[OWN : OWN + 1, 0:128])
    outer_ref[...] = jnp.where(outer, jnp.ones_like(outer_ref), jnp.zeros_like(outer_ref))
    left, right = sides(even_ref, cross_ref, slice(25, 27))
    rank_ref[...] = jnp.zeros_like(rank_ref)
    rank_ref[0:2, :HANDS] = left
    rank_ref[2:4, :HANDS] = right
    fill(rank_ref, apart_ref, column_ref, [(1, near_ref, 0), (2, near_ref, 1)])

    @pl.when(outer)
    def _():
        fill(rank_ref, apart_ref, column_ref, [(0, far_ref, 0), (3, far_ref, 1)])


BUILD_COST = pl.CostEstimate(
    flops=32 * WIDE * WIDE, bytes_accessed=8 * WIDE * WIDE, transcendentals=0
)


def matrices_shape(boards):
    return jax.ShapeDtypeStruct((boards, WIDE, WIDE), BF16)


def build_own(holding, ranks):
    return pl.pallas_call(
        build_own_kernel,
        out_shape=(matrices_shape(4), jax.ShapeDtypeStruct((WIDE, WIDE), BF16)),
        in_specs=[VMEM()] * 2,
        out_specs=[VMEM()] * 2,
        scratch_shapes=[pltpu.VMEM((WIDE, 128), F32)],
        compiler_params=pltpu.CompilerParams(vmem_limit_bytes=LIMIT),
        cost_estimate=BUILD_COST,
        name="build_own",
    )(holding, ranks)


def build_side(even, cross, nodes, regrets_other, apart):
    return pl.pallas_call(
        build_side_kernel,
        out_shape=(
            matrices_shape(2),
            matrices_shape(2),
            jax.ShapeDtypeStruct((8, 128), F32),
        ),
        in_specs=[VMEM()] * 5,
        out_specs=[VMEM()] * 3,
        scratch_shapes=[pltpu.VMEM((8, WIDE), F32), pltpu.VMEM((WIDE, 128), F32)],
        compiler_params=pltpu.CompilerParams(vmem_limit_bytes=LIMIT),
        cost_estimate=BUILD_COST,
        name="build_side",
    )(even, cross, nodes, regrets_other, apart)


def node_totals(same, values):
    high = values.astype(BF16)
    rest = values - high.astype(F32)
    middle = rest.astype(BF16)
    low = (rest - middle.astype(F32)).astype(BF16)
    parts = jnp.concatenate([high, middle, low], axis=0)
    return jnp.dot(same, parts, preferred_element_type=F32)


def policy_of(same, regrets):
    positive = jnp.maximum(regrets, 0.0) + DELTA
    return positive / node_totals(same, positive)


def split_terms(reach):
    high = reach.astype(BF16).astype(F32)
    return [high, reach - high]


def joined(out, first):
    middle = first + BOARD_LEAVES
    return out[first:middle] + out[middle : middle + BOARD_LEAVES]


def column_of(row):
    return jnp.broadcast_to(row, (128, 128)).T


def same_node(row):
    equal = jnp.where(jnp.broadcast_to(row, (128, 128)) == column_of(row), 1.0, 0.0)
    equal = equal[:WINDOW, :WINDOW]
    return jnp.concatenate([equal, equal, equal], axis=1).astype(BF16)


def board_rows(free, boards):
    return jnp.concatenate(
        [jnp.broadcast_to(free[b : b + 1], (BOARD_LEAVES, WIDE)) for b in boards], axis=0
    )


def first_kernel(
    outer_ref,
    regrets_ref,
    chance_ref,
    even_ref,
    cross_ref,
    regrets_other_ref,
    chance_other_ref,
    even_other_ref,
    cross_other_ref,
    nodes_ref,
    own_free_ref,
    pots_ref,
    own_matrix_ref,
    near_ref,
    far_ref,
    window_ref,
    reached_ref,
    instant_ref,
    sums_ref,
    same_ref,
    free_ref,
    pot_ref,
    policy_ref,
    terms_ref,
    values_ref,
):
    left, right = sides(even_ref, cross_ref, slice(0, 30))
    left_other, right_other = sides(even_other_ref, cross_other_ref, slice(0, 15))
    same_ref[0] = same_node(nodes_ref[0:1, :])
    same_ref[1] = same_node(regrets_other_ref[OWN : OWN + 1, 0:128])
    free_ref[...] = jnp.zeros_like(free_ref)
    free_ref[0:2, :HANDS] = left[27:29]
    free_ref[2:6] = own_free_ref[0:4]
    free_ref[6:8, :HANDS] = right[27:29]
    pot_ref[0:SIDE] = column_of(left[29:30, 0:128])[SIDE:OWN]
    pot_ref[SIDE : SIDE + OWN] = column_of(pots_ref[0:1, :])[:OWN]
    pot_ref[SIDE + OWN :] = column_of(right[29:30, 0:128])[:SIDE]
    window_ref[...] = jnp.zeros_like(window_ref)
    reached_ref[...] = jnp.zeros_like(reached_ref)
    policy_ref[...] = jnp.zeros_like(policy_ref)
    low, high = SIDE, SIDE + OWN
    window_ref[0, low - 15 : low, :HANDS] = left[0:15]
    window_ref[0, low:high, :HANDS] = regrets_ref[:OWN]
    window_ref[0, high : high + 15, :HANDS] = right[0:15]
    policy_ref[0, low - 10 : low, :HANDS] = left[15:25]
    policy_ref[0, low : high - EARLY, :HANDS] = chance_ref[...]
    policy_ref[0, high - EARLY : high, :HANDS] = regrets_ref[OWN + 1 :]
    policy_ref[0, high : high + 10, :HANDS] = right[15:25]
    window_ref[1, low - 10 : low, :HANDS] = left_other[0:10]
    window_ref[1, low:high, :HANDS] = regrets_other_ref[:OWN]
    window_ref[1, high : high + 10, :HANDS] = right_other[0:10]
    reached_ref[low - 5 : low, :HANDS] = left_other[10:15]
    reached_ref[low : high - EARLY, :HANDS] = chance_other_ref[...]
    reached_ref[high - EARLY : high, :HANDS] = regrets_other_ref[OWN + 1 :]
    reached_ref[high : high + 5, :HANDS] = right_other[10:15]
    free = board_rows(free_ref, range(8))
    reached_ref[...] = reached_ref[...] * free
    terms = []
    for p in range(2):
        chance = policy_ref[0] * free if p == 0 else reached_ref[...]
        policy = policy_of(same_ref[p], window_ref[p])
        policy_ref[p] = policy
        terms.append(split_terms(chance * policy))
    for b in range(8):
        rows = slice(b * BOARD_LEAVES, (b + 1) * BOARD_LEAVES)
        block = jnp.concatenate([term[rows] for player in terms for term in player], axis=0)
        terms_ref[b] = block.astype(BF16)

    def board(b, matrix):
        out = jnp.dot(terms_ref[b], matrix, preferred_element_type=F32)
        rows = slice(b * BOARD_LEAVES, (b + 1) * BOARD_LEAVES)
        factor = pot_ref[rows, 0:1] * (-1.0 / HANDS)
        free = free_ref[b : b + 1, :]
        values_ref[1, rows, :] = joined(out, 0) * factor * free
        values_ref[0, rows, :] = joined(out, PIECES * BOARD_LEAVES) * factor * free

    for b in range(4):
        board(b + 2, own_matrix_ref[b])
    board(1, near_ref[0])
    board(6, near_ref[1])

    outer = jnp.max(outer_ref[0:1, :]) > 0.5

    @pl.when(outer)
    def _():
        board(0, far_ref[0])
        board(7, far_ref[1])

    @pl.when(jnp.logical_not(outer))
    def _():
        for p in range(2):
            for b in (0, 7):
                rows = slice(b * BOARD_LEAVES, (b + 1) * BOARD_LEAVES)
                values_ref[p, rows, :] = jnp.zeros((BOARD_LEAVES, WIDE), F32)

    sums = []
    for p in range(2):
        values = values_ref[p]
        instant = values - node_totals(same_ref[p], policy_ref[p] * values)
        instant_ref[p] = instant
        mine = instant[SIDE : SIDE + OWN]
        sums.append(jnp.sum(mine * mine))
    lane = lax.broadcasted_iota(jnp.int32, sums_ref.shape, 1)
    sums_ref[...] = jnp.where(lane == 0, sums[0], jnp.where(lane == 1, sums[1], 0.0))


def first(arrays):
    shapes = (
        jax.ShapeDtypeStruct((2, WINDOW, WIDE), F32),
        jax.ShapeDtypeStruct((WINDOW, WIDE), F32),
        jax.ShapeDtypeStruct((2, WINDOW, WIDE), F32),
        jax.ShapeDtypeStruct((128, 128), F32),
        jax.ShapeDtypeStruct((2, WINDOW, 3 * WINDOW), BF16),
        jax.ShapeDtypeStruct((8, WIDE), F32),
        jax.ShapeDtypeStruct((WINDOW, 128), F32),
    )
    return pl.pallas_call(
        first_kernel,
        out_shape=shapes,
        in_specs=[VMEM()] * len(arrays),
        out_specs=[VMEM()] * len(shapes),
        scratch_shapes=[
            pltpu.VMEM((2, WINDOW, WIDE), F32),
            pltpu.VMEM((8, 2 * PIECES * BOARD_LEAVES, WIDE), BF16),
            pltpu.VMEM((2, WINDOW, WIDE), F32),
        ],
        compiler_params=pltpu.CompilerParams(vmem_limit_bytes=LIMIT),
        name="first",
    )(*arrays)


def second_kernel(
    gathered_ref,
    window_ref,
    reached_ref,
    instant_ref,
    same_ref,
    free_ref,
    pot_ref,
    own_matrix_ref,
    near_ref,
    out_values_ref,
    moved_ref,
    mine_ref,
    sums_ref,
    policy_ref,
    terms_ref,
    values_ref,
    *,
    count,
):
    values_ref[...] = jnp.zeros_like(values_ref)
    sums = jnp.sum(gathered_ref[...], axis=0, keepdims=True)
    scale = jnp.sqrt(sums / count + EPSILON)
    moved = window_ref[0] + instant_ref[0] / scale[:, 0:1]
    moved_ref[...] = moved[SIDE : SIDE + OWN]
    policy_ref[...] = policy_of(same_ref[0], moved)
    other = window_ref[1] + instant_ref[1] / scale[:, 1:2]
    terms = split_terms(reached_ref[...] * policy_of(same_ref[1], other))
    for b in range(8):
        rows = slice(b * BOARD_LEAVES, (b + 1) * BOARD_LEAVES)
        block = jnp.concatenate([term[rows] for term in terms], axis=0)
        terms_ref[b] = block.astype(BF16)

    def board(b, matrix):
        out = jnp.dot(terms_ref[b], matrix, preferred_element_type=F32)
        rows = slice(b * BOARD_LEAVES, (b + 1) * BOARD_LEAVES)
        factor = pot_ref[rows, 0:1] * (-1.0 / HANDS)
        values_ref[rows, :] = joined(out, 0) * factor * free_ref[b : b + 1, :]

    for b in range(4):
        board(b + 2, own_matrix_ref[b])
    board(1, near_ref[0])
    board(6, near_ref[1])

    values = values_ref[...]
    instant = values - node_totals(same_ref[0], policy_ref[...] * values)
    mine = instant[SIDE : SIDE + OWN]
    mine_ref[...] = mine
    out_values_ref[...] = values[SIDE : SIDE + OWN, :HANDS]
    lane = lax.broadcasted_iota(jnp.int32, sums_ref.shape, 1)
    sums_ref[...] = jnp.where(lane == 0, jnp.sum(mine * mine), 0.0)


def second(gathered, window, reached, instant, same, free, pot, matrices, count):
    shapes = (
        jax.ShapeDtypeStruct((OWN, HANDS), F32),
        jax.ShapeDtypeStruct((OWN, WIDE), F32),
        jax.ShapeDtypeStruct((OWN, WIDE), F32),
        jax.ShapeDtypeStruct((128, 128), F32),
    )
    arrays = (gathered, window, reached, instant, same, free, pot) + matrices
    return pl.pallas_call(
        functools.partial(second_kernel, count=count),
        out_shape=shapes,
        in_specs=[VMEM()] * len(arrays),
        out_specs=[VMEM()] * len(shapes),
        scratch_shapes=[
            pltpu.VMEM((WINDOW, WIDE), F32),
            pltpu.VMEM((8, PIECES * BOARD_LEAVES, WIDE), BF16),
            pltpu.VMEM((WINDOW, WIDE), F32),
        ],
        compiler_params=pltpu.CompilerParams(vmem_limit_bytes=LIMIT),
        name="second",
    )(*arrays)


def tail_kernel(gathered_ref, moved_ref, mine_ref, out_ref, *, count):
    sums = jnp.sum(gathered_ref[...], axis=0, keepdims=True)
    scale = jnp.sqrt(sums / count + EPSILON)[:, 0:1]
    out_ref[...] = (moved_ref[...] + mine_ref[...] / scale)[:, :HANDS]


def tail(gathered, moved, mine, count):
    return pl.pallas_call(
        functools.partial(tail_kernel, count=count),
        out_shape=jax.ShapeDtypeStruct((OWN, HANDS), F32),
        in_specs=[VMEM()] * 3,
        out_specs=VMEM(),
        compiler_params=pltpu.CompilerParams(vmem_limit_bytes=SMALL),
        name="tail",
    )(gathered, moved, mine)


def local(chance_reach, regrets_start, pot, parent, hand_cards, board_cards, hand_rank):
    devices = lax.axis_size(LEAF)
    leaf_count = parent.shape[1]

    even_pairs = [(i, i ^ 1) for i in range(devices)]
    cross_pairs = [(i, i + 1) for i in range(1, devices - 1, 2)]
    cross_pairs = cross_pairs + [(j, i) for i, j in cross_pairs]

    diagonal = [(2 * i + p, 2 * j + 1 - p) for i, j in cross_pairs for p in range(2)]

    regrets, chance, even, cross, cross_other, ranks, free, holding, pots, nodes = pack(
        board_cards, pot[None], regrets_start[0], chance_reach[0], hand_rank,
        hand_cards.T, parent.reshape(-1, 128),
    )
    cross = lax.ppermute(cross, LEAF, cross_pairs)
    even = lax.ppermute(even, LEAF, even_pairs)
    regrets_other = lax.ppermute(regrets, "player", [(0, 1), (1, 0)])
    chance_other = lax.ppermute(chance, "player", [(0, 1), (1, 0)])
    cross_other = lax.ppermute(cross_other, LEAF + ("player",), diagonal)

    own_matrix, apart = build_own(holding, ranks)
    near, far, outer = build_side(even, cross, nodes, regrets_other, apart)

    even_other = lax.ppermute(forward(regrets_other, chance_other, outer), LEAF, even_pairs)

    def gathered(sums):
        return lax.all_to_all(sums.reshape(devices, 1, 128), LEAF, 0, 0).reshape(128, 128)

    count = float(leaf_count * HANDS)
    window, reached, instant, sums, same, all_free, all_pot = first(
        (outer, regrets, chance, even, cross, regrets_other, chance_other, even_other)
        + (cross_other,)
        + (nodes, free, pots, own_matrix, near, far),
    )
    values, moved, mine, sums = second(
        gathered(sums), window, reached, instant, same, all_free, all_pot,
        (own_matrix, near), count,
    )
    final = tail(gathered(sums), moved, mine, count)
    return (final[None], values[None])


def solution(mesh):
    split = Mesh(
        mesh.devices.reshape(*LEAF_SIZES, mesh.shape["player"]),
        LEAF + ("player",),
    )
    placed = (
        P("player", LEAF, None),
        P("player", LEAF, None),
        P(LEAF),
        P("player", None),
        P(),
        P(LEAF, None),
        P(LEAF, None),
    )
    return jax.shard_map(
        local,
        mesh=split,
        in_specs=placed,
        out_specs=(P("player", LEAF, None), P("player", LEAF, None)),
        check_vma=False,
    )
```

```python
import functools

import jax
import jax.numpy as jnp
from jax import lax
from jax.experimental import pallas as pl
from jax.experimental.pallas import tpu as pltpu
from jax.sharding import Mesh
from jax.sharding import PartitionSpec as P

LEAF = ("leaf_0", "leaf_1", "leaf_2", "leaf_3")
LEAF_SIZES = (4, 4, 4, 2)
DELTA = 0.05
EPSILON = 1e-06

HANDS = 1326
WIDE = 1408
OWN = 32
SIDE = 16
WINDOW = OWN + 2 * SIDE
BOARD_LEAVES = 8
EDGE = 32
EARLY = 2
LIMIT = 10 << 20
SMALL = 6 << 20
PIECES = 2
BF16 = jnp.bfloat16
F32 = jnp.float32
VMEM = functools.partial(pl.BlockSpec, memory_space=pltpu.VMEM)


def leaf_block():
    index = 0
    for axis, size in zip(LEAF, LEAF_SIZES):
        index = index * size + lax.axis_index(axis)
    return index


def is_odd():
    return lax.axis_index(LEAF[-1]) == 1


def edge_rows(regrets_ref, chance_ref, edge_ref, last):
    at = OWN - 10 if last else 0
    edge_ref[0:10] = regrets_ref[at : at + 10]
    if last:
        edge_ref[10 : 15 - EARLY] = chance_ref[OWN - 5 : OWN - EARLY]
        edge_ref[15 - EARLY : 15] = regrets_ref[OWN + 1 :]
    else:
        edge_ref[10:15] = chance_ref[0:5]
    edge_ref[15:16] = jnp.zeros((1, HANDS), F32)


def pack_kernel(
    boards_hbm, pot_hbm, regrets_hbm, chance_hbm, rank_hbm, cards_hbm, parent_hbm,
    regrets_ref, chance_ref, even_ref, cross_ref, even_other_ref, cross_other_ref,
    wide_rank_ref, free_ref, holding_ref, pots_ref, nodes_ref,
    board_cards_ref, pot_ref, rank_ref, cards_ref, parent_ref, all_chance_ref, sems,
):
    moves = [
        (boards_hbm, board_cards_ref),
        (rank_hbm, rank_ref),
        (cards_hbm, cards_ref),
        (parent_hbm, parent_ref),
        (regrets_hbm, regrets_ref.at[:OWN]),
        (chance_hbm, all_chance_ref),
        (pot_hbm, pot_ref),
    ]
    copies = [
        pltpu.make_async_copy(source, target, sems.at[at])
        for at, (source, target) in enumerate(moves)
    ]
    for copy in copies:
        copy.start()
    pots_ref[...] = jnp.zeros_like(pots_ref)
    wide_rank_ref[...] = jnp.zeros_like(wide_rank_ref)
    free_ref[...] = jnp.zeros_like(free_ref)
    holding_ref[...] = jnp.zeros_like(holding_ref)
    for copy in copies[:4]:
        copy.wait()
    ranks = rank_ref[...].astype(F32)
    lower, upper = cards_ref[0:1, :], cards_ref[1:2, :]
    rows = []
    for b in range(4):
        taken = jnp.zeros((1, HANDS), jnp.bool_)
        for j in range(5):
            card = board_cards_ref[b, j]
            taken = taken | (lower == card) | (upper == card)
        rows.append(jnp.where(taken, 0.0, 1.0))
    wide_rank_ref[0:4, :HANDS] = ranks
    for b in range(4):
        free_ref[b : b + 1, :HANDS] = rows[b]
    deck = lax.broadcasted_iota(jnp.int32, (128, HANDS), 0)
    holding_ref[:, :HANDS] = jnp.where((deck == lower) | (deck == upper), 1.0, 0.0).astype(BF16)

    leaves = parent_ref.shape[0] * 128
    begin = leaf_block() * OWN - SIDE
    line = (begin + 128) // 128 - 1
    held = [
        parent_ref[pl.ds(jnp.clip(line + j, 0, leaves // 128 - 1), 1), :].astype(F32)
        for j in range(2)
    ]
    held = jnp.broadcast_to(jnp.concatenate(held, axis=1), (8, 256))
    held = pltpu.roll(held, lax.rem((line + 2) * 128 - begin, 256), 1)[0:1, 0:128]
    leaf = begin + lax.broadcasted_iota(jnp.int32, (1, 128), 1)
    held = jnp.where((leaf >= 0) & (leaf < leaves), held, -1.0)
    nodes_ref[...] = jnp.broadcast_to(held, nodes_ref.shape)
    for copy in copies[4:]:
        copy.wait()
    pots_ref[0:1, 0:OWN] = pot_ref[...]
    chance_ref[...] = all_chance_ref[0 : OWN - EARLY]
    regrets_ref[OWN + 1 :] = all_chance_ref[OWN - EARLY :]

    odd = is_odd()

    def ends(ref, last):
        at = OWN - 15 if last else 0
        ref[0:15] = regrets_ref[at : at + 15]
        at = OWN - 10 if last else 0
        ref[15:25] = all_chance_ref[at : at + 10]
        at = 2 if last else 0
        ref[25:27] = ranks[at : at + 2]
        ref[27:28] = rows[at]
        ref[28:29] = rows[at + 1]
        ref[29:30] = jnp.zeros((1, HANDS), F32)
        ref[29:30, 0:128] = pots_ref[0:1, :]
        ref[30:] = jnp.zeros((EDGE - 30, HANDS), F32)

    @pl.when(odd)
    def _():
        ends(even_ref, False)
        ends(cross_ref, True)
        edge_rows(regrets_ref, chance_ref, even_other_ref, False)
        edge_rows(regrets_ref, chance_ref, cross_other_ref, True)

    @pl.when(jnp.logical_not(odd))
    def _():
        ends(even_ref, True)
        ends(cross_ref, False)
        edge_rows(regrets_ref, chance_ref, even_other_ref, True)
        edge_rows(regrets_ref, chance_ref, cross_other_ref, False)

    regrets_ref[OWN : OWN + 1] = jnp.zeros((1, HANDS), F32)
    regrets_ref[OWN : OWN + 1, 0:128] = held


HBM = functools.partial(pl.BlockSpec, memory_space=pltpu.HBM)


def in_hbm(array):
    return pltpu.with_memory_space_constraint(array, pltpu.HBM)


def pack(board_cards, pot_row, regrets, chance, hand_rank, cards, parent):
    shapes = (
        jax.ShapeDtypeStruct((OWN + 1 + EARLY, HANDS), F32),
        jax.ShapeDtypeStruct((OWN - EARLY, HANDS), F32),
        jax.ShapeDtypeStruct((EDGE, HANDS), F32),
        jax.ShapeDtypeStruct((EDGE, HANDS), F32),
        jax.ShapeDtypeStruct((16, HANDS), F32),
        jax.ShapeDtypeStruct((16, HANDS), F32),
        jax.ShapeDtypeStruct((8, WIDE), F32),
        jax.ShapeDtypeStruct((8, WIDE), F32),
        jax.ShapeDtypeStruct((128, WIDE), BF16),
        jax.ShapeDtypeStruct((8, 128), F32),
        jax.ShapeDtypeStruct((8, 128), F32),
    )
    large = (board_cards, pot_row, regrets, chance, hand_rank, cards, parent)
    return pl.pallas_call(
        pack_kernel,
        out_shape=shapes,
        in_specs=[HBM()] * len(large),
        out_specs=[VMEM()] * len(shapes),
        scratch_shapes=[
            pltpu.SMEM((4, 5), jnp.int32),
            pltpu.VMEM((1, OWN), F32),
            pltpu.VMEM((4, HANDS), jnp.int32),
            pltpu.VMEM((2, HANDS), jnp.int32),
            pltpu.VMEM(parent.shape, jnp.int32),
            pltpu.VMEM((OWN, HANDS), F32),
            pltpu.SemaphoreType.DMA((7,)),
        ],
        compiler_params=pltpu.CompilerParams(vmem_limit_bytes=SMALL),
        name="pack",
    )(*map(in_hbm, large))


def sides(even_ref, cross_ref, rows):
    odd = is_odd()
    even, cross = even_ref[rows], cross_ref[rows]
    return jnp.where(odd, even, cross), jnp.where(odd, cross, even)


def fill(rank_ref, apart_ref, column_ref, targets, step):
    ranks = rank_ref[...]
    for t in range(WIDE // 128):
        lanes = slice(t * 128, (t + 1) * 128)
        tile = jnp.concatenate([ranks[:, lanes], jnp.zeros((120, 128), F32)], axis=0)
        column_ref[lanes, :] = tile.T

    @pl.loop(0, WIDE // step)
    def _(i):
        rows = pl.ds(pl.multiple_of(i * step, step), step)
        column = column_ref[rows, :]
        own = [jnp.broadcast_to(column[:, b : b + 1], (step, 128)) for b, _, _ in targets]
        for t in range(WIDE // 128):
            lanes = slice(t * 128, (t + 1) * 128)
            apart = apart_ref[rows, lanes]
            minus = -apart
            for at, (b, matrix_ref, slot) in enumerate(targets):
                gap = (own[at] - rank_ref[b : b + 1, lanes]).astype(BF16)
                matrix_ref[slot, rows, lanes] = jnp.minimum(jnp.maximum(gap, minus), apart)


def build_own_kernel(holding_ref, rank_ref, matrix_ref, apart_ref, column_ref):
    holding = holding_ref[...]
    half = WIDE // 2
    for rows in (slice(0, half), slice(half, WIDE)):
        shared = jnp.dot(holding.T[rows], holding, preferred_element_type=F32)
        apart_ref[rows, :] = (1.0 - jnp.minimum(shared, 1.0)).astype(BF16)
    fill(rank_ref, apart_ref, column_ref, [(b, matrix_ref, b) for b in range(4)], 352)


def outer_boards(mine, other):
    leaf = lax.broadcasted_iota(jnp.int32, mine.shape, 1)
    inside = leaf < WINDOW

    def node_at(row, at):
        return jnp.max(jnp.where(leaf == at, row, -2.0))

    def ends_of(row, node):
        held = inside & (row == node)
        return jnp.min(jnp.where(held, leaf, WINDOW)), jnp.max(jnp.where(held, leaf, -1))

    begin, _ = ends_of(mine, node_at(mine, SIDE))
    begin, _ = ends_of(other, node_at(other, begin))
    _, end = ends_of(mine, node_at(mine, SIDE + OWN - 1))
    _, end = ends_of(other, node_at(other, end))
    return (begin < BOARD_LEAVES) | (end >= WINDOW - BOARD_LEAVES)


def build_side_kernel(
    even_ref, cross_ref, nodes_ref, regrets_other_ref, apart_ref,
    near_ref, far_ref, outer_ref, rank_ref, column_ref,
):
    outer = outer_boards(nodes_ref[0:1, :], regrets_other_ref[OWN : OWN + 1, 0:128])
    outer_ref[...] = jnp.where(outer, jnp.ones_like(outer_ref), jnp.zeros_like(outer_ref))
    left, right = sides(even_ref, cross_ref, slice(25, 27))
    rank_ref[...] = jnp.zeros_like(rank_ref)
    rank_ref[0:2, :HANDS] = left
    rank_ref[2:4, :HANDS] = right
    fill(rank_ref, apart_ref, column_ref, [(1, near_ref, 0), (2, near_ref, 1)], 704)

    @pl.when(outer)
    def _():
        fill(rank_ref, apart_ref, column_ref, [(0, far_ref, 0), (3, far_ref, 1)], 704)


BUILD_COST = pl.CostEstimate(
    flops=32 * WIDE * WIDE, bytes_accessed=8 * WIDE * WIDE, transcendentals=0
)


def matrices_shape(boards):
    return jax.ShapeDtypeStruct((boards, WIDE, WIDE), BF16)


def build_own(holding, ranks):
    return pl.pallas_call(
        build_own_kernel,
        out_shape=(matrices_shape(4), jax.ShapeDtypeStruct((WIDE, WIDE), BF16)),
        in_specs=[VMEM()] * 2,
        out_specs=[VMEM()] * 2,
        scratch_shapes=[pltpu.VMEM((WIDE, 128), F32)],
        compiler_params=pltpu.CompilerParams(vmem_limit_bytes=LIMIT),
        cost_estimate=BUILD_COST,
        name="build_own",
    )(holding, ranks)


def build_side(even, cross, nodes, regrets_other, apart):
    return pl.pallas_call(
        build_side_kernel,
        out_shape=(
            matrices_shape(2),
            matrices_shape(2),
            jax.ShapeDtypeStruct((8, 128), F32),
        ),
        in_specs=[VMEM()] * 5,
        out_specs=[VMEM()] * 3,
        scratch_shapes=[pltpu.VMEM((8, WIDE), F32), pltpu.VMEM((WIDE, 128), F32)],
        compiler_params=pltpu.CompilerParams(vmem_limit_bytes=LIMIT),
        cost_estimate=BUILD_COST,
        name="build_side",
    )(even, cross, nodes, regrets_other, apart)


def node_totals(same, values):
    high = values.astype(BF16)
    rest = values - high.astype(F32)
    middle = rest.astype(BF16)
    low = (rest - middle.astype(F32)).astype(BF16)
    parts = jnp.concatenate([high, middle, low], axis=0)
    return jnp.dot(same, parts, preferred_element_type=F32)


def policy_of(same, regrets):
    positive = jnp.maximum(regrets, 0.0) + DELTA
    return positive / node_totals(same, positive)


def split_terms(reach):
    high = reach.astype(BF16).astype(F32)
    return [high, reach - high]


def joined(out, first):
    middle = first + BOARD_LEAVES
    return out[first:middle] + out[middle : middle + BOARD_LEAVES]


def column_of(row):
    return jnp.broadcast_to(row, (128, 128)).T


def same_node(row):
    equal = jnp.where(jnp.broadcast_to(row, (128, 128)) == column_of(row), 1.0, 0.0)
    equal = equal[:WINDOW, :WINDOW]
    return jnp.concatenate([equal, equal, equal], axis=1).astype(BF16)


def board_rows(free, boards):
    return jnp.concatenate(
        [jnp.broadcast_to(free[b : b + 1], (BOARD_LEAVES, WIDE)) for b in boards], axis=0
    )


def first_kernel(
    outer_ref,
    regrets_ref,
    chance_ref,
    even_ref,
    cross_ref,
    regrets_other_ref,
    chance_other_ref,
    even_other_ref,
    cross_other_ref,
    nodes_ref,
    own_free_ref,
    pots_ref,
    own_matrix_ref,
    near_ref,
    far_ref,
    window_ref,
    reached_ref,
    instant_ref,
    sums_ref,
    same_ref,
    free_ref,
    pot_ref,
    policy_ref,
    terms_ref,
    values_ref,
):
    left, right = sides(even_ref, cross_ref, slice(0, 30))
    left_other, right_other = sides(even_other_ref, cross_other_ref, slice(0, 15))
    same_ref[0] = same_node(nodes_ref[0:1, :])
    same_ref[1] = same_node(regrets_other_ref[OWN : OWN + 1, 0:128])
    free_ref[...] = jnp.zeros_like(free_ref)
    free_ref[0:2, :HANDS] = left[27:29]
    free_ref[2:6] = own_free_ref[0:4]
    free_ref[6:8, :HANDS] = right[27:29]
    pot_ref[0:SIDE] = column_of(left[29:30, 0:128])[SIDE:OWN]
    pot_ref[SIDE : SIDE + OWN] = column_of(pots_ref[0:1, :])[:OWN]
    pot_ref[SIDE + OWN :] = column_of(right[29:30, 0:128])[:SIDE]
    window_ref[...] = jnp.zeros_like(window_ref)
    reached_ref[...] = jnp.zeros_like(reached_ref)
    policy_ref[...] = jnp.zeros_like(policy_ref)
    low, high = SIDE, SIDE + OWN
    window_ref[0, low - 15 : low, :HANDS] = left[0:15]
    window_ref[0, low:high, :HANDS] = regrets_ref[:OWN]
    window_ref[0, high : high + 15, :HANDS] = right[0:15]
    policy_ref[0, low - 10 : low, :HANDS] = left[15:25]
    policy_ref[0, low : high - EARLY, :HANDS] = chance_ref[...]
    policy_ref[0, high - EARLY : high, :HANDS] = regrets_ref[OWN + 1 :]
    policy_ref[0, high : high + 10, :HANDS] = right[15:25]
    window_ref[1, low - 10 : low, :HANDS] = left_other[0:10]
    window_ref[1, low:high, :HANDS] = regrets_other_ref[:OWN]
    window_ref[1, high : high + 10, :HANDS] = right_other[0:10]
    reached_ref[low - 5 : low, :HANDS] = left_other[10:15]
    reached_ref[low : high - EARLY, :HANDS] = chance_other_ref[...]
    reached_ref[high - EARLY : high, :HANDS] = regrets_other_ref[OWN + 1 :]
    reached_ref[high : high + 5, :HANDS] = right_other[10:15]
    free = board_rows(free_ref, range(8))
    reached_ref[...] = reached_ref[...] * free
    terms = []
    for p in range(2):
        chance = policy_ref[0] * free if p == 0 else reached_ref[...]
        policy = policy_of(same_ref[p], window_ref[p])
        policy_ref[p] = policy
        terms.append(split_terms(chance * policy))
    for b in range(8):
        rows = slice(b * BOARD_LEAVES, (b + 1) * BOARD_LEAVES)
        block = jnp.concatenate([term[rows] for player in terms for term in player], axis=0)
        terms_ref[b] = block.astype(BF16)

    def board(b, matrix):
        out = jnp.dot(terms_ref[b], matrix, preferred_element_type=F32)
        rows = slice(b * BOARD_LEAVES, (b + 1) * BOARD_LEAVES)
        factor = pot_ref[rows, 0:1] * (-1.0 / HANDS)
        free = free_ref[b : b + 1, :]
        values_ref[1, rows, :] = joined(out, 0) * factor * free
        values_ref[0, rows, :] = joined(out, PIECES * BOARD_LEAVES) * factor * free

    for b in range(4):
        board(b + 2, own_matrix_ref[b])
    board(1, near_ref[0])
    board(6, near_ref[1])

    outer = jnp.max(outer_ref[0:1, :]) > 0.5

    @pl.when(outer)
    def _():
        board(0, far_ref[0])
        board(7, far_ref[1])

    @pl.when(jnp.logical_not(outer))
    def _():
        for p in range(2):
            for b in (0, 7):
                rows = slice(b * BOARD_LEAVES, (b + 1) * BOARD_LEAVES)
                values_ref[p, rows, :] = jnp.zeros((BOARD_LEAVES, WIDE), F32)

    sums = []
    for p in range(2):
        values = values_ref[p]
        instant = values - node_totals(same_ref[p], policy_ref[p] * values)
        instant_ref[p] = instant
        mine = instant[SIDE : SIDE + OWN]
        sums.append(jnp.sum(mine * mine))
    lane = lax.broadcasted_iota(jnp.int32, sums_ref.shape, 1)
    sums_ref[...] = jnp.where(lane == 0, sums[0], jnp.where(lane == 1, sums[1], 0.0))


def first(arrays):
    shapes = (
        jax.ShapeDtypeStruct((2, WINDOW, WIDE), F32),
        jax.ShapeDtypeStruct((WINDOW, WIDE), F32),
        jax.ShapeDtypeStruct((2, WINDOW, WIDE), F32),
        jax.ShapeDtypeStruct((128, 128), F32),
        jax.ShapeDtypeStruct((2, WINDOW, 3 * WINDOW), BF16),
        jax.ShapeDtypeStruct((8, WIDE), F32),
        jax.ShapeDtypeStruct((WINDOW, 128), F32),
    )
    return pl.pallas_call(
        first_kernel,
        out_shape=shapes,
        in_specs=[VMEM()] * len(arrays),
        out_specs=[VMEM()] * len(shapes),
        scratch_shapes=[
            pltpu.VMEM((2, WINDOW, WIDE), F32),
            pltpu.VMEM((8, 2 * PIECES * BOARD_LEAVES, WIDE), BF16),
            pltpu.VMEM((2, WINDOW, WIDE), F32),
        ],
        compiler_params=pltpu.CompilerParams(vmem_limit_bytes=LIMIT),
        name="first",
    )(*arrays)


def second_kernel(
    gathered_ref,
    window_ref,
    reached_ref,
    instant_ref,
    same_ref,
    free_ref,
    pot_ref,
    own_matrix_ref,
    near_ref,
    out_values_ref,
    moved_ref,
    mine_ref,
    sums_ref,
    policy_ref,
    terms_ref,
    values_ref,
    *,
    count,
):
    values_ref[...] = jnp.zeros_like(values_ref)
    sums = jnp.sum(gathered_ref[...], axis=0, keepdims=True)
    scale = jnp.sqrt(sums / count + EPSILON)
    moved = window_ref[0] + instant_ref[0] / scale[:, 0:1]
    moved_ref[...] = moved[SIDE : SIDE + OWN]
    policy_ref[...] = policy_of(same_ref[0], moved)
    other = window_ref[1] + instant_ref[1] / scale[:, 1:2]
    terms = split_terms(reached_ref[...] * policy_of(same_ref[1], other))
    for b in range(8):
        rows = slice(b * BOARD_LEAVES, (b + 1) * BOARD_LEAVES)
        block = jnp.concatenate([term[rows] for term in terms], axis=0)
        terms_ref[b] = block.astype(BF16)

    def board(b, matrix):
        out = jnp.dot(terms_ref[b], matrix, preferred_element_type=F32)
        rows = slice(b * BOARD_LEAVES, (b + 1) * BOARD_LEAVES)
        factor = pot_ref[rows, 0:1] * (-1.0 / HANDS)
        values_ref[rows, :] = joined(out, 0) * factor * free_ref[b : b + 1, :]

    for b in range(4):
        board(b + 2, own_matrix_ref[b])
    board(1, near_ref[0])
    board(6, near_ref[1])

    values = values_ref[...]
    instant = values - node_totals(same_ref[0], policy_ref[...] * values)
    mine = instant[SIDE : SIDE + OWN]
    mine_ref[...] = mine
    out_values_ref[...] = values[SIDE : SIDE + OWN, :HANDS]
    lane = lax.broadcasted_iota(jnp.int32, sums_ref.shape, 1)
    sums_ref[...] = jnp.where(lane == 0, jnp.sum(mine * mine), 0.0)


def second(gathered, window, reached, instant, same, free, pot, matrices, count):
    shapes = (
        jax.ShapeDtypeStruct((OWN, HANDS), F32),
        jax.ShapeDtypeStruct((OWN, WIDE), F32),
        jax.ShapeDtypeStruct((OWN, WIDE), F32),
        jax.ShapeDtypeStruct((128, 128), F32),
    )
    arrays = (gathered, window, reached, instant, same, free, pot) + matrices
    return pl.pallas_call(
        functools.partial(second_kernel, count=count),
        out_shape=shapes,
        in_specs=[VMEM()] * len(arrays),
        out_specs=[VMEM()] * len(shapes),
        scratch_shapes=[
            pltpu.VMEM((WINDOW, WIDE), F32),
            pltpu.VMEM((8, PIECES * BOARD_LEAVES, WIDE), BF16),
            pltpu.VMEM((WINDOW, WIDE), F32),
        ],
        compiler_params=pltpu.CompilerParams(vmem_limit_bytes=LIMIT),
        name="second",
    )(*arrays)


def tail_kernel(gathered_ref, moved_ref, mine_ref, out_ref, *, count):
    sums = jnp.sum(gathered_ref[...], axis=0, keepdims=True)
    scale = jnp.sqrt(sums / count + EPSILON)[:, 0:1]
    out_ref[...] = (moved_ref[...] + mine_ref[...] / scale)[:, :HANDS]


def tail(gathered, moved, mine, count):
    return pl.pallas_call(
        functools.partial(tail_kernel, count=count),
        out_shape=jax.ShapeDtypeStruct((OWN, HANDS), F32),
        in_specs=[VMEM()] * 3,
        out_specs=VMEM(),
        compiler_params=pltpu.CompilerParams(vmem_limit_bytes=SMALL),
        name="tail",
    )(gathered, moved, mine)


def local(chance_reach, regrets_start, pot, parent, hand_cards, board_cards, hand_rank):
    devices = lax.axis_size(LEAF)
    leaf_count = parent.shape[1]

    even_pairs = [(i, i ^ 1) for i in range(devices)]
    cross_pairs = [(i, i + 1) for i in range(1, devices - 1, 2)]
    cross_pairs = cross_pairs + [(j, i) for i, j in cross_pairs]

    def diagonal(pairs):
        return [(2 * i + p, 2 * j + 1 - p) for i, j in pairs for p in range(2)]

    regrets, chance, even, cross, even_other, cross_other, ranks, free, holding, pots, nodes = pack(
        board_cards, pot[None], regrets_start[0], chance_reach[0], hand_rank,
        hand_cards.T, parent.reshape(-1, 128),
    )
    cross = lax.ppermute(cross, LEAF, cross_pairs)
    even = lax.ppermute(even, LEAF, even_pairs)
    regrets_other = lax.ppermute(regrets, "player", [(0, 1), (1, 0)])
    chance_other = lax.ppermute(chance, "player", [(0, 1), (1, 0)])
    both = LEAF + ("player",)
    even_other = lax.ppermute(even_other, both, diagonal(even_pairs))
    cross_other = lax.ppermute(cross_other, both, diagonal(cross_pairs))

    own_matrix, apart = build_own(holding, ranks)
    near, far, outer = build_side(even, cross, nodes, regrets_other, apart)


    def gathered(sums):
        return lax.all_to_all(sums.reshape(devices, 1, 128), LEAF, 0, 0).reshape(128, 128)

    count = float(leaf_count * HANDS)
    window, reached, instant, sums, same, all_free, all_pot = first(
        (outer, regrets, chance, even, cross, regrets_other, chance_other, even_other)
        + (cross_other,)
        + (nodes, free, pots, own_matrix, near, far),
    )
    values, moved, mine, sums = second(
        gathered(sums), window, reached, instant, same, all_free, all_pot,
        (own_matrix, near), count,
    )
    final = tail(gathered(sums), moved, mine, count)
    return (final[None], values[None])


def solution(mesh):
    split = Mesh(
        mesh.devices.reshape(*LEAF_SIZES, mesh.shape["player"]),
        LEAF + ("player",),
    )
    placed = (
        P("player", LEAF, None),
        P("player", LEAF, None),
        P(LEAF),
        P("player", None),
        P(),
        P(LEAF, None),
        P(LEAF, None),
    )
    return jax.shard_map(
        local,
        mesh=split,
        in_specs=placed,
        out_specs=(P("player", LEAF, None), P("player", LEAF, None)),
        check_vma=False,
    )
```

```python
import functools

import jax
import jax.numpy as jnp
from jax import lax
from jax.experimental import pallas as pl
from jax.experimental.pallas import tpu as pltpu
from jax.sharding import Mesh
from jax.sharding import PartitionSpec as P

LEAF = ("leaf_0", "leaf_1", "leaf_2", "leaf_3")
LEAF_SIZES = (4, 4, 4, 2)
DELTA = 0.05
EPSILON = 1e-06

HANDS = 1326
WIDE = 1408
OWN = 32
SIDE = 16
WINDOW = OWN + 2 * SIDE
BOARD_LEAVES = 8
EDGE = 32
EARLY = 2
LIMIT = 7 << 20
SMALL = 6 << 20
PIECES = 2
BF16 = jnp.bfloat16
F32 = jnp.float32
VMEM = functools.partial(pl.BlockSpec, memory_space=pltpu.VMEM)


def leaf_block():
    index = 0
    for axis, size in zip(LEAF, LEAF_SIZES):
        index = index * size + lax.axis_index(axis)
    return index


def is_odd():
    return lax.axis_index(LEAF[-1]) == 1


def edge_rows(regrets_ref, chance_ref, edge_ref, last):
    at = OWN - 10 if last else 0
    edge_ref[0:10] = regrets_ref[at : at + 10]
    if last:
        edge_ref[10 : 15 - EARLY] = chance_ref[OWN - 5 : OWN - EARLY]
        edge_ref[15 - EARLY : 15] = regrets_ref[OWN + 1 :]
    else:
        edge_ref[10:15] = chance_ref[0:5]
    edge_ref[15:16] = jnp.zeros((1, HANDS), F32)


def forward_kernel(regrets_ref, chance_ref, after_ref, edge_ref):
    odd = is_odd()

    @pl.when(odd)
    def _():
        edge_rows(regrets_ref, chance_ref, edge_ref, False)

    @pl.when(jnp.logical_not(odd))
    def _():
        edge_rows(regrets_ref, chance_ref, edge_ref, True)


def forward(regrets, chance, after):
    return pl.pallas_call(
        forward_kernel,
        out_shape=jax.ShapeDtypeStruct((16, HANDS), F32),
        in_specs=[VMEM()] * 3,
        out_specs=VMEM(),
        compiler_params=pltpu.CompilerParams(vmem_limit_bytes=SMALL),
        name="forward",
    )(regrets, chance, after)


def pack_kernel(
    boards_hbm, pot_hbm, regrets_hbm, chance_hbm, rank_hbm, cards_hbm, parent_hbm,
    regrets_ref, chance_ref, even_ref, cross_ref, cross_other_ref,
    wide_rank_ref, free_ref, holding_ref, pots_ref, nodes_ref,
    board_cards_ref, pot_ref, rank_ref, cards_ref, parent_ref, all_chance_ref, sems,
):
    moves = [
        (boards_hbm, board_cards_ref),
        (rank_hbm, rank_ref),
        (cards_hbm, cards_ref),
        (parent_hbm, parent_ref),
        (regrets_hbm, regrets_ref.at[:OWN]),
        (chance_hbm, all_chance_ref),
        (pot_hbm, pot_ref),
    ]
    copies = [
        pltpu.make_async_copy(source, target, sems.at[at])
        for at, (source, target) in enumerate(moves)
    ]
    for copy in copies:
        copy.start()
    pots_ref[...] = jnp.zeros_like(pots_ref)
    wide_rank_ref[...] = jnp.zeros_like(wide_rank_ref)
    free_ref[...] = jnp.zeros_like(free_ref)
    holding_ref[...] = jnp.zeros_like(holding_ref)
    for copy in copies[:4]:
        copy.wait()
    ranks = rank_ref[...].astype(F32)
    lower, upper = cards_ref[0:1, :], cards_ref[1:2, :]
    rows = []
    for b in range(4):
        taken = jnp.zeros((1, HANDS), jnp.bool_)
        for j in range(5):
            card = board_cards_ref[b, j]
            taken = taken | (lower == card) | (upper == card)
        rows.append(jnp.where(taken, 0.0, 1.0))
    wide_rank_ref[0:4, :HANDS] = ranks
    for b in range(4):
        free_ref[b : b + 1, :HANDS] = rows[b]
    deck = lax.broadcasted_iota(jnp.int32, (128, HANDS), 0)
    holding_ref[:, :HANDS] = jnp.where((deck == lower) | (deck == upper), 1.0, 0.0).astype(BF16)

    leaves = parent_ref.shape[0] * 128
    begin = leaf_block() * OWN - SIDE
    line = (begin + 128) // 128 - 1
    held = [
        parent_ref[pl.ds(jnp.clip(line + j, 0, leaves // 128 - 1), 1), :].astype(F32)
        for j in range(2)
    ]
    held = jnp.broadcast_to(jnp.concatenate(held, axis=1), (8, 256))
    held = pltpu.roll(held, lax.rem((line + 2) * 128 - begin, 256), 1)[0:1, 0:128]
    leaf = begin + lax.broadcasted_iota(jnp.int32, (1, 128), 1)
    held = jnp.where((leaf >= 0) & (leaf < leaves), held, -1.0)
    nodes_ref[...] = jnp.broadcast_to(held, nodes_ref.shape)
    for copy in copies[4:]:
        copy.wait()
    pots_ref[0:1, 0:OWN] = pot_ref[...]
    chance_ref[...] = all_chance_ref[0 : OWN - EARLY]
    regrets_ref[OWN + 1 :] = all_chance_ref[OWN - EARLY :]

    odd = is_odd()

    def ends(ref, last):
        at = OWN - 15 if last else 0
        ref[0:15] = regrets_ref[at : at + 15]
        at = OWN - 10 if last else 0
        ref[15:25] = all_chance_ref[at : at + 10]
        at = 2 if last else 0
        ref[25:27] = ranks[at : at + 2]
        ref[27:28] = rows[at]
        ref[28:29] = rows[at + 1]
        ref[29:30] = jnp.zeros((1, HANDS), F32)
        ref[29:30, 0:128] = pots_ref[0:1, :]
        ref[30:] = jnp.zeros((EDGE - 30, HANDS), F32)

    @pl.when(odd)
    def _():
        ends(even_ref, False)
        ends(cross_ref, True)
        edge_rows(regrets_ref, chance_ref, cross_other_ref, True)

    @pl.when(jnp.logical_not(odd))
    def _():
        ends(even_ref, True)
        ends(cross_ref, False)
        edge_rows(regrets_ref, chance_ref, cross_other_ref, False)

    regrets_ref[OWN : OWN + 1] = jnp.zeros((1, HANDS), F32)
    regrets_ref[OWN : OWN + 1, 0:128] = held


HBM = functools.partial(pl.BlockSpec, memory_space=pltpu.HBM)


def in_hbm(array):
    return pltpu.with_memory_space_constraint(array, pltpu.HBM)


def pack(board_cards, pot_row, regrets, chance, hand_rank, cards, parent):
    shapes = (
        jax.ShapeDtypeStruct((OWN + 1 + EARLY, HANDS), F32),
        jax.ShapeDtypeStruct((OWN - EARLY, HANDS), F32),
        jax.ShapeDtypeStruct((EDGE, HANDS), F32),
        jax.ShapeDtypeStruct((EDGE, HANDS), F32),
        jax.ShapeDtypeStruct((16, HANDS), F32),
        jax.ShapeDtypeStruct((8, WIDE), F32),
        jax.ShapeDtypeStruct((8, WIDE), F32),
        jax.ShapeDtypeStruct((128, WIDE), BF16),
        jax.ShapeDtypeStruct((8, 128), F32),
        jax.ShapeDtypeStruct((8, 128), F32),
    )
    large = (board_cards, pot_row, regrets, chance, hand_rank, cards, parent)
    return pl.pallas_call(
        pack_kernel,
        out_shape=shapes,
        in_specs=[HBM()] * len(large),
        out_specs=[VMEM()] * len(shapes),
        scratch_shapes=[
            pltpu.SMEM((4, 5), jnp.int32),
            pltpu.VMEM((1, OWN), F32),
            pltpu.VMEM((4, HANDS), jnp.int32),
            pltpu.VMEM((2, HANDS), jnp.int32),
            pltpu.VMEM(parent.shape, jnp.int32),
            pltpu.VMEM((OWN, HANDS), F32),
            pltpu.SemaphoreType.DMA((7,)),
        ],
        compiler_params=pltpu.CompilerParams(vmem_limit_bytes=SMALL),
        name="pack",
    )(*map(in_hbm, large))


def sides(even_ref, cross_ref, rows):
    odd = is_odd()
    even, cross = even_ref[rows], cross_ref[rows]
    return jnp.where(odd, even, cross), jnp.where(odd, cross, even)


def fill(rank_ref, apart_ref, column_ref, targets, step):
    ranks = rank_ref[...]
    for t in range(WIDE // 128):
        lanes = slice(t * 128, (t + 1) * 128)
        tile = jnp.concatenate([ranks[:, lanes], jnp.zeros((120, 128), F32)], axis=0)
        column_ref[lanes, :] = tile.T

    @pl.loop(0, WIDE // step)
    def _(i):
        rows = pl.ds(pl.multiple_of(i * step, step), step)
        column = column_ref[rows, :]
        own = [jnp.broadcast_to(column[:, b : b + 1], (step, 128)) for b, _, _ in targets]
        for t in range(WIDE // 128):
            lanes = slice(t * 128, (t + 1) * 128)
            apart = apart_ref[rows, lanes]
            minus = -apart
            for at, (b, matrix_ref, slot) in enumerate(targets):
                gap = (own[at] - rank_ref[b : b + 1, lanes]).astype(BF16)
                matrix_ref[slot, rows, lanes] = jnp.minimum(jnp.maximum(gap, minus), apart)


def build_own_kernel(holding_ref, rank_ref, matrix_ref, apart_ref, column_ref):
    holding = holding_ref[...]
    half = WIDE // 2
    for rows in (slice(0, half), slice(half, WIDE)):
        shared = jnp.dot(holding.T[rows], holding, preferred_element_type=F32)
        apart_ref[rows, :] = (1.0 - jnp.minimum(shared, 1.0)).astype(BF16)
    fill(rank_ref, apart_ref, column_ref, [(b, matrix_ref, b) for b in range(4)], 352)


def outer_boards(mine, other):
    leaf = lax.broadcasted_iota(jnp.int32, mine.shape, 1)
    inside = leaf < WINDOW

    def node_at(row, at):
        return jnp.max(jnp.where(leaf == at, row, -2.0))

    def ends_of(row, node):
        held = inside & (row == node)
        return jnp.min(jnp.where(held, leaf, WINDOW)), jnp.max(jnp.where(held, leaf, -1))

    begin, _ = ends_of(mine, node_at(mine, SIDE))
    begin, _ = ends_of(other, node_at(other, begin))
    _, end = ends_of(mine, node_at(mine, SIDE + OWN - 1))
    _, end = ends_of(other, node_at(other, end))
    return (begin < BOARD_LEAVES) | (end >= WINDOW - BOARD_LEAVES)


def side_ranks(even_ref, cross_ref, rank_ref):
    left, right = sides(even_ref, cross_ref, slice(25, 27))
    rank_ref[...] = jnp.zeros_like(rank_ref)
    rank_ref[0:2, :HANDS] = left
    rank_ref[2:4, :HANDS] = right


def build_near_kernel(
    even_ref, cross_ref, apart_ref, near_ref, token_ref, rank_ref, column_ref
):
    token_ref[...] = jnp.zeros_like(token_ref)
    side_ranks(even_ref, cross_ref, rank_ref)
    fill(rank_ref, apart_ref, column_ref, [(1, near_ref, 0), (2, near_ref, 1)], 128)


def build_far_kernel(
    even_ref, cross_ref, nodes_ref, regrets_other_ref, apart_ref, after_ref,
    far_ref, outer_ref, rank_ref, column_ref,
):
    outer = outer_boards(nodes_ref[0:1, :], regrets_other_ref[OWN : OWN + 1, 0:128])
    outer_ref[...] = jnp.where(outer, jnp.ones_like(outer_ref), jnp.zeros_like(outer_ref))

    @pl.when(outer)
    def _():
        side_ranks(even_ref, cross_ref, rank_ref)
        fill(rank_ref, apart_ref, column_ref, [(0, far_ref, 0), (3, far_ref, 1)], 128)


BUILD_COST = pl.CostEstimate(
    flops=32 * WIDE * WIDE, bytes_accessed=8 * WIDE * WIDE, transcendentals=0
)


def matrices_shape(boards):
    return jax.ShapeDtypeStruct((boards, WIDE, WIDE), BF16)


def build_own(holding, ranks):
    return pl.pallas_call(
        build_own_kernel,
        out_shape=(matrices_shape(4), jax.ShapeDtypeStruct((WIDE, WIDE), BF16)),
        in_specs=[VMEM()] * 2,
        out_specs=[VMEM()] * 2,
        scratch_shapes=[pltpu.VMEM((WIDE, 128), F32)],
        compiler_params=pltpu.CompilerParams(vmem_limit_bytes=LIMIT),
        cost_estimate=BUILD_COST,
        name="build_own",
    )(holding, ranks)


def build_pair(kernel, name, arrays):
    return pl.pallas_call(
        kernel,
        out_shape=(matrices_shape(2), jax.ShapeDtypeStruct((8, 128), F32)),
        in_specs=[VMEM()] * len(arrays),
        out_specs=[VMEM()] * 2,
        scratch_shapes=[pltpu.VMEM((8, WIDE), F32), pltpu.VMEM((WIDE, 128), F32)],
        compiler_params=pltpu.CompilerParams(vmem_limit_bytes=LIMIT),
        cost_estimate=BUILD_COST,
        name=name,
    )(*arrays)


def node_totals(same, values):
    high = values.astype(BF16)
    rest = values - high.astype(F32)
    middle = rest.astype(BF16)
    low = (rest - middle.astype(F32)).astype(BF16)
    parts = jnp.concatenate([high, middle, low], axis=0)
    return jnp.dot(same, parts, preferred_element_type=F32)


def policy_of(same, regrets):
    positive = jnp.maximum(regrets, 0.0) + DELTA
    return positive / node_totals(same, positive)


def split_terms(reach):
    high = reach.astype(BF16).astype(F32)
    return [high, reach - high]


def joined(out, first):
    middle = first + BOARD_LEAVES
    return out[first:middle] + out[middle : middle + BOARD_LEAVES]


def column_of(row):
    return jnp.broadcast_to(row, (128, 128)).T


def same_node(row):
    equal = jnp.where(jnp.broadcast_to(row, (128, 128)) == column_of(row), 1.0, 0.0)
    equal = equal[:WINDOW, :WINDOW]
    return jnp.concatenate([equal, equal, equal], axis=1).astype(BF16)


def board_rows(free, boards):
    return jnp.concatenate(
        [jnp.broadcast_to(free[b : b + 1], (BOARD_LEAVES, WIDE)) for b in boards], axis=0
    )


def first_kernel(
    outer_ref,
    regrets_ref,
    chance_ref,
    even_ref,
    cross_ref,
    regrets_other_ref,
    chance_other_ref,
    even_other_ref,
    cross_other_ref,
    nodes_ref,
    own_free_ref,
    pots_ref,
    own_matrix_ref,
    near_ref,
    far_ref,
    window_ref,
    reached_ref,
    instant_ref,
    sums_ref,
    same_ref,
    free_ref,
    pot_ref,
    policy_ref,
    terms_ref,
    values_ref,
):
    left, right = sides(even_ref, cross_ref, slice(0, 30))
    left_other, right_other = sides(even_other_ref, cross_other_ref, slice(0, 15))
    same_ref[0] = same_node(nodes_ref[0:1, :])
    same_ref[1] = same_node(regrets_other_ref[OWN : OWN + 1, 0:128])
    free_ref[...] = jnp.zeros_like(free_ref)
    free_ref[0:2, :HANDS] = left[27:29]
    free_ref[2:6] = own_free_ref[0:4]
    free_ref[6:8, :HANDS] = right[27:29]
    pot_ref[0:SIDE] = column_of(left[29:30, 0:128])[SIDE:OWN]
    pot_ref[SIDE : SIDE + OWN] = column_of(pots_ref[0:1, :])[:OWN]
    pot_ref[SIDE + OWN :] = column_of(right[29:30, 0:128])[:SIDE]
    window_ref[...] = jnp.zeros_like(window_ref)
    reached_ref[...] = jnp.zeros_like(reached_ref)
    policy_ref[...] = jnp.zeros_like(policy_ref)
    low, high = SIDE, SIDE + OWN
    window_ref[0, low - 15 : low, :HANDS] = left[0:15]
    window_ref[0, low:high, :HANDS] = regrets_ref[:OWN]
    window_ref[0, high : high + 15, :HANDS] = right[0:15]
    policy_ref[0, low - 10 : low, :HANDS] = left[15:25]
    policy_ref[0, low : high - EARLY, :HANDS] = chance_ref[...]
    policy_ref[0, high - EARLY : high, :HANDS] = regrets_ref[OWN + 1 :]
    policy_ref[0, high : high + 10, :HANDS] = right[15:25]
    window_ref[1, low - 10 : low, :HANDS] = left_other[0:10]
    window_ref[1, low:high, :HANDS] = regrets_other_ref[:OWN]
    window_ref[1, high : high + 10, :HANDS] = right_other[0:10]
    reached_ref[low - 5 : low, :HANDS] = left_other[10:15]
    reached_ref[low : high - EARLY, :HANDS] = chance_other_ref[...]
    reached_ref[high - EARLY : high, :HANDS] = regrets_other_ref[OWN + 1 :]
    reached_ref[high : high + 5, :HANDS] = right_other[10:15]
    free = board_rows(free_ref, range(8))
    reached_ref[...] = reached_ref[...] * free
    terms = []
    for p in range(2):
        chance = policy_ref[0] * free if p == 0 else reached_ref[...]
        policy = policy_of(same_ref[p], window_ref[p])
        policy_ref[p] = policy
        terms.append(split_terms(chance * policy))
    for b in range(8):
        rows = slice(b * BOARD_LEAVES, (b + 1) * BOARD_LEAVES)
        block = jnp.concatenate([term[rows] for player in terms for term in player], axis=0)
        terms_ref[b] = block.astype(BF16)

    def board(b, matrix):
        out = jnp.dot(terms_ref[b], matrix, preferred_element_type=F32)
        rows = slice(b * BOARD_LEAVES, (b + 1) * BOARD_LEAVES)
        factor = pot_ref[rows, 0:1] * (-1.0 / HANDS)
        free = free_ref[b : b + 1, :]
        values_ref[1, rows, :] = joined(out, 0) * factor * free
        values_ref[0, rows, :] = joined(out, PIECES * BOARD_LEAVES) * factor * free

    for b in range(4):
        board(b + 2, own_matrix_ref[b])
    board(1, near_ref[0])
    board(6, near_ref[1])

    outer = jnp.max(outer_ref[0:1, :]) > 0.5

    @pl.when(outer)
    def _():
        board(0, far_ref[0])
        board(7, far_ref[1])

    @pl.when(jnp.logical_not(outer))
    def _():
        for p in range(2):
            for b in (0, 7):
                rows = slice(b * BOARD_LEAVES, (b + 1) * BOARD_LEAVES)
                values_ref[p, rows, :] = jnp.zeros((BOARD_LEAVES, WIDE), F32)

    sums = []
    for p in range(2):
        values = values_ref[p]
        instant = values - node_totals(same_ref[p], policy_ref[p] * values)
        instant_ref[p] = instant
        mine = instant[SIDE : SIDE + OWN]
        sums.append(jnp.sum(mine * mine))
    lane = lax.broadcasted_iota(jnp.int32, sums_ref.shape, 1)
    sums_ref[...] = jnp.where(lane == 0, sums[0], jnp.where(lane == 1, sums[1], 0.0))


def first(arrays):
    shapes = (
        jax.ShapeDtypeStruct((2, WINDOW, WIDE), F32),
        jax.ShapeDtypeStruct((WINDOW, WIDE), F32),
        jax.ShapeDtypeStruct((2, WINDOW, WIDE), F32),
        jax.ShapeDtypeStruct((128, 128), F32),
        jax.ShapeDtypeStruct((2, WINDOW, 3 * WINDOW), BF16),
        jax.ShapeDtypeStruct((8, WIDE), F32),
        jax.ShapeDtypeStruct((WINDOW, 128), F32),
    )
    return pl.pallas_call(
        first_kernel,
        out_shape=shapes,
        in_specs=[VMEM()] * len(arrays),
        out_specs=[VMEM()] * len(shapes),
        scratch_shapes=[
            pltpu.VMEM((2, WINDOW, WIDE), F32),
            pltpu.VMEM((8, 2 * PIECES * BOARD_LEAVES, WIDE), BF16),
            pltpu.VMEM((2, WINDOW, WIDE), F32),
        ],
        compiler_params=pltpu.CompilerParams(vmem_limit_bytes=LIMIT),
        name="first",
    )(*arrays)


def second_kernel(
    gathered_ref,
    window_ref,
    reached_ref,
    instant_ref,
    same_ref,
    free_ref,
    pot_ref,
    own_matrix_ref,
    near_ref,
    out_values_ref,
    moved_ref,
    mine_ref,
    sums_ref,
    policy_ref,
    terms_ref,
    values_ref,
    *,
    count,
):
    values_ref[...] = jnp.zeros_like(values_ref)
    sums = jnp.sum(gathered_ref[...], axis=0, keepdims=True)
    scale = jnp.sqrt(sums / count + EPSILON)
    moved = window_ref[0] + instant_ref[0] / scale[:, 0:1]
    moved_ref[...] = moved[SIDE : SIDE + OWN]
    policy_ref[...] = policy_of(same_ref[0], moved)
    other = window_ref[1] + instant_ref[1] / scale[:, 1:2]
    terms = split_terms(reached_ref[...] * policy_of(same_ref[1], other))
    for b in range(8):
        rows = slice(b * BOARD_LEAVES, (b + 1) * BOARD_LEAVES)
        block = jnp.concatenate([term[rows] for term in terms], axis=0)
        terms_ref[b] = block.astype(BF16)

    def board(b, matrix):
        out = jnp.dot(terms_ref[b], matrix, preferred_element_type=F32)
        rows = slice(b * BOARD_LEAVES, (b + 1) * BOARD_LEAVES)
        factor = pot_ref[rows, 0:1] * (-1.0 / HANDS)
        values_ref[rows, :] = joined(out, 0) * factor * free_ref[b : b + 1, :]

    for b in range(4):
        board(b + 2, own_matrix_ref[b])
    board(1, near_ref[0])
    board(6, near_ref[1])

    values = values_ref[...]
    instant = values - node_totals(same_ref[0], policy_ref[...] * values)
    mine = instant[SIDE : SIDE + OWN]
    mine_ref[...] = mine
    out_values_ref[...] = values[SIDE : SIDE + OWN, :HANDS]
    lane = lax.broadcasted_iota(jnp.int32, sums_ref.shape, 1)
    sums_ref[...] = jnp.where(lane == 0, jnp.sum(mine * mine), 0.0)


def second(gathered, window, reached, instant, same, free, pot, matrices, count):
    shapes = (
        jax.ShapeDtypeStruct((OWN, HANDS), F32),
        jax.ShapeDtypeStruct((OWN, WIDE), F32),
        jax.ShapeDtypeStruct((OWN, WIDE), F32),
        jax.ShapeDtypeStruct((128, 128), F32),
    )
    arrays = (gathered, window, reached, instant, same, free, pot) + matrices
    return pl.pallas_call(
        functools.partial(second_kernel, count=count),
        out_shape=shapes,
        in_specs=[VMEM()] * len(arrays),
        out_specs=[VMEM()] * len(shapes),
        scratch_shapes=[
            pltpu.VMEM((WINDOW, WIDE), F32),
            pltpu.VMEM((8, PIECES * BOARD_LEAVES, WIDE), BF16),
            pltpu.VMEM((WINDOW, WIDE), F32),
        ],
        compiler_params=pltpu.CompilerParams(vmem_limit_bytes=LIMIT),
        name="second",
    )(*arrays)


def tail_kernel(gathered_ref, moved_ref, mine_ref, out_ref, *, count):
    sums = jnp.sum(gathered_ref[...], axis=0, keepdims=True)
    scale = jnp.sqrt(sums / count + EPSILON)[:, 0:1]
    out_ref[...] = (moved_ref[...] + mine_ref[...] / scale)[:, :HANDS]


def tail(gathered, moved, mine, count):
    return pl.pallas_call(
        functools.partial(tail_kernel, count=count),
        out_shape=jax.ShapeDtypeStruct((OWN, HANDS), F32),
        in_specs=[VMEM()] * 3,
        out_specs=VMEM(),
        compiler_params=pltpu.CompilerParams(vmem_limit_bytes=SMALL),
        name="tail",
    )(gathered, moved, mine)


def local(chance_reach, regrets_start, pot, parent, hand_cards, board_cards, hand_rank):
    devices = lax.axis_size(LEAF)
    leaf_count = parent.shape[1]

    even_pairs = [(i, i ^ 1) for i in range(devices)]
    cross_pairs = [(i, i + 1) for i in range(1, devices - 1, 2)]
    cross_pairs = cross_pairs + [(j, i) for i, j in cross_pairs]

    diagonal = [(2 * i + p, 2 * j + 1 - p) for i, j in cross_pairs for p in range(2)]

    regrets, chance, even, cross, cross_other, ranks, free, holding, pots, nodes = pack(
        board_cards, pot[None], regrets_start[0], chance_reach[0], hand_rank,
        hand_cards.T, parent.reshape(-1, 128),
    )
    cross = lax.ppermute(cross, LEAF, cross_pairs)
    even = lax.ppermute(even, LEAF, even_pairs)
    regrets_other = lax.ppermute(regrets, "player", [(0, 1), (1, 0)])
    chance_other = lax.ppermute(chance, "player", [(0, 1), (1, 0)])
    cross_other = lax.ppermute(cross_other, LEAF + ("player",), diagonal)

    own_matrix, apart = build_own(holding, ranks)
    near, built = build_pair(build_near_kernel, "build_near", (even, cross, apart))
    rows = forward(regrets_other, chance_other, built)
    even_other = lax.ppermute(rows, LEAF, even_pairs)
    far, outer = build_pair(
        build_far_kernel, "build_far", (even, cross, nodes, regrets_other, apart, rows)
    )

    def gathered(sums):
        return lax.all_to_all(sums.reshape(devices, 1, 128), LEAF, 0, 0).reshape(128, 128)

    count = float(leaf_count * HANDS)
    window, reached, instant, sums, same, all_free, all_pot = first(
        (outer, regrets, chance, even, cross, regrets_other, chance_other, even_other)
        + (cross_other,)
        + (nodes, free, pots, own_matrix, near, far),
    )
    values, moved, mine, sums = second(
        gathered(sums), window, reached, instant, same, all_free, all_pot,
        (own_matrix, near), count,
    )
    final = tail(gathered(sums), moved, mine, count)
    return (final[None], values[None])


def solution(mesh):
    split = Mesh(
        mesh.devices.reshape(*LEAF_SIZES, mesh.shape["player"]),
        LEAF + ("player",),
    )
    placed = (
        P("player", LEAF, None),
        P("player", LEAF, None),
        P(LEAF),
        P("player", None),
        P(),
        P(LEAF, None),
        P(LEAF, None),
    )
    return jax.shard_map(
        local,
        mesh=split,
        in_specs=placed,
        out_specs=(P("player", LEAF, None), P("player", LEAF, None)),
        check_vma=False,
    )
```

```python
import functools

import jax
import jax.numpy as jnp
from jax import lax
from jax.experimental import pallas as pl
from jax.experimental.pallas import tpu as pltpu
from jax.sharding import Mesh
from jax.sharding import PartitionSpec as P

LEAF = ("leaf_0", "leaf_1", "leaf_2", "leaf_3")
LEAF_SIZES = (4, 4, 4, 2)
DELTA = 0.05
EPSILON = 1e-06

HANDS = 1326
WIDE = 1408
OWN = 32
SIDE = 16
WINDOW = OWN + 2 * SIDE
BOARD_LEAVES = 8
EDGE = 35
EARLY = 1
LIMIT = 7 << 20
SMALL = 6 << 20
PIECES = 2
BF16 = jnp.bfloat16
F32 = jnp.float32
VMEM = functools.partial(pl.BlockSpec, memory_space=pltpu.VMEM)


def leaf_block():
    index = 0
    for axis, size in zip(LEAF, LEAF_SIZES):
        index = index * size + lax.axis_index(axis)
    return index


def is_odd():
    return lax.axis_index(LEAF[-1]) == 1


def edge_rows(regrets_ref, chance_ref, edge_ref, last):
    at = OWN - 10 if last else 0
    edge_ref[0:10] = regrets_ref[at : at + 10]
    if last:
        edge_ref[10 : 15 - EARLY] = chance_ref[OWN - 5 : OWN - EARLY]
        edge_ref[15 - EARLY : 15] = regrets_ref[OWN + 1 :]
    else:
        edge_ref[10:15] = chance_ref[0:5]
    edge_ref[15:16] = jnp.zeros((1, HANDS), F32)


def forward_kernel(regrets_ref, chance_ref, after_ref, edge_ref):
    odd = is_odd()

    @pl.when(odd)
    def _():
        edge_rows(regrets_ref, chance_ref, edge_ref, False)

    @pl.when(jnp.logical_not(odd))
    def _():
        edge_rows(regrets_ref, chance_ref, edge_ref, True)


def forward(regrets, chance, after):
    return pl.pallas_call(
        forward_kernel,
        out_shape=jax.ShapeDtypeStruct((16, HANDS), F32),
        in_specs=[VMEM()] * 3,
        out_specs=VMEM(),
        compiler_params=pltpu.CompilerParams(vmem_limit_bytes=SMALL),
        name="forward",
    )(regrets, chance, after)


def pack_kernel(
    boards_hbm, pot_hbm, regrets_hbm, chance_hbm, rank_hbm, cards_hbm, parent_hbm,
    regrets_ref, chance_ref, even_ref, cross_ref, cross_other_ref,
    wide_rank_ref, free_ref, holding_ref, pots_ref, nodes_ref,
    board_cards_ref, pot_ref, rank_ref, cards_ref, parent_ref, all_chance_ref, sems,
):
    moves = [
        (boards_hbm, board_cards_ref),
        (rank_hbm, rank_ref),
        (cards_hbm, cards_ref),
        (parent_hbm, parent_ref),
        (regrets_hbm, regrets_ref.at[:OWN]),
        (chance_hbm, all_chance_ref),
        (pot_hbm, pot_ref),
    ]
    copies = [
        pltpu.make_async_copy(source, target, sems.at[at])
        for at, (source, target) in enumerate(moves)
    ]
    for copy in copies:
        copy.start()
    pots_ref[...] = jnp.zeros_like(pots_ref)
    wide_rank_ref[...] = jnp.zeros_like(wide_rank_ref)
    free_ref[...] = jnp.zeros_like(free_ref)
    holding_ref[...] = jnp.zeros_like(holding_ref)
    for copy in copies[:4]:
        copy.wait()
    ranks = rank_ref[...].astype(F32)
    lower, upper = cards_ref[0:1, :], cards_ref[1:2, :]
    rows = []
    for b in range(4):
        taken = jnp.zeros((1, HANDS), jnp.bool_)
        for j in range(5):
            card = board_cards_ref[b, j]
            taken = taken | (lower == card) | (upper == card)
        rows.append(jnp.where(taken, 0.0, 1.0))
    wide_rank_ref[0:4, :HANDS] = ranks
    for b in range(4):
        free_ref[b : b + 1, :HANDS] = rows[b]
    deck = lax.broadcasted_iota(jnp.int32, (128, HANDS), 0)
    holding_ref[:, :HANDS] = jnp.where((deck == lower) | (deck == upper), 1.0, 0.0).astype(BF16)

    leaves = parent_ref.shape[0] * 128
    begin = leaf_block() * OWN - SIDE
    line = (begin + 128) // 128 - 1
    held = [
        parent_ref[pl.ds(jnp.clip(line + j, 0, leaves // 128 - 1), 1), :].astype(F32)
        for j in range(2)
    ]
    held = jnp.broadcast_to(jnp.concatenate(held, axis=1), (8, 256))
    held = pltpu.roll(held, lax.rem((line + 2) * 128 - begin, 256), 1)[0:1, 0:128]
    leaf = begin + lax.broadcasted_iota(jnp.int32, (1, 128), 1)
    held = jnp.where((leaf >= 0) & (leaf < leaves), held, -1.0)
    nodes_ref[...] = jnp.broadcast_to(held, nodes_ref.shape)
    for copy in copies[4:]:
        copy.wait()
    pots_ref[0:1, 0:OWN] = pot_ref[...]
    chance_ref[...] = all_chance_ref[0 : OWN - EARLY]
    regrets_ref[OWN + 1 :] = all_chance_ref[OWN - EARLY :]

    odd = is_odd()

    def ends(ref, last):
        at = OWN - 15 if last else 0
        ref[0:15] = regrets_ref[at : at + 15]
        at = OWN - 10 if last else 0
        ref[15:25] = all_chance_ref[at : at + 10]
        at = 2 if last else 0
        ref[25:27] = ranks[at : at + 2]
        ref[27:28] = rows[at]
        ref[28:29] = rows[at + 1]
        ref[29:30] = jnp.zeros((1, HANDS), F32)
        ref[29:30, 0:128] = pots_ref[0:1, :]
        ref[30:] = jnp.zeros((EDGE - 30, HANDS), F32)

    @pl.when(odd)
    def _():
        ends(even_ref, False)
        ends(cross_ref, True)
        edge_rows(regrets_ref, chance_ref, cross_other_ref, True)

    @pl.when(jnp.logical_not(odd))
    def _():
        ends(even_ref, True)
        ends(cross_ref, False)
        edge_rows(regrets_ref, chance_ref, cross_other_ref, False)

    regrets_ref[OWN : OWN + 1] = jnp.zeros((1, HANDS), F32)
    regrets_ref[OWN : OWN + 1, 0:128] = held


HBM = functools.partial(pl.BlockSpec, memory_space=pltpu.HBM)


def in_hbm(array):
    return pltpu.with_memory_space_constraint(array, pltpu.HBM)


def pack(board_cards, pot_row, regrets, chance, hand_rank, cards, parent):
    shapes = (
        jax.ShapeDtypeStruct((OWN + 1 + EARLY, HANDS), F32),
        jax.ShapeDtypeStruct((OWN - EARLY, HANDS), F32),
        jax.ShapeDtypeStruct((EDGE, HANDS), F32),
        jax.ShapeDtypeStruct((EDGE, HANDS), F32),
        jax.ShapeDtypeStruct((16, HANDS), F32),
        jax.ShapeDtypeStruct((8, WIDE), F32),
        jax.ShapeDtypeStruct((8, WIDE), F32),
        jax.ShapeDtypeStruct((128, WIDE), BF16),
        jax.ShapeDtypeStruct((8, 128), F32),
        jax.ShapeDtypeStruct((8, 128), F32),
    )
    large = (board_cards, pot_row, regrets, chance, hand_rank, cards, parent)
    return pl.pallas_call(
        pack_kernel,
        out_shape=shapes,
        in_specs=[HBM()] * len(large),
        out_specs=[VMEM()] * len(shapes),
        scratch_shapes=[
            pltpu.SMEM((4, 5), jnp.int32),
            pltpu.VMEM((1, OWN), F32),
            pltpu.VMEM((4, HANDS), jnp.int32),
            pltpu.VMEM((2, HANDS), jnp.int32),
            pltpu.VMEM(parent.shape, jnp.int32),
            pltpu.VMEM((OWN, HANDS), F32),
            pltpu.SemaphoreType.DMA((7,)),
        ],
        compiler_params=pltpu.CompilerParams(vmem_limit_bytes=SMALL),
        name="pack",
    )(*map(in_hbm, large))


def sides(even_ref, cross_ref, rows):
    odd = is_odd()
    even, cross = even_ref[rows], cross_ref[rows]
    return jnp.where(odd, even, cross), jnp.where(odd, cross, even)


def fill(rank_ref, apart_ref, column_ref, targets, step):
    ranks = rank_ref[...]
    for t in range(WIDE // 128):
        lanes = slice(t * 128, (t + 1) * 128)
        tile = jnp.concatenate([ranks[:, lanes], jnp.zeros((120, 128), F32)], axis=0)
        column_ref[lanes, :] = tile.T

    @pl.loop(0, WIDE // step)
    def _(i):
        rows = pl.ds(pl.multiple_of(i * step, step), step)
        column = column_ref[rows, :]
        own = [jnp.broadcast_to(column[:, b : b + 1], (step, 128)) for b, _, _ in targets]
        for t in range(WIDE // 128):
            lanes = slice(t * 128, (t + 1) * 128)
            apart = apart_ref[rows, lanes]
            minus = -apart
            for at, (b, matrix_ref, slot) in enumerate(targets):
                gap = (own[at] - rank_ref[b : b + 1, lanes]).astype(BF16)
                matrix_ref[slot, rows, lanes] = jnp.minimum(jnp.maximum(gap, minus), apart)


def build_own_kernel(holding_ref, rank_ref, matrix_ref, apart_ref, column_ref):
    holding = holding_ref[...]
    half = WIDE // 2
    for rows in (slice(0, half), slice(half, WIDE)):
        shared = jnp.dot(holding.T[rows], holding, preferred_element_type=F32)
        apart_ref[rows, :] = (1.0 - jnp.minimum(shared, 1.0)).astype(BF16)
    fill(rank_ref, apart_ref, column_ref, [(b, matrix_ref, b) for b in range(4)], 352)


def outer_boards(mine, other):
    leaf = lax.broadcasted_iota(jnp.int32, mine.shape, 1)
    inside = leaf < WINDOW

    def node_at(row, at):
        return jnp.max(jnp.where(leaf == at, row, -2.0))

    def ends_of(row, node):
        held = inside & (row == node)
        return jnp.min(jnp.where(held, leaf, WINDOW)), jnp.max(jnp.where(held, leaf, -1))

    begin, _ = ends_of(mine, node_at(mine, SIDE))
    begin, _ = ends_of(other, node_at(other, begin))
    _, end = ends_of(mine, node_at(mine, SIDE + OWN - 1))
    _, end = ends_of(other, node_at(other, end))
    return (begin < BOARD_LEAVES) | (end >= WINDOW - BOARD_LEAVES)


def side_ranks(even_ref, cross_ref, rank_ref):
    left, right = sides(even_ref, cross_ref, slice(25, 27))
    rank_ref[...] = jnp.zeros_like(rank_ref)
    rank_ref[0:2, :HANDS] = left
    rank_ref[2:4, :HANDS] = right


def build_near_kernel(
    even_ref, cross_ref, apart_ref, near_ref, token_ref, rank_ref, column_ref
):
    token_ref[...] = jnp.zeros_like(token_ref)
    side_ranks(even_ref, cross_ref, rank_ref)
    fill(rank_ref, apart_ref, column_ref, [(1, near_ref, 0), (2, near_ref, 1)], 128)


def build_far_kernel(
    even_ref, cross_ref, nodes_ref, regrets_other_ref, apart_ref, after_ref,
    far_ref, outer_ref, rank_ref, column_ref,
):
    outer = outer_boards(nodes_ref[0:1, :], regrets_other_ref[OWN : OWN + 1, 0:128])
    outer_ref[...] = jnp.where(outer, jnp.ones_like(outer_ref), jnp.zeros_like(outer_ref))

    @pl.when(outer)
    def _():
        side_ranks(even_ref, cross_ref, rank_ref)
        fill(rank_ref, apart_ref, column_ref, [(0, far_ref, 0), (3, far_ref, 1)], 128)


BUILD_COST = pl.CostEstimate(
    flops=32 * WIDE * WIDE, bytes_accessed=8 * WIDE * WIDE, transcendentals=0
)


def matrices_shape(boards):
    return jax.ShapeDtypeStruct((boards, WIDE, WIDE), BF16)


def build_own(holding, ranks):
    return pl.pallas_call(
        build_own_kernel,
        out_shape=(matrices_shape(4), jax.ShapeDtypeStruct((WIDE, WIDE), BF16)),
        in_specs=[VMEM()] * 2,
        out_specs=[VMEM()] * 2,
        scratch_shapes=[pltpu.VMEM((WIDE, 128), F32)],
        compiler_params=pltpu.CompilerParams(vmem_limit_bytes=LIMIT),
        cost_estimate=BUILD_COST,
        name="build_own",
    )(holding, ranks)


def build_pair(kernel, name, arrays):
    return pl.pallas_call(
        kernel,
        out_shape=(matrices_shape(2), jax.ShapeDtypeStruct((8, 128), F32)),
        in_specs=[VMEM()] * len(arrays),
        out_specs=[VMEM()] * 2,
        scratch_shapes=[pltpu.VMEM((8, WIDE), F32), pltpu.VMEM((WIDE, 128), F32)],
        compiler_params=pltpu.CompilerParams(vmem_limit_bytes=LIMIT),
        cost_estimate=BUILD_COST,
        name=name,
    )(*arrays)


def node_totals(same, values):
    high = values.astype(BF16)
    rest = values - high.astype(F32)
    middle = rest.astype(BF16)
    low = (rest - middle.astype(F32)).astype(BF16)
    parts = jnp.concatenate([high, middle, low], axis=0)
    return jnp.dot(same, parts, preferred_element_type=F32)


def policy_of(same, regrets):
    positive = jnp.maximum(regrets, 0.0) + DELTA
    return positive / node_totals(same, positive)


def split_terms(reach):
    high = reach.astype(BF16).astype(F32)
    return [high, reach - high]


def joined(out, first):
    middle = first + BOARD_LEAVES
    return out[first:middle] + out[middle : middle + BOARD_LEAVES]


def column_of(row):
    return jnp.broadcast_to(row, (128, 128)).T


def same_node(row):
    equal = jnp.where(jnp.broadcast_to(row, (128, 128)) == column_of(row), 1.0, 0.0)
    equal = equal[:WINDOW, :WINDOW]
    return jnp.concatenate([equal, equal, equal], axis=1).astype(BF16)


def board_rows(free, boards):
    return jnp.concatenate(
        [jnp.broadcast_to(free[b : b + 1], (BOARD_LEAVES, WIDE)) for b in boards], axis=0
    )


def first_kernel(
    outer_ref,
    regrets_ref,
    chance_ref,
    even_ref,
    cross_ref,
    regrets_other_ref,
    chance_other_ref,
    even_other_ref,
    cross_other_ref,
    nodes_ref,
    own_free_ref,
    pots_ref,
    own_matrix_ref,
    near_ref,
    far_ref,
    window_ref,
    reached_ref,
    instant_ref,
    sums_ref,
    same_ref,
    free_ref,
    pot_ref,
    policy_ref,
    terms_ref,
    values_ref,
):
    left, right = sides(even_ref, cross_ref, slice(0, 30))
    left_other, right_other = sides(even_other_ref, cross_other_ref, slice(0, 15))
    same_ref[0] = same_node(nodes_ref[0:1, :])
    same_ref[1] = same_node(regrets_other_ref[OWN : OWN + 1, 0:128])
    free_ref[...] = jnp.zeros_like(free_ref)
    free_ref[0:2, :HANDS] = left[27:29]
    free_ref[2:6] = own_free_ref[0:4]
    free_ref[6:8, :HANDS] = right[27:29]
    pot_ref[0:SIDE] = column_of(left[29:30, 0:128])[SIDE:OWN]
    pot_ref[SIDE : SIDE + OWN] = column_of(pots_ref[0:1, :])[:OWN]
    pot_ref[SIDE + OWN :] = column_of(right[29:30, 0:128])[:SIDE]
    window_ref[...] = jnp.zeros_like(window_ref)
    reached_ref[...] = jnp.zeros_like(reached_ref)
    policy_ref[...] = jnp.zeros_like(policy_ref)
    low, high = SIDE, SIDE + OWN
    window_ref[0, low - 15 : low, :HANDS] = left[0:15]
    window_ref[0, low:high, :HANDS] = regrets_ref[:OWN]
    window_ref[0, high : high + 15, :HANDS] = right[0:15]
    policy_ref[0, low - 10 : low, :HANDS] = left[15:25]
    policy_ref[0, low : high - EARLY, :HANDS] = chance_ref[...]
    policy_ref[0, high - EARLY : high, :HANDS] = regrets_ref[OWN + 1 :]
    policy_ref[0, high : high + 10, :HANDS] = right[15:25]
    window_ref[1, low - 10 : low, :HANDS] = left_other[0:10]
    window_ref[1, low:high, :HANDS] = regrets_other_ref[:OWN]
    window_ref[1, high : high + 10, :HANDS] = right_other[0:10]
    reached_ref[low - 5 : low, :HANDS] = left_other[10:15]
    reached_ref[low : high - EARLY, :HANDS] = chance_other_ref[...]
    reached_ref[high - EARLY : high, :HANDS] = regrets_other_ref[OWN + 1 :]
    reached_ref[high : high + 5, :HANDS] = right_other[10:15]
    free = board_rows(free_ref, range(8))
    reached_ref[...] = reached_ref[...] * free
    terms = []
    for p in range(2):
        chance = policy_ref[0] * free if p == 0 else reached_ref[...]
        policy = policy_of(same_ref[p], window_ref[p])
        policy_ref[p] = policy
        terms.append(split_terms(chance * policy))
    for b in range(8):
        rows = slice(b * BOARD_LEAVES, (b + 1) * BOARD_LEAVES)
        block = jnp.concatenate([term[rows] for player in terms for term in player], axis=0)
        terms_ref[b] = block.astype(BF16)

    def board(b, matrix):
        out = jnp.dot(terms_ref[b], matrix, preferred_element_type=F32)
        rows = slice(b * BOARD_LEAVES, (b + 1) * BOARD_LEAVES)
        factor = pot_ref[rows, 0:1] * (-1.0 / HANDS)
        free = free_ref[b : b + 1, :]
        values_ref[1, rows, :] = joined(out, 0) * factor * free
        values_ref[0, rows, :] = joined(out, PIECES * BOARD_LEAVES) * factor * free

    for b in range(4):
        board(b + 2, own_matrix_ref[b])
    board(1, near_ref[0])
    board(6, near_ref[1])

    outer = jnp.max(outer_ref[0:1, :]) > 0.5

    @pl.when(outer)
    def _():
        board(0, far_ref[0])
        board(7, far_ref[1])

    @pl.when(jnp.logical_not(outer))
    def _():
        for p in range(2):
            for b in (0, 7):
                rows = slice(b * BOARD_LEAVES, (b + 1) * BOARD_LEAVES)
                values_ref[p, rows, :] = jnp.zeros((BOARD_LEAVES, WIDE), F32)

    sums = []
    for p in range(2):
        values = values_ref[p]
        instant = values - node_totals(same_ref[p], policy_ref[p] * values)
        instant_ref[p] = instant
        mine = instant[SIDE : SIDE + OWN]
        sums.append(jnp.sum(mine * mine))
    lane = lax.broadcasted_iota(jnp.int32, sums_ref.shape, 1)
    sums_ref[...] = jnp.where(lane == 0, sums[0], jnp.where(lane == 1, sums[1], 0.0))


def first(arrays):
    shapes = (
        jax.ShapeDtypeStruct((2, WINDOW, WIDE), F32),
        jax.ShapeDtypeStruct((WINDOW, WIDE), F32),
        jax.ShapeDtypeStruct((2, WINDOW, WIDE), F32),
        jax.ShapeDtypeStruct((128, 128), F32),
        jax.ShapeDtypeStruct((2, WINDOW, 3 * WINDOW), BF16),
        jax.ShapeDtypeStruct((8, WIDE), F32),
        jax.ShapeDtypeStruct((WINDOW, 128), F32),
    )
    return pl.pallas_call(
        first_kernel,
        out_shape=shapes,
        in_specs=[VMEM()] * len(arrays),
        out_specs=[VMEM()] * len(shapes),
        scratch_shapes=[
            pltpu.VMEM((2, WINDOW, WIDE), F32),
            pltpu.VMEM((8, 2 * PIECES * BOARD_LEAVES, WIDE), BF16),
            pltpu.VMEM((2, WINDOW, WIDE), F32),
        ],
        compiler_params=pltpu.CompilerParams(vmem_limit_bytes=LIMIT),
        name="first",
    )(*arrays)


def second_kernel(
    gathered_ref,
    window_ref,
    reached_ref,
    instant_ref,
    same_ref,
    free_ref,
    pot_ref,
    own_matrix_ref,
    near_ref,
    out_values_ref,
    moved_ref,
    mine_ref,
    sums_ref,
    policy_ref,
    terms_ref,
    values_ref,
    *,
    count,
):
    values_ref[...] = jnp.zeros_like(values_ref)
    sums = jnp.sum(gathered_ref[...], axis=0, keepdims=True)
    scale = jnp.sqrt(sums / count + EPSILON)
    moved = window_ref[0] + instant_ref[0] / scale[:, 0:1]
    moved_ref[...] = moved[SIDE : SIDE + OWN]
    policy_ref[...] = policy_of(same_ref[0], moved)
    other = window_ref[1] + instant_ref[1] / scale[:, 1:2]
    terms = split_terms(reached_ref[...] * policy_of(same_ref[1], other))
    for b in range(8):
        rows = slice(b * BOARD_LEAVES, (b + 1) * BOARD_LEAVES)
        block = jnp.concatenate([term[rows] for term in terms], axis=0)
        terms_ref[b] = block.astype(BF16)

    def board(b, matrix):
        out = jnp.dot(terms_ref[b], matrix, preferred_element_type=F32)
        rows = slice(b * BOARD_LEAVES, (b + 1) * BOARD_LEAVES)
        factor = pot_ref[rows, 0:1] * (-1.0 / HANDS)
        values_ref[rows, :] = joined(out, 0) * factor * free_ref[b : b + 1, :]

    for b in range(4):
        board(b + 2, own_matrix_ref[b])
    board(1, near_ref[0])
    board(6, near_ref[1])

    values = values_ref[...]
    instant = values - node_totals(same_ref[0], policy_ref[...] * values)
    mine = instant[SIDE : SIDE + OWN]
    mine_ref[...] = mine
    out_values_ref[...] = values[SIDE : SIDE + OWN, :HANDS]
    lane = lax.broadcasted_iota(jnp.int32, sums_ref.shape, 1)
    sums_ref[...] = jnp.where(lane == 0, jnp.sum(mine * mine), 0.0)


def second(gathered, window, reached, instant, same, free, pot, matrices, count):
    shapes = (
        jax.ShapeDtypeStruct((OWN, HANDS), F32),
        jax.ShapeDtypeStruct((OWN, WIDE), F32),
        jax.ShapeDtypeStruct((OWN, WIDE), F32),
        jax.ShapeDtypeStruct((128, 128), F32),
    )
    arrays = (gathered, window, reached, instant, same, free, pot) + matrices
    return pl.pallas_call(
        functools.partial(second_kernel, count=count),
        out_shape=shapes,
        in_specs=[VMEM()] * len(arrays),
        out_specs=[VMEM()] * len(shapes),
        scratch_shapes=[
            pltpu.VMEM((WINDOW, WIDE), F32),
            pltpu.VMEM((8, PIECES * BOARD_LEAVES, WIDE), BF16),
            pltpu.VMEM((WINDOW, WIDE), F32),
        ],
        compiler_params=pltpu.CompilerParams(vmem_limit_bytes=LIMIT),
        name="second",
    )(*arrays)


def tail_kernel(gathered_ref, moved_ref, mine_ref, out_ref, *, count):
    sums = jnp.sum(gathered_ref[...], axis=0, keepdims=True)
    scale = jnp.sqrt(sums / count + EPSILON)[:, 0:1]
    out_ref[...] = (moved_ref[...] + mine_ref[...] / scale)[:, :HANDS]


def tail(gathered, moved, mine, count):
    return pl.pallas_call(
        functools.partial(tail_kernel, count=count),
        out_shape=jax.ShapeDtypeStruct((OWN, HANDS), F32),
        in_specs=[VMEM()] * 3,
        out_specs=VMEM(),
        compiler_params=pltpu.CompilerParams(vmem_limit_bytes=SMALL),
        name="tail",
    )(gathered, moved, mine)


def local(chance_reach, regrets_start, pot, parent, hand_cards, board_cards, hand_rank):
    devices = lax.axis_size(LEAF)
    leaf_count = parent.shape[1]

    even_pairs = [(i, i ^ 1) for i in range(devices)]
    cross_pairs = [(i, i + 1) for i in range(1, devices - 1, 2)]
    cross_pairs = cross_pairs + [(j, i) for i, j in cross_pairs]

    diagonal = [(2 * i + p, 2 * j + 1 - p) for i, j in cross_pairs for p in range(2)]

    regrets, chance, even, cross, cross_other, ranks, free, holding, pots, nodes = pack(
        board_cards, pot[None], regrets_start[0], chance_reach[0], hand_rank,
        hand_cards.T, parent.reshape(-1, 128),
    )
    cross = lax.ppermute(cross, LEAF, cross_pairs)
    even = lax.ppermute(even, LEAF, even_pairs)
    regrets_other = lax.ppermute(regrets, "player", [(0, 1), (1, 0)])
    chance_other = lax.ppermute(chance, "player", [(0, 1), (1, 0)])
    cross_other = lax.ppermute(cross_other, LEAF + ("player",), diagonal)

    own_matrix, apart = build_own(holding, ranks)
    near, built = build_pair(build_near_kernel, "build_near", (even, cross, apart))
    rows = forward(regrets_other, chance_other, built)
    even_other = lax.ppermute(rows, LEAF, even_pairs)
    far, outer = build_pair(
        build_far_kernel, "build_far", (even, cross, nodes, regrets_other, apart, rows)
    )

    def gathered(sums):
        return lax.all_to_all(sums.reshape(devices, 1, 128), LEAF, 0, 0).reshape(128, 128)

    count = float(leaf_count * HANDS)
    window, reached, instant, sums, same, all_free, all_pot = first(
        (outer, regrets, chance, even, cross, regrets_other, chance_other, even_other)
        + (cross_other,)
        + (nodes, free, pots, own_matrix, near, far),
    )
    values, moved, mine, sums = second(
        gathered(sums), window, reached, instant, same, all_free, all_pot,
        (own_matrix, near), count,
    )
    final = tail(gathered(sums), moved, mine, count)
    return (final[None], values[None])


def solution(mesh):
    split = Mesh(
        mesh.devices.reshape(*LEAF_SIZES, mesh.shape["player"]),
        LEAF + ("player",),
    )
    placed = (
        P("player", LEAF, None),
        P("player", LEAF, None),
        P(LEAF),
        P("player", None),
        P(),
        P(LEAF, None),
        P(LEAF, None),
    )
    return jax.shard_map(
        local,
        mesh=split,
        in_specs=placed,
        out_specs=(P("player", LEAF, None), P("player", LEAF, None)),
        check_vma=False,
    )
```

```python
import functools

import jax
import jax.numpy as jnp
from jax import lax
from jax.experimental import pallas as pl
from jax.experimental.pallas import tpu as pltpu
from jax.sharding import Mesh
from jax.sharding import PartitionSpec as P

LEAF = ("leaf_0", "leaf_1", "leaf_2", "leaf_3")
LEAF_SIZES = (4, 4, 4, 2)
DELTA = 0.05
EPSILON = 1e-06

HANDS = 1326
WIDE = 1408
OWN = 32
SIDE = 16
WINDOW = OWN + 2 * SIDE
BOARD_LEAVES = 8
EDGE = 31
EARLY = 2
LIMIT = 7 << 20
SMALL = 6 << 20
PIECES = 2
BF16 = jnp.bfloat16
F32 = jnp.float32
VMEM = functools.partial(pl.BlockSpec, memory_space=pltpu.VMEM)


def leaf_block():
    index = 0
    for axis, size in zip(LEAF, LEAF_SIZES):
        index = index * size + lax.axis_index(axis)
    return index


def is_odd():
    return lax.axis_index(LEAF[-1]) == 1


def edge_rows(regrets_ref, chance_ref, edge_ref, last):
    at = OWN - 10 if last else 0
    edge_ref[0:10] = regrets_ref[at : at + 10]
    if last:
        edge_ref[10 : 15 - EARLY] = chance_ref[OWN - 5 : OWN - EARLY]
        edge_ref[15 - EARLY : 15] = regrets_ref[OWN + 1 :]
    else:
        edge_ref[10:15] = chance_ref[0:5]


def forward_kernel(regrets_ref, chance_ref, after_ref, edge_ref):
    odd = is_odd()

    @pl.when(odd)
    def _():
        edge_rows(regrets_ref, chance_ref, edge_ref, False)

    @pl.when(jnp.logical_not(odd))
    def _():
        edge_rows(regrets_ref, chance_ref, edge_ref, True)


def forward(regrets, chance, after):
    return pl.pallas_call(
        forward_kernel,
        out_shape=jax.ShapeDtypeStruct((15, HANDS), F32),
        in_specs=[VMEM()] * 3,
        out_specs=VMEM(),
        compiler_params=pltpu.CompilerParams(vmem_limit_bytes=SMALL),
        name="forward",
    )(regrets, chance, after)


def pack_kernel(
    boards_hbm, pot_hbm, regrets_hbm, chance_hbm, rank_hbm, cards_hbm, parent_hbm,
    regrets_ref, chance_ref, even_ref, cross_ref, cross_other_ref,
    wide_rank_ref, free_ref, holding_ref, pots_ref, nodes_ref,
    board_cards_ref, pot_ref, rank_ref, cards_ref, parent_ref, all_chance_ref, sems,
):
    moves = [
        (boards_hbm, board_cards_ref),
        (rank_hbm, rank_ref),
        (cards_hbm, cards_ref),
        (parent_hbm, parent_ref),
        (regrets_hbm, regrets_ref.at[:OWN]),
        (chance_hbm, all_chance_ref),
        (pot_hbm, pot_ref),
    ]
    copies = [
        pltpu.make_async_copy(source, target, sems.at[at])
        for at, (source, target) in enumerate(moves)
    ]
    for copy in copies:
        copy.start()
    pots_ref[...] = jnp.zeros_like(pots_ref)
    wide_rank_ref[...] = jnp.zeros_like(wide_rank_ref)
    free_ref[...] = jnp.zeros_like(free_ref)
    holding_ref[...] = jnp.zeros_like(holding_ref)
    for copy in copies[:4]:
        copy.wait()
    ranks = rank_ref[...].astype(F32)
    lower, upper = cards_ref[0:1, :], cards_ref[1:2, :]
    rows = []
    for b in range(4):
        taken = jnp.zeros((1, HANDS), jnp.bool_)
        for j in range(5):
            card = board_cards_ref[b, j]
            taken = taken | (lower == card) | (upper == card)
        rows.append(jnp.where(taken, 0.0, 1.0))
    wide_rank_ref[0:4, :HANDS] = ranks
    for b in range(4):
        free_ref[b : b + 1, :HANDS] = rows[b]
    deck = lax.broadcasted_iota(jnp.int32, (128, HANDS), 0)
    holding_ref[:, :HANDS] = jnp.where((deck == lower) | (deck == upper), 1.0, 0.0).astype(BF16)

    leaves = parent_ref.shape[0] * 128
    begin = leaf_block() * OWN - SIDE
    line = (begin + 128) // 128 - 1
    held = [
        parent_ref[pl.ds(jnp.clip(line + j, 0, leaves // 128 - 1), 1), :].astype(F32)
        for j in range(2)
    ]
    held = jnp.broadcast_to(jnp.concatenate(held, axis=1), (8, 256))
    held = pltpu.roll(held, lax.rem((line + 2) * 128 - begin, 256), 1)[0:1, 0:128]
    leaf = begin + lax.broadcasted_iota(jnp.int32, (1, 128), 1)
    held = jnp.where((leaf >= 0) & (leaf < leaves), held, -1.0)
    nodes_ref[...] = jnp.broadcast_to(held, nodes_ref.shape)
    for copy in copies[4:]:
        copy.wait()
    pots_ref[0:1, 0:OWN] = pot_ref[...]
    chance_ref[...] = all_chance_ref[0 : OWN - EARLY]
    regrets_ref[OWN + 1 :] = all_chance_ref[OWN - EARLY :]

    odd = is_odd()

    def ends(ref, last):
        at = OWN - 15 if last else 0
        ref[0:15] = regrets_ref[at : at + 15]
        at = OWN - 10 if last else 0
        ref[15:25] = all_chance_ref[at : at + 10]
        at = 2 if last else 0
        ref[25:27] = ranks[at : at + 2]
        ref[27:28] = rows[at]
        ref[28:29] = rows[at + 1]
        ref[29:30] = jnp.zeros((1, HANDS), F32)
        ref[29:30, 0:128] = pots_ref[0:1, :]
        ref[30:] = jnp.zeros((EDGE - 30, HANDS), F32)

    @pl.when(odd)
    def _():
        ends(even_ref, False)
        ends(cross_ref, True)
        edge_rows(regrets_ref, chance_ref, cross_other_ref, True)

    @pl.when(jnp.logical_not(odd))
    def _():
        ends(even_ref, True)
        ends(cross_ref, False)
        edge_rows(regrets_ref, chance_ref, cross_other_ref, False)

    regrets_ref[OWN : OWN + 1] = jnp.zeros((1, HANDS), F32)
    regrets_ref[OWN : OWN + 1, 0:128] = held


HBM = functools.partial(pl.BlockSpec, memory_space=pltpu.HBM)


def in_hbm(array):
    return pltpu.with_memory_space_constraint(array, pltpu.HBM)


def pack(board_cards, pot_row, regrets, chance, hand_rank, cards, parent):
    shapes = (
        jax.ShapeDtypeStruct((OWN + 1 + EARLY, HANDS), F32),
        jax.ShapeDtypeStruct((OWN - EARLY, HANDS), F32),
        jax.ShapeDtypeStruct((EDGE, HANDS), F32),
        jax.ShapeDtypeStruct((EDGE, HANDS), F32),
        jax.ShapeDtypeStruct((15, HANDS), F32),
        jax.ShapeDtypeStruct((8, WIDE), F32),
        jax.ShapeDtypeStruct((8, WIDE), F32),
        jax.ShapeDtypeStruct((128, WIDE), BF16),
        jax.ShapeDtypeStruct((8, 128), F32),
        jax.ShapeDtypeStruct((8, 128), F32),
    )
    large = (board_cards, pot_row, regrets, chance, hand_rank, cards, parent)
    return pl.pallas_call(
        pack_kernel,
        out_shape=shapes,
        in_specs=[HBM()] * len(large),
        out_specs=[VMEM()] * len(shapes),
        scratch_shapes=[
            pltpu.SMEM((4, 5), jnp.int32),
            pltpu.VMEM((1, OWN), F32),
            pltpu.VMEM((4, HANDS), jnp.int32),
            pltpu.VMEM((2, HANDS), jnp.int32),
            pltpu.VMEM(parent.shape, jnp.int32),
            pltpu.VMEM((OWN, HANDS), F32),
            pltpu.SemaphoreType.DMA((7,)),
        ],
        compiler_params=pltpu.CompilerParams(vmem_limit_bytes=SMALL),
        name="pack",
    )(*map(in_hbm, large))


def sides(even_ref, cross_ref, rows):
    odd = is_odd()
    even, cross = even_ref[rows], cross_ref[rows]
    return jnp.where(odd, even, cross), jnp.where(odd, cross, even)


def fill(rank_ref, apart_ref, column_ref, targets, step):
    ranks = rank_ref[...]
    for t in range(WIDE // 128):
        lanes = slice(t * 128, (t + 1) * 128)
        tile = jnp.concatenate([ranks[:, lanes], jnp.zeros((120, 128), F32)], axis=0)
        column_ref[lanes, :] = tile.T

    @pl.loop(0, WIDE // step)
    def _(i):
        rows = pl.ds(pl.multiple_of(i * step, step), step)
        column = column_ref[rows, :]
        own = [jnp.broadcast_to(column[:, b : b + 1], (step, 128)) for b, _, _ in targets]
        for t in range(WIDE // 128):
            lanes = slice(t * 128, (t + 1) * 128)
            apart = apart_ref[rows, lanes]
            minus = -apart
            for at, (b, matrix_ref, slot) in enumerate(targets):
                gap = (own[at] - rank_ref[b : b + 1, lanes]).astype(BF16)
                matrix_ref[slot, rows, lanes] = jnp.minimum(jnp.maximum(gap, minus), apart)


def build_own_kernel(holding_ref, rank_ref, matrix_ref, apart_ref, column_ref):
    holding = holding_ref[...]
    half = WIDE // 2
    for rows in (slice(0, half), slice(half, WIDE)):
        shared = jnp.dot(holding.T[rows], holding, preferred_element_type=F32)
        apart_ref[rows, :] = (1.0 - jnp.minimum(shared, 1.0)).astype(BF16)
    fill(rank_ref, apart_ref, column_ref, [(b, matrix_ref, b) for b in range(4)], 352)


def outer_boards(mine, other):
    leaf = lax.broadcasted_iota(jnp.int32, mine.shape, 1)
    inside = leaf < WINDOW

    def node_at(row, at):
        return jnp.max(jnp.where(leaf == at, row, -2.0))

    def ends_of(row, node):
        held = inside & (row == node)
        return jnp.min(jnp.where(held, leaf, WINDOW)), jnp.max(jnp.where(held, leaf, -1))

    begin, _ = ends_of(mine, node_at(mine, SIDE))
    begin, _ = ends_of(other, node_at(other, begin))
    _, end = ends_of(mine, node_at(mine, SIDE + OWN - 1))
    _, end = ends_of(other, node_at(other, end))
    return (begin < BOARD_LEAVES) | (end >= WINDOW - BOARD_LEAVES)


def side_ranks(even_ref, cross_ref, rank_ref):
    left, right = sides(even_ref, cross_ref, slice(25, 27))
    rank_ref[...] = jnp.zeros_like(rank_ref)
    rank_ref[0:2, :HANDS] = left
    rank_ref[2:4, :HANDS] = right


def build_near_kernel(
    even_ref, cross_ref, apart_ref, near_ref, token_ref, rank_ref, column_ref
):
    token_ref[...] = jnp.zeros_like(token_ref)
    side_ranks(even_ref, cross_ref, rank_ref)
    fill(rank_ref, apart_ref, column_ref, [(1, near_ref, 0), (2, near_ref, 1)], 128)


def build_far_kernel(
    even_ref, cross_ref, nodes_ref, regrets_other_ref, apart_ref, after_ref,
    far_ref, outer_ref, rank_ref, column_ref,
):
    outer = outer_boards(nodes_ref[0:1, :], regrets_other_ref[OWN : OWN + 1, 0:128])
    outer_ref[...] = jnp.where(outer, jnp.ones_like(outer_ref), jnp.zeros_like(outer_ref))

    @pl.when(outer)
    def _():
        side_ranks(even_ref, cross_ref, rank_ref)
        fill(rank_ref, apart_ref, column_ref, [(0, far_ref, 0), (3, far_ref, 1)], 128)


BUILD_COST = pl.CostEstimate(
    flops=32 * WIDE * WIDE, bytes_accessed=8 * WIDE * WIDE, transcendentals=0
)


def matrices_shape(boards):
    return jax.ShapeDtypeStruct((boards, WIDE, WIDE), BF16)


def build_own(holding, ranks):
    return pl.pallas_call(
        build_own_kernel,
        out_shape=(matrices_shape(4), jax.ShapeDtypeStruct((WIDE, WIDE), BF16)),
        in_specs=[VMEM()] * 2,
        out_specs=[VMEM()] * 2,
        scratch_shapes=[pltpu.VMEM((WIDE, 128), F32)],
        compiler_params=pltpu.CompilerParams(vmem_limit_bytes=LIMIT),
        cost_estimate=BUILD_COST,
        name="build_own",
    )(holding, ranks)


def build_pair(kernel, name, arrays):
    return pl.pallas_call(
        kernel,
        out_shape=(matrices_shape(2), jax.ShapeDtypeStruct((8, 128), F32)),
        in_specs=[VMEM()] * len(arrays),
        out_specs=[VMEM()] * 2,
        scratch_shapes=[pltpu.VMEM((8, WIDE), F32), pltpu.VMEM((WIDE, 128), F32)],
        compiler_params=pltpu.CompilerParams(vmem_limit_bytes=LIMIT),
        cost_estimate=BUILD_COST,
        name=name,
    )(*arrays)


def node_totals(same, values):
    high = values.astype(BF16)
    rest = values - high.astype(F32)
    parts = jnp.concatenate([high, rest.astype(BF16)], axis=0)
    return jnp.dot(same, parts, preferred_element_type=F32)


def policy_of(same, regrets):
    positive = jnp.maximum(regrets, 0.0) + DELTA
    return positive / node_totals(same, positive)


def split_terms(reach):
    high = reach.astype(BF16).astype(F32)
    return [high, reach - high]


def joined(out, first):
    middle = first + BOARD_LEAVES
    return out[first:middle] + out[middle : middle + BOARD_LEAVES]


def column_of(row):
    return jnp.broadcast_to(row, (128, 128)).T


def same_node(row):
    equal = jnp.where(jnp.broadcast_to(row, (128, 128)) == column_of(row), 1.0, 0.0)
    equal = equal[:WINDOW, :WINDOW]
    return jnp.concatenate([equal, equal], axis=1).astype(BF16)


def board_rows(free, boards):
    return jnp.concatenate(
        [jnp.broadcast_to(free[b : b + 1], (BOARD_LEAVES, WIDE)) for b in boards], axis=0
    )


def first_kernel(
    outer_ref,
    regrets_ref,
    chance_ref,
    even_ref,
    cross_ref,
    regrets_other_ref,
    chance_other_ref,
    even_other_ref,
    cross_other_ref,
    nodes_ref,
    own_free_ref,
    pots_ref,
    own_matrix_ref,
    near_ref,
    far_ref,
    window_ref,
    reached_ref,
    instant_ref,
    sums_ref,
    same_ref,
    free_ref,
    pot_ref,
    policy_ref,
    terms_ref,
    values_ref,
):
    left, right = sides(even_ref, cross_ref, slice(0, 30))
    left_other, right_other = sides(even_other_ref, cross_other_ref, slice(0, 15))
    same_ref[0] = same_node(nodes_ref[0:1, :])
    same_ref[1] = same_node(regrets_other_ref[OWN : OWN + 1, 0:128])
    free_ref[...] = jnp.zeros_like(free_ref)
    free_ref[0:2, :HANDS] = left[27:29]
    free_ref[2:6] = own_free_ref[0:4]
    free_ref[6:8, :HANDS] = right[27:29]
    pot_ref[0:SIDE] = column_of(left[29:30, 0:128])[SIDE:OWN]
    pot_ref[SIDE : SIDE + OWN] = column_of(pots_ref[0:1, :])[:OWN]
    pot_ref[SIDE + OWN :] = column_of(right[29:30, 0:128])[:SIDE]
    window_ref[...] = jnp.zeros_like(window_ref)
    reached_ref[...] = jnp.zeros_like(reached_ref)
    policy_ref[...] = jnp.zeros_like(policy_ref)
    low, high = SIDE, SIDE + OWN
    window_ref[0, low - 15 : low, :HANDS] = left[0:15]
    window_ref[0, low:high, :HANDS] = regrets_ref[:OWN]
    window_ref[0, high : high + 15, :HANDS] = right[0:15]
    policy_ref[0, low - 10 : low, :HANDS] = left[15:25]
    policy_ref[0, low : high - EARLY, :HANDS] = chance_ref[...]
    policy_ref[0, high - EARLY : high, :HANDS] = regrets_ref[OWN + 1 :]
    policy_ref[0, high : high + 10, :HANDS] = right[15:25]
    window_ref[1, low - 10 : low, :HANDS] = left_other[0:10]
    window_ref[1, low:high, :HANDS] = regrets_other_ref[:OWN]
    window_ref[1, high : high + 10, :HANDS] = right_other[0:10]
    reached_ref[low - 5 : low, :HANDS] = left_other[10:15]
    reached_ref[low : high - EARLY, :HANDS] = chance_other_ref[...]
    reached_ref[high - EARLY : high, :HANDS] = regrets_other_ref[OWN + 1 :]
    reached_ref[high : high + 5, :HANDS] = right_other[10:15]
    free = board_rows(free_ref, range(8))
    reached_ref[...] = reached_ref[...] * free
    terms = []
    for p in range(2):
        chance = policy_ref[0] * free if p == 0 else reached_ref[...]
        policy = policy_of(same_ref[p], window_ref[p])
        policy_ref[p] = policy
        terms.append(split_terms(chance * policy))
    for b in range(8):
        rows = slice(b * BOARD_LEAVES, (b + 1) * BOARD_LEAVES)
        block = jnp.concatenate([term[rows] for player in terms for term in player], axis=0)
        terms_ref[b] = block.astype(BF16)

    def board(b, matrix):
        out = jnp.dot(terms_ref[b], matrix, preferred_element_type=F32)
        rows = slice(b * BOARD_LEAVES, (b + 1) * BOARD_LEAVES)
        factor = pot_ref[rows, 0:1] * (-1.0 / HANDS)
        free = free_ref[b : b + 1, :]
        values_ref[1, rows, :] = joined(out, 0) * factor * free
        values_ref[0, rows, :] = joined(out, PIECES * BOARD_LEAVES) * factor * free

    for b in range(4):
        board(b + 2, own_matrix_ref[b])
    board(1, near_ref[0])
    board(6, near_ref[1])

    outer = jnp.max(outer_ref[0:1, :]) > 0.5

    @pl.when(outer)
    def _():
        board(0, far_ref[0])
        board(7, far_ref[1])

    @pl.when(jnp.logical_not(outer))
    def _():
        for p in range(2):
            for b in (0, 7):
                rows = slice(b * BOARD_LEAVES, (b + 1) * BOARD_LEAVES)
                values_ref[p, rows, :] = jnp.zeros((BOARD_LEAVES, WIDE), F32)

    sums = []
    for p in range(2):
        values = values_ref[p]
        instant = values - node_totals(same_ref[p], policy_ref[p] * values)
        instant_ref[p] = instant
        mine = instant[SIDE : SIDE + OWN]
        sums.append(jnp.sum(mine * mine))
    lane = lax.broadcasted_iota(jnp.int32, sums_ref.shape, 1)
    sums_ref[...] = jnp.where(lane == 0, sums[0], jnp.where(lane == 1, sums[1], 0.0))


def first(arrays):
    shapes = (
        jax.ShapeDtypeStruct((2, WINDOW, WIDE), F32),
        jax.ShapeDtypeStruct((WINDOW, WIDE), F32),
        jax.ShapeDtypeStruct((2, WINDOW, WIDE), F32),
        jax.ShapeDtypeStruct((128, 128), F32),
        jax.ShapeDtypeStruct((2, WINDOW, 2 * WINDOW), BF16),
        jax.ShapeDtypeStruct((8, WIDE), F32),
        jax.ShapeDtypeStruct((WINDOW, 128), F32),
    )
    return pl.pallas_call(
        first_kernel,
        out_shape=shapes,
        in_specs=[VMEM()] * len(arrays),
        out_specs=[VMEM()] * len(shapes),
        scratch_shapes=[
            pltpu.VMEM((2, WINDOW, WIDE), F32),
            pltpu.VMEM((8, 2 * PIECES * BOARD_LEAVES, WIDE), BF16),
            pltpu.VMEM((2, WINDOW, WIDE), F32),
        ],
        compiler_params=pltpu.CompilerParams(vmem_limit_bytes=LIMIT),
        name="first",
    )(*arrays)


def second_kernel(
    gathered_ref,
    window_ref,
    reached_ref,
    instant_ref,
    same_ref,
    free_ref,
    pot_ref,
    own_matrix_ref,
    near_ref,
    out_values_ref,
    moved_ref,
    mine_ref,
    sums_ref,
    policy_ref,
    terms_ref,
    values_ref,
    *,
    count,
):
    values_ref[...] = jnp.zeros_like(values_ref)
    sums = jnp.sum(gathered_ref[...], axis=0, keepdims=True)
    scale = jnp.sqrt(sums / count + EPSILON)
    moved = window_ref[0] + instant_ref[0] / scale[:, 0:1]
    moved_ref[...] = moved[SIDE : SIDE + OWN]
    policy_ref[...] = policy_of(same_ref[0], moved)
    other = window_ref[1] + instant_ref[1] / scale[:, 1:2]
    terms = split_terms(reached_ref[...] * policy_of(same_ref[1], other))
    for b in range(8):
        rows = slice(b * BOARD_LEAVES, (b + 1) * BOARD_LEAVES)
        block = jnp.concatenate([term[rows] for term in terms], axis=0)
        terms_ref[b] = block.astype(BF16)

    def board(b, matrix):
        out = jnp.dot(terms_ref[b], matrix, preferred_element_type=F32)
        rows = slice(b * BOARD_LEAVES, (b + 1) * BOARD_LEAVES)
        factor = pot_ref[rows, 0:1] * (-1.0 / HANDS)
        values_ref[rows, :] = joined(out, 0) * factor * free_ref[b : b + 1, :]

    for b in range(4):
        board(b + 2, own_matrix_ref[b])
    board(1, near_ref[0])
    board(6, near_ref[1])

    values = values_ref[...]
    instant = values - node_totals(same_ref[0], policy_ref[...] * values)
    mine = instant[SIDE : SIDE + OWN]
    mine_ref[...] = mine
    out_values_ref[...] = values[SIDE : SIDE + OWN, :HANDS]
    lane = lax.broadcasted_iota(jnp.int32, sums_ref.shape, 1)
    sums_ref[...] = jnp.where(lane == 0, jnp.sum(mine * mine), 0.0)


def second(gathered, window, reached, instant, same, free, pot, matrices, count):
    shapes = (
        jax.ShapeDtypeStruct((OWN, HANDS), F32),
        jax.ShapeDtypeStruct((OWN, WIDE), F32),
        jax.ShapeDtypeStruct((OWN, WIDE), F32),
        jax.ShapeDtypeStruct((128, 128), F32),
    )
    arrays = (gathered, window, reached, instant, same, free, pot) + matrices
    return pl.pallas_call(
        functools.partial(second_kernel, count=count),
        out_shape=shapes,
        in_specs=[VMEM()] * len(arrays),
        out_specs=[VMEM()] * len(shapes),
        scratch_shapes=[
            pltpu.VMEM((WINDOW, WIDE), F32),
            pltpu.VMEM((8, PIECES * BOARD_LEAVES, WIDE), BF16),
            pltpu.VMEM((WINDOW, WIDE), F32),
        ],
        compiler_params=pltpu.CompilerParams(vmem_limit_bytes=LIMIT),
        name="second",
    )(*arrays)


def tail_kernel(gathered_ref, moved_ref, mine_ref, out_ref, *, count):
    sums = jnp.sum(gathered_ref[...], axis=0, keepdims=True)
    scale = jnp.sqrt(sums / count + EPSILON)[:, 0:1]
    out_ref[...] = (moved_ref[...] + mine_ref[...] / scale)[:, :HANDS]


def tail(gathered, moved, mine, count):
    return pl.pallas_call(
        functools.partial(tail_kernel, count=count),
        out_shape=jax.ShapeDtypeStruct((OWN, HANDS), F32),
        in_specs=[VMEM()] * 3,
        out_specs=VMEM(),
        compiler_params=pltpu.CompilerParams(vmem_limit_bytes=SMALL),
        name="tail",
    )(gathered, moved, mine)


def local(chance_reach, regrets_start, pot, parent, hand_cards, board_cards, hand_rank):
    devices = lax.axis_size(LEAF)
    leaf_count = parent.shape[1]

    even_pairs = [(i, i ^ 1) for i in range(devices)]
    cross_pairs = [(i, i + 1) for i in range(1, devices - 1, 2)]
    cross_pairs = cross_pairs + [(j, i) for i, j in cross_pairs]

    diagonal = [(2 * i + p, 2 * j + 1 - p) for i, j in cross_pairs for p in range(2)]

    regrets, chance, even, cross, cross_other, ranks, free, holding, pots, nodes = pack(
        board_cards, pot[None], regrets_start[0], chance_reach[0], hand_rank,
        hand_cards.T, parent.reshape(-1, 128),
    )
    cross = lax.ppermute(cross, LEAF, cross_pairs)
    even = lax.ppermute(even, LEAF, even_pairs)
    regrets_other = lax.ppermute(regrets, "player", [(0, 1), (1, 0)])
    chance_other = lax.ppermute(chance, "player", [(0, 1), (1, 0)])
    cross_other = lax.ppermute(cross_other, LEAF + ("player",), diagonal)

    own_matrix, apart = build_own(holding, ranks)
    near, built = build_pair(build_near_kernel, "build_near", (even, cross, apart))
    rows = forward(regrets_other, chance_other, built)
    even_other = lax.ppermute(rows, LEAF, even_pairs)
    far, outer = build_pair(
        build_far_kernel, "build_far", (even, cross, nodes, regrets_other, apart, rows)
    )

    def gathered(sums):
        return lax.all_to_all(sums.reshape(devices, 1, 128), LEAF, 0, 0).reshape(128, 128)

    count = float(leaf_count * HANDS)
    window, reached, instant, sums, same, all_free, all_pot = first(
        (outer, regrets, chance, even, cross, regrets_other, chance_other, even_other)
        + (cross_other,)
        + (nodes, free, pots, own_matrix, near, far),
    )
    values, moved, mine, sums = second(
        gathered(sums), window, reached, instant, same, all_free, all_pot,
        (own_matrix, near), count,
    )
    final = tail(gathered(sums), moved, mine, count)
    return (final[None], values[None])


def solution(mesh):
    split = Mesh(
        mesh.devices.reshape(*LEAF_SIZES, mesh.shape["player"]),
        LEAF + ("player",),
    )
    placed = (
        P("player", LEAF, None),
        P("player", LEAF, None),
        P(LEAF),
        P("player", None),
        P(),
        P(LEAF, None),
        P(LEAF, None),
    )
    return jax.shard_map(
        local,
        mesh=split,
        in_specs=placed,
        out_specs=(P("player", LEAF, None), P("player", LEAF, None)),
        check_vma=False,
    )
```
